256 devices in a mesh: dp: 8 (over x, core), expert: 32 (over y, z).
Axes of the slice: x: 4, y: 4, z: 8, core: 2. Of those that a mesh axis runs over, the one named last changes fastest.
Arguments:
- tokens: bfloat16 [6144, 2048], P(('dp', 'expert')), may hold values from -6 to 6
- out_grad: bfloat16 [6144, 2048], P(('dp', 'expert')), may hold values from -0.59765625 to 0.59765625
- expert_ids: int32 [6144, 8], P(('dp', 'expert')), may hold values from 0 to 31, all different within a row; in each aligned block of 24 rows (0 to 23, 24 to 47, ...) at most 8 rows name the same one
- router_weight: bfloat16 [2048, 32], replicated, may hold values from -0.1875 to 0.1875
- w_gate: bfloat16 [32, 2048, 768], P('expert'), may hold values from -0.125 to 0.125
- w_up: bfloat16 [32, 2048, 768], P('expert'), may hold values from -0.125 to 0.125
- w_down: bfloat16 [32, 768, 2048], P('expert'), may hold values from -0.21875 to 0.21875
Outputs:
- grad_tokens: bfloat16 [6144, 2048], P(('dp', 'expert'))
- grad_router: float32 [2048, 32], replicated
- grad_gate: bfloat16 [32, 2048, 768], P('expert', 'dp')
- grad_up: bfloat16 [32, 2048, 768], P('expert', 'dp')
- grad_down: bfloat16 [32, 768, 2048], P('expert', 'dp')
The draws below stay inside these ranges and needn't reach their ends.
Inputs may be any that keep to these rules, and one draw needn't show every extreme that they name: `expert_ids`: each row names 8 different experts. Among the 24 tokens of one device (aligned blocks of rows), no expert is named by more than 8 tokens, and in some blocks one expert is named by exactly 8.
All inputs are finite; a program needn't handle non-finite values.
Results may differ from the reference program's by a relative error of at most 0.017.
Values may be sent and summed in bfloat16 or wider, within the bound.
A program may use at most 128 MiB of HBM per device.

```python
import math
from functools import partial
import jax
import jax.numpy as jnp
import numpy as np
from jax import lax

D = 2048
FF = 768
TOP = 8
PASSES = 3
TOK_DEV = 24
EXPERTS = 32
CAP = 8
TOKENS = 6144
N_DP = 8
N_EXPERT = 32


def level_of(rng, extent, split, least, top_value):
    def one(axis_at, parts):
        steps = jax.random.uniform(jax.random.fold_in(jax.random.fold_in(rng, 6), axis_at), (parts,), jnp.float32, least / len(split), top_value / len(split))
        return jnp.repeat(jnp.exp(steps), extent[axis_at] // parts).reshape((-1,) + (1,) * (len(extent) - axis_at - 1))

    level = one(*split[0])
    for cut in split[1:]:
        level = level * one(*cut)
    return level


def shared_out(stream_key, own, number, rows, number_of, top, reach, skew):
    sequence = jax.random.permutation(stream_key, number_of)
    packed, ordinary = shares(number_of, rows * top, reach, skew, True), shares(number_of, rows * top, reach, skew, False)
    places = jnp.arange(number_of)

    def named(lengths, offset_by):
        used = int((lengths > 0).sum())
        fixed = max(1, used // 4)
        shifted = fixed + (places - fixed + offset_by * (used - fixed)) % max(1, number_of - fixed)
        return jnp.zeros((number_of,), jnp.int32).at[sequence[jnp.where(places < fixed, places, shifted)]].set(jnp.asarray(lengths, jnp.int32))

    lengths = jnp.where(number % 4 == 0, named(packed, number // 4), named(ordinary, number - number // 4 - 1))
    mixed = jax.random.permutation(jax.random.fold_in(own, 3), number_of)
    giver, taker = mixed[0:number_of // 2 * 2:2], mixed[1:number_of // 2 * 2:2]
    slack = jnp.minimum(lengths[giver] - 1, reach - lengths[taker]) // 2
    slack = jnp.where((giver == sequence[0]) | (taker == sequence[0]) | (lengths[taker] == 0), 0, jnp.maximum(slack, 0))
    shifted = jax.random.randint(jax.random.fold_in(own, 4), (number_of // 2,), 0, 1 << 20) % (slack + 1)
    lengths = lengths.at[giver].add(-shifted).at[taker].add(shifted)
    labels = jnp.searchsorted(jnp.cumsum(lengths), jnp.arange(rows * top), side="right").astype(jnp.int32)
    listing = labels.reshape(top, rows).T
    listing = listing[jax.random.permutation(jax.random.fold_in(own, 1), rows)]
    offset_by = jax.random.randint(jax.random.fold_in(own, 2), (rows, 1), 0, top)
    return jnp.take_along_axis(listing, (jnp.arange(top)[None, :] + offset_by) % top, axis=1)


def shares(count, total, reach, skew, full):
    portions = [(1 << 20) // math.isqrt(grade ** skew) + 1 for grade in range(1, count + 1)]
    largest = reach if full else min(reach, max(-(-total // count), total * portions[0] // sum(portions)))
    least = 1 if total - largest >= count - 1 else 0
    holding, surplus = [largest] + [least] * (count - 1), total - largest - least * (count - 1)
    while surplus > 0:
        free = [i for i in range(1, count) if holding[i] < largest] or [i for i in range(1, count) if holding[i] < reach]
        mass, left = sum([portions[i] for i in free]), surplus
        for i in free:
            addition = min(reach - holding[i], max(1, left * portions[i] // mass), surplus)
            holding[i] = holding[i] + addition
            surplus = surplus - addition
    return np.array(holding)


def centred(key, extent, scale, most, pieces=(), held_as=jnp.bfloat16):
    drawn = scale * jax.random.normal(key, extent, jnp.float32)
    if pieces:
        drawn = drawn * level_of(key, extent, pieces, -0.22, 0.18)
    return jnp.clip(drawn, -most, most).astype(held_as)


def setup_inputs(seed: int = 0) -> dict:
    key_of = jax.random.split(jax.random.key(seed), 8)
    tokens = centred(key_of[0], (TOKENS, D), 1.0, 6.0, ((0, 256),))
    out_grad = centred(key_of[1], (TOKENS, D), 0.1, 0.59765625, ((0, 256),))
    expert_ids_keys = jax.random.split(jax.random.fold_in(key_of[2], 1), TOKENS // TOK_DEV)
    expert_ids_turns = jax.random.permutation(jax.random.fold_in(key_of[2], 3), TOKENS // TOK_DEV)
    expert_ids = jax.vmap(lambda own, number: shared_out(jax.random.fold_in(key_of[2], 2), own, number, TOK_DEV, EXPERTS, TOP, CAP, 2))(expert_ids_keys, expert_ids_turns).reshape((TOKENS, TOP))
    router_weight = centred(key_of[3], (D, EXPERTS), (D // 2) ** -0.5, 0.1875)
    w_gate = centred(key_of[4], (EXPERTS, D, FF), D ** -0.5, 0.125, ((0, 32),))
    w_up = centred(key_of[5], (EXPERTS, D, FF), D ** -0.5, 0.125, ((0, 32),))
    w_down = centred(key_of[6], (EXPERTS, FF, D), FF ** -0.5, 0.21875, ((0, 32),))
    return {"tokens": tokens, "out_grad": out_grad, "expert_ids": expert_ids, "router_weight": router_weight, "w_gate": w_gate, "w_up": w_up, "w_down": w_down}


def expert_rows(rows_in, rows_grad, weight_gate, weight_up, weight_down):
    gate_pre = jnp.dot(rows_in, weight_gate, preferred_element_type=jnp.float32)
    up_pre = jnp.dot(rows_in, weight_up, preferred_element_type=jnp.float32)
    sigmoid_gate = jax.nn.sigmoid(gate_pre)
    activation = gate_pre * sigmoid_gate
    hidden = activation * up_pre
    contract_cols = (((1,), (1,)), ((), ()))
    hidden_grad = lax.dot_general(rows_grad, weight_down, contract_cols, preferred_element_type=jnp.float32)
    score_grad = jnp.sum(hidden_grad * hidden, axis=1).astype(jnp.bfloat16)
    gate_grad = (hidden_grad * up_pre * sigmoid_gate * (1.0 + gate_pre * (1.0 - sigmoid_gate))).astype(jnp.bfloat16)
    up_grad = (hidden_grad * activation).astype(jnp.bfloat16)
    input_grad = lax.dot_general(gate_grad, weight_gate, contract_cols, preferred_element_type=jnp.float32)
    input_grad = input_grad + lax.dot_general(up_grad, weight_up, contract_cols, preferred_element_type=jnp.float32)
    return hidden.astype(jnp.bfloat16), gate_grad, up_grad, input_grad.astype(jnp.bfloat16), score_grad


def scaled_rows(gate_values, rows_grad, gate_grad, up_grad):
    gate_scale = gate_values.astype(jnp.float32)[:, None]
    return ((gate_scale * rows_grad).astype(jnp.bfloat16), (gate_scale * gate_grad).astype(jnp.bfloat16),
            (gate_scale * up_grad).astype(jnp.bfloat16))


def balancer_forward_pass(router_logit_rows):
    expert_density_rows = [jnp.exp(router_logit_rows)]
    division_ratios, column_totals, row_totals = [], [], []
    for repeat in range(PASSES):
        column_sum = jnp.sum(expert_density_rows[-1], axis=0)
        quotient = expert_density_rows[-1] / column_sum
        row_sum = jnp.sum(quotient, axis=1, keepdims=True)
        expert_density_rows.append(quotient / row_sum)
        division_ratios.append(quotient)
        column_totals.append(column_sum)
        row_totals.append(row_sum)
    return expert_density_rows, division_ratios, column_totals, row_totals


def balancer_adjoint_pass(density_gradient, expert_density_rows, division_ratios, column_totals, row_totals):
    for repeat in reversed(range(PASSES)):
        density = expert_density_rows[repeat + 1]
        quotient_grad = (density_gradient - jnp.sum(density_gradient * density, axis=1, keepdims=True)) / row_totals[repeat]
        shared = jnp.sum(quotient_grad * division_ratios[repeat], axis=0)
        density_gradient = (quotient_grad - shared) / column_totals[repeat]
    return density_gradient * expert_density_rows[0]


def one_group(expert, group_index, grouped_in, grouped_grad, picked_groups, gates_groups, sent_groups,
              w_gate, w_up, w_down):
    slot_total = N_EXPERT * CAP
    group_tokens = TOK_DEV * N_EXPERT
    route_mask = picked_groups[group_index][:, expert]
    route_count = jnp.sum(route_mask)
    positions = jnp.nonzero(route_mask, size=slot_total, fill_value=0)[0].astype(jnp.int32)
    live_slot = jnp.arange(slot_total, dtype=jnp.int32) < route_count
    zero_value = jnp.zeros((), jnp.bfloat16)
    rows_in = jnp.where(live_slot[:, None], grouped_in[group_index][positions], zero_value)
    rows_grad = jnp.where(live_slot[:, None], grouped_grad[group_index][positions], zero_value)
    gate_values = jnp.where(live_slot, sent_groups[group_index][positions, expert], zero_value)
    hidden, gate_grad, up_grad, input_grad, score_grad = expert_rows(
        rows_in, rows_grad, w_gate[expert], w_up[expert], w_down[expert])
    down_scaled, gate_scaled, up_scaled = scaled_rows(gate_values, rows_grad, gate_grad, up_grad)
    contract_rows = (((0,), (0,)), ((), ()))
    part_gate = lax.dot_general(rows_in, gate_scaled, contract_rows, preferred_element_type=jnp.float32)
    part_up = lax.dot_general(rows_in, up_scaled, contract_rows, preferred_element_type=jnp.float32)
    part_down = lax.dot_general(hidden, down_scaled, contract_rows, preferred_element_type=jnp.float32)
    gate_full = jnp.where(live_slot, gates_groups[group_index][positions, expert], 0.0)
    input_part = jnp.zeros((group_tokens, D), jnp.float32).at[positions].add(
        gate_full[:, None] * input_grad.astype(jnp.float32))
    score_part = jnp.zeros((group_tokens,), jnp.float32).at[positions].add(
        jnp.where(live_slot, score_grad.astype(jnp.float32), 0.0))
    return (input_part, score_part, part_gate.astype(jnp.bfloat16), part_up.astype(jnp.bfloat16),
            part_down.astype(jnp.bfloat16))


def reference(tokens, out_grad, expert_ids, router_weight, w_gate, w_up, w_down):
    router_logit_rows = jnp.dot(tokens, router_weight, preferred_element_type=jnp.float32)
    expert_density_rows, division_ratios, column_totals, row_totals = balancer_forward_pass(router_logit_rows)
    gate_matrix = EXPERTS * expert_density_rows[-1]
    expert_range = jnp.arange(EXPERTS, dtype=jnp.int32)
    picked = jnp.sum((expert_ids[:, :, None] == expert_range[None, None, :]).astype(jnp.int32), axis=1)
    group_tokens = TOK_DEV * N_EXPERT
    grouped_in = tokens.reshape(N_DP, group_tokens, D)
    grouped_grad = out_grad.reshape(N_DP, group_tokens, D)
    picked_groups = picked.reshape(N_DP, group_tokens, EXPERTS)
    gates_groups = gate_matrix.reshape(N_DP, group_tokens, EXPERTS)
    sent_groups = gate_matrix.astype(jnp.bfloat16).reshape(N_DP, group_tokens, EXPERTS)

    def one_expert(input_acc, expert):
        group_fn = partial(one_group, expert, grouped_in=grouped_in, grouped_grad=grouped_grad,
                           picked_groups=picked_groups, gates_groups=gates_groups, sent_groups=sent_groups,
                           w_gate=w_gate, w_up=w_up, w_down=w_down)
        input_part, score_part, part_gate, part_up, part_down = lax.map(
            group_fn, jnp.arange(N_DP, dtype=jnp.int32))
        grad_gate_one = jnp.sum(part_gate.astype(jnp.float32), axis=0).astype(jnp.bfloat16)
        grad_up_one = jnp.sum(part_up.astype(jnp.float32), axis=0).astype(jnp.bfloat16)
        grad_down_one = jnp.sum(part_down.astype(jnp.float32), axis=0).astype(jnp.bfloat16)
        return input_acc + input_part, (score_part.reshape(TOKENS), grad_gate_one, grad_up_one, grad_down_one)

    input_start = jnp.zeros((N_DP, group_tokens, D), jnp.float32)
    input_acc, (score_cols, grad_gate, grad_up, grad_down) = lax.scan(one_expert, input_start, expert_range)
    density_gradient = EXPERTS * score_cols.T
    logit_gradient = balancer_adjoint_pass(density_gradient, expert_density_rows, division_ratios, column_totals, row_totals).astype(jnp.bfloat16)
    grad_router = lax.dot_general(tokens, logit_gradient, (((0,), (0,)), ((), ())), preferred_element_type=jnp.float32)
    router_input = lax.dot_general(logit_gradient, router_weight, (((1,), (1,)), ((), ())),
                                   preferred_element_type=jnp.float32)
    grad_tokens = (input_acc.reshape(TOKENS, D) + router_input).astype(jnp.bfloat16)
    return grad_tokens, grad_router, grad_gate, grad_up, grad_down
```

```python
import functools

import jax
import jax.numpy as jnp
from jax import lax
from jax.experimental import pallas as pl
from jax.experimental.pallas import tpu as pltpu
from jax.sharding import PartitionSpec as P

HI = lax.Precision.HIGHEST
F32 = jnp.float32
BF16 = jnp.bfloat16
NE = 32
ND = 8
NX = 4
TOK = 24
CAP = 8
D = 2048
FF = 768
VM = pl.BlockSpec(memory_space=pltpu.VMEM)
MESH = pl.DeviceIdType.MESH


def iota(shape, dim):
    return lax.broadcasted_iota(jnp.int32, shape, dim)


def remote(src, dst, send, recv, dev):
    return pltpu.make_async_remote_copy(
        src_ref=src, dst_ref=dst, send_sem=send, recv_sem=recv, device_id=dev, device_id_type=MESH
    )


def drain(ref, sem):
    pltpu.make_async_copy(ref, ref, sem).wait()


def place():
    me_d = lax.axis_index("dp")
    return me_d, lax.axis_index("expert"), me_d // 2, lax.rem(me_d, 2)


def others(n, body):
    lax.fori_loop(1, n, lambda k, c: (body(k), c)[1], 0)


def greet(me_d, me_e):
    barrier = pltpu.get_barrier_semaphore()
    others(
        NE,
        lambda k: pl.semaphore_signal(
            barrier, inc=1, device_id=(me_d, lax.rem(me_e + k, NE)), device_id_type=MESH
        ),
    )
    others(
        ND,
        lambda k: pl.semaphore_signal(
            barrier, inc=1, device_id=(lax.rem(me_d + k, ND), me_e), device_id_type=MESH
        ),
    )
    pl.semaphore_wait(barrier, NE - 1 + ND - 1)


def own_state(logits, cols):
    lane = iota((TOK, 128), 1)
    d = jnp.where(lane < NE, jnp.exp(logits), 0.0)
    ds, qs = [d], []
    for p in range(3):
        q = d / cols[p : p + 1, :]
        d = q / jnp.sum(q, axis=1, keepdims=True)
        qs.append(q)
        ds.append(d)
    return ds, qs


def dispatch_kernel(
    packed, logits, rank, xs, xr, gate_out, cols, gram,
    lall, dd, gtile, gbuf, s_sem, r_sem, xs_sem, xr_sem, x_s, x_r, p_s, p_r, g_s, g_r,
):
    me_d, me_e, x, core = place()
    greet(me_d, me_e)

    pltpu.make_async_copy(packed, lall.at[core, x, me_e], r_sem).start()
    others(
        NE,
        lambda k: remote(
            packed, lall.at[core, x, me_e], s_sem, r_sem, (me_d, lax.rem(me_e + k, NE))
        ).start(),
    )
    pltpu.make_async_copy(xs.at[me_e], xr.at[me_e], xr_sem).start()

    def send_rows(k):
        to = lax.rem(me_e + k, NE)
        remote(xs.at[to], xr.at[me_e], xs_sem, xr_sem, (me_d, to)).start()

    others(NE, send_rows)

    drain(lall.at[core, x], r_sem)
    others(
        NX,
        lambda k: remote(
            lall.at[core, x], lall.at[core, x], x_s, x_r, (lax.rem(x + k, NX) * 2 + core, me_e)
        ).start(),
    )
    drain(lall.at[core, pl.ds(0, NX - 1)], x_r)
    partner = (x * 2 + 1 - core, me_e)
    pair = remote(lall.at[core], lall.at[core], p_s, p_r, partner)
    pair.start()
    drain(lall.at[1 - core], p_r)

    row = iota((256, 128), 0)
    valid = lax.rem(row, 8) < 6
    li, lj = iota((128, 128), 0), iota((128, 128), 1)
    fold = (lax.rem(li, 32) == lax.rem(lj, 32)).astype(F32)
    block = (li // 32 == lj // 32).astype(F32)

    def rows_of(a):
        return jnp.sum(a.reshape(32, 8, 128), axis=0)

    def first(i, acc):
        d0 = jnp.where(valid, jnp.exp(lall[i // NX, lax.rem(i, NX)].reshape(256, 128)), 0.0)
        dd[i] = d0
        return acc + rows_of(d0)

    acc = lax.fori_loop(0, 8, first, jnp.zeros((8, 128), F32))
    pad = jnp.where(valid, 0.0, 1.0)

    def total(acc):
        one = jnp.broadcast_to(jnp.sum(acc, axis=0, keepdims=True), (8, 128))
        return jnp.dot(one, fold, precision=HI, preferred_element_type=F32)

    c = total(acc)
    cols[0:8, :] = c
    for p in range(2):
        def step(i, carry):
            acc, g = carry
            q = dd[i] / c[0:1, :]
            rs = jnp.dot(q, block, precision=HI, preferred_element_type=F32)
            d = q / (rs + pad)
            dd[i] = d
            g = g + lax.dot_general(
                d, d, (((0,), (0,)), ((), ())), precision=HI, preferred_element_type=F32
            )
            return acc + rows_of(d), g

        acc, g = lax.fori_loop(
            0, 8, step, (jnp.zeros((8, 128), F32), jnp.zeros((128, 128), F32))
        )
        g = jnp.dot(fold, g * block, precision=HI, preferred_element_type=F32)
        gram[p] = jnp.dot(g, fold, precision=HI, preferred_element_type=F32)
        c = total(acc)
        cols[8 * p + 8 : 8 * p + 16, :] = c

    c3 = jnp.concatenate([cols[0:1, :], cols[8:9, :], cols[16:17, :]], axis=0)
    ds, _ = own_state(logits[...], c3)
    gates = NE * ds[3]
    sub = iota((8, 128), 0)
    tile = jnp.zeros((8, 128), F32)
    for slot in range(CAP):
        one = jnp.sum(jnp.where(rank[...] == slot, gates, 0.0), axis=0, keepdims=True)
        tile = tile + jnp.where(sub == slot, jnp.broadcast_to(one, (8, 128)), 0.0)
    gtile[...] = tile
    pltpu.make_async_copy(gtile, gbuf.at[me_e], g_r).start()
    others(
        NE,
        lambda k: remote(
            gtile, gbuf.at[me_e], g_s, g_r, (me_d, lax.rem(me_e + k, NE))
        ).start(),
    )
    drain(gbuf, g_r)
    flat = gbuf[...].reshape(256, 128)
    mine = jnp.sum(jnp.where(iota((256, 128), 1) == me_e, flat, 0.0), axis=1, keepdims=True)
    gate_out[...] = jnp.broadcast_to(mine, (256, 128))

    drain(xr, xr_sem)
    drain(xs.at[pl.ds(0, NE - 1)], xs_sem)
    drain(gbuf.at[pl.ds(0, NE - 1)], g_s)
    drain(lall.at[0, 0, pl.ds(0, NE - 1)], s_sem)
    drain(lall.at[0, pl.ds(0, NX - 1)], x_s)
    pair.wait_send()


def dispatch(packed, logits, rank, xs):
    dma = pltpu.SemaphoreType.DMA
    return pl.pallas_call(
        dispatch_kernel,
        out_shape=(
            jax.ShapeDtypeStruct((NE, 16, D), BF16),
            jax.ShapeDtypeStruct((256, 128), F32),
            jax.ShapeDtypeStruct((24, 128), F32),
            jax.ShapeDtypeStruct((2, 128, 128), F32),
        ),
        in_specs=[VM] * 4,
        out_specs=(VM,) * 4,
        scratch_shapes=[
            pltpu.VMEM((2, NX, NE, 8, 128), F32),
            pltpu.VMEM((8, 256, 128), F32),
            pltpu.VMEM((8, 128), F32),
            pltpu.VMEM((NE, 8, 128), F32),
        ]
        + [dma] * 10,
        compiler_params=pltpu.CompilerParams(collective_id=0, has_side_effects=True),
    )(packed, logits, rank, xs)


def finish_kernel(
    gp, gd, back, score, tokens, logits, rank, cols, gram, rw_t,
    gt_out, pair_out, down_out, router_out,
    rp1, rp2, t1, t2, ra1, ra2, rb1, rb2, u1, u2, w1, w2, rc1, rc2, rd1, rd2,
    ret, sbuf, atile, abuf, btile, bbuf, rsend, rrecv, dsum, drecv, fin,
    p_s, p_r, h_s, h_r, f_s, f_r, ret_s, ret_r, sc_s, sc_r, a_s, a_r, b_s, b_r,
    rs_s, rs_r, d_s, d_r, o_s, o_r,
):
    me_d, me_e, x, core = place()
    greet(me_d, me_e)
    partner = (x * 2 + 1 - core, me_e)
    right = (lax.rem(x + 1, NX) * 2 + core, me_e)
    left = (lax.rem(x + 3, NX) * 2 + core, me_e)

    def plane(src, dst, send, recv):
        pltpu.make_async_copy(src(me_e), dst.at[me_e], recv).start()

        def go(k):
            to = lax.rem(me_e + k, NE)
            remote(src(to), dst.at[me_e], send, recv, (me_d, to)).start()

        others(NE, go)

    plane(lambda e: score.at[e], sbuf, sc_s, sc_r)
    pairs = []
    for n, j in enumerate((2, 1, 3, 0)):
        o = lax.rem(x + j, NX)
        c1 = remote(gp.at[o, 1 - core], rp1.at[j], p_s.at[j, 0], p_r.at[j, 0], partner)
        c2 = remote(gd.at[o, 1 - core], rp2.at[j], p_s.at[j, 1], p_r.at[j, 1], partner)
        c1.start()
        c2.start()
        pairs += [c1, c2]
    plane(lambda e: back.at[e], ret, ret_s, ret_r)

    def got_pair(j):
        drain(rp1.at[j], p_r.at[j, 0])
        drain(rp2.at[j], p_r.at[j, 1])

    def add_rows(n, rows, terms, out):
        def one(i, c):
            at = pl.ds(pl.multiple_of(i * rows, rows), rows)
            out[at, :] = functools.reduce(
                lambda a, b: a + b, [t(at).astype(F32) for t in terms]
            ).astype(BF16)
            return c

        lax.fori_loop(0, n // rows, one, 0)

    def own1(j):
        o = lax.rem(x + j, NX)
        return lambda at: gp[o, core, at, :]

    def own2(j):
        o = lax.rem(x + j, NX)
        return lambda at: gd[o, core, at, :]

    got_pair(2)
    add_rows(256, 32, [own1(2), lambda at: rp1[2, at, :]], t1)
    add_rows(96, 48, [own2(2), lambda at: rp2[2, at, :]], t2)
    half = [
        remote(t1.at[pl.ds(0, 128)], ra1, h_s.at[0], h_r.at[0], right),
        remote(t2.at[pl.ds(0, 48)], ra2, h_s.at[1], h_r.at[1], right),
        remote(t1.at[pl.ds(128, 128)], rb1, h_s.at[2], h_r.at[2], left),
        remote(t2.at[pl.ds(48, 48)], rb2, h_s.at[3], h_r.at[3], left),
    ]
    for c in half:
        c.start()

    c3 = jnp.concatenate([cols[0:1, :], cols[8:9, :], cols[16:17, :]], axis=0)
    ds, qs = own_state(logits[...], c3)
    lane = iota((TOK, 128), 1)
    drain(sbuf, sc_r)
    lane8 = iota((8, 128), 1)
    scores = jnp.zeros((8, 128), F32)
    for e in range(NE):
        scores = scores + jnp.where(lane8 == e, sbuf[e], 0.0)
    grad3 = jnp.zeros((TOK, 128), F32)
    for slot in range(CAP):
        grad3 = grad3 + jnp.where(
            rank[...] == slot, jnp.broadcast_to(scores[slot : slot + 1, :], (TOK, 128)), 0.0
        )
    g = NE * grad3 * ds[3]
    h3 = g - ds[3] * jnp.sum(g, axis=1, keepdims=True)
    atile[...] = jnp.broadcast_to(jnp.sum(h3, axis=0, keepdims=True), (8, 128))
    plane(lambda e: atile, abuf, a_s, a_r)

    got_pair(1)
    got_pair(3)
    for c in half:
        c.wait_recv()

    add_rows(128, 32, [own1(1), lambda at: rp1[1, at, :], lambda at: ra1[at, :]], u1)
    add_rows(48, 48, [own2(1), lambda at: rp2[1, at, :], lambda at: ra2[at, :]], u2)

    def shifted(f, by):
        return lambda at: f(pl.ds(pl.multiple_of(at.start + by, 16), at.size))

    add_rows(
        128, 32, [shifted(own1(1), 128), shifted(lambda at: rp1[1, at, :], 128)],
        u1.at[pl.ds(128, 128)],
    )
    add_rows(
        48, 48, [shifted(own2(1), 48), shifted(lambda at: rp2[1, at, :], 48)],
        u2.at[pl.ds(48, 48)],
    )
    full = [
        remote(u1, rc1, f_s.at[0], f_r.at[0], right),
        remote(u2, rc2, f_s.at[1], f_r.at[1], right),
    ]
    full[0].start()
    full[1].start()
    add_rows(128, 32, [own1(3), lambda at: rp1[3, at, :]], w1)
    add_rows(48, 48, [own2(3), lambda at: rp2[3, at, :]], w2)
    add_rows(
        128, 32,
        [shifted(own1(3), 128), shifted(lambda at: rp1[3, at, :], 128), lambda at: rb1[at, :]],
        w1.at[pl.ds(128, 128)],
    )
    add_rows(
        48, 48,
        [shifted(own2(3), 48), shifted(lambda at: rp2[3, at, :], 48), lambda at: rb2[at, :]],
        w2.at[pl.ds(48, 48)],
    )
    full += [
        remote(w1, rd1, f_s.at[2], f_r.at[2], left),
        remote(w2, rd2, f_s.at[3], f_r.at[3], left),
    ]
    full[2].start()
    full[3].start()

    drain(abuf, a_r)
    btile[...] = jnp.sum(abuf[...], axis=0)
    pltpu.make_async_copy(btile, bbuf.at[me_d], b_r).start()
    others(
        ND,
        lambda k: remote(
            btile, bbuf.at[me_d], b_s, b_r, (lax.rem(me_d + k, ND), me_e)
        ).start(),
    )
    gates = NE * ds[3]
    ex_i, ex_j = iota((128, 512), 0), iota((128, 512), 1)
    spread = ((ex_i < NE) & (ex_j // 16 == ex_i)).astype(BF16)
    g_hi = gates.astype(BF16)
    g_lo = (gates - g_hi.astype(F32)).astype(BF16)
    wide = jnp.dot(
        jnp.concatenate([rank[...], g_hi.astype(F32), g_lo.astype(F32)], axis=0).astype(BF16),
        spread,
        preferred_element_type=F32,
    )
    k16 = lax.rem(iota((TOK, 512), 1), 16)
    rank_w = wide[0:TOK].astype(jnp.int32)
    left_m, right_m = rank_w == k16, rank_w == k16 - 8
    parts = []
    for m in (left_m, right_m):
        parts += [jnp.where(m, wide[TOK : 2 * TOK], 0.0), jnp.where(m, wide[2 * TOK :], 0.0)]
    weights = jnp.concatenate(parts, axis=0).astype(BF16)

    drain(bbuf, b_r)
    v = jnp.sum(bbuf[...], axis=0)
    first32 = lane8 < NE
    u = jnp.dot(
        jnp.where(first32, v / cols[16:24, :], 0.0), gram[1], precision=HI,
        preferred_element_type=F32,
    )
    s = jnp.dot(
        jnp.where(first32, u / cols[8:16, :], 0.0), gram[0], precision=HI,
        preferred_element_type=F32,
    )
    qv = qs[2] * v[0:1, :]
    h2 = h3 - qv + ds[2] * jnp.sum(qv, axis=1, keepdims=True)
    qu = qs[1] * u[0:1, :]
    h1 = h2 - qu + ds[1] * jnp.sum(qu, axis=1, keepdims=True)
    lgrad = (h1 - qs[0] * s[0:1, :]).astype(BF16)[:, :NE]
    router_t = lax.dot_general(
        lgrad, tokens[...], (((0,), (0,)), ((), ())), preferred_element_type=F32
    )
    for p in range(NE):
        h, b = p % 2, p // 2
        rsend[p] = router_t[16 * h : 16 * h + 16, 128 * b : 128 * b + 128]
    plane(lambda e: rsend.at[e], rrecv, rs_s, rs_r)
    router_in = jnp.dot(lgrad, rw_t[...], preferred_element_type=F32)

    drain(ret, ret_r)
    flat = ret[...].reshape(512, 1024)
    mixed = jnp.dot(weights, flat, preferred_element_type=F32)
    gt_out[:, 0:1024] = (mixed[0:24] + mixed[24:48] + router_in[:, 0:1024]).astype(BF16)
    gt_out[:, 1024:2048] = (mixed[48:72] + mixed[72:96] + router_in[:, 1024:2048]).astype(BF16)

    drain(rrecv, rs_r)
    dsum[...] = jnp.sum(rrecv[...], axis=0)
    pltpu.make_async_copy(dsum, drecv.at[me_d], d_r).start()
    others(
        ND,
        lambda k: remote(
            dsum, drecv.at[me_d], d_s, d_r, (lax.rem(me_d + k, ND), me_e)
        ).start(),
    )
    drain(drecv, d_r)
    fin[...] = jnp.sum(drecv[...], axis=0)
    plane(lambda e: fin, router_out, o_s, o_r)

    got_pair(0)
    for c in full:
        c.wait_recv()
    add_rows(
        256, 32,
        [own1(0), lambda at: rp1[0, at, :], lambda at: rc1[at, :], lambda at: rd1[at, :]],
        pair_out,
    )
    add_rows(
        96, 48,
        [own2(0), lambda at: rp2[0, at, :], lambda at: rc2[at, :], lambda at: rd2[at, :]],
        down_out,
    )
    drain(router_out, o_r)
    for c in pairs + half + full:
        c.wait_send()
    drain(ret.at[pl.ds(0, NE - 1)], ret_s)
    drain(sbuf.at[pl.ds(0, NE - 1)], sc_s)
    drain(abuf.at[pl.ds(0, NE - 1)], a_s)
    drain(bbuf.at[pl.ds(0, ND - 1)], b_s)
    drain(rrecv.at[pl.ds(0, NE - 1)], rs_s)
    drain(drecv.at[pl.ds(0, ND - 1)], d_s)
    drain(router_out.at[pl.ds(0, NE - 1)], o_s)


def finish(*args):
    dma = pltpu.SemaphoreType.DMA
    V = pltpu.VMEM
    return pl.pallas_call(
        finish_kernel,
        out_shape=(
            jax.ShapeDtypeStruct((TOK, D), BF16),
            jax.ShapeDtypeStruct((256, 2 * FF), BF16),
            jax.ShapeDtypeStruct((96, D), BF16),
            jax.ShapeDtypeStruct((NE, 16, 128), F32),
        ),
        in_specs=[VM] * 10,
        out_specs=(VM,) * 4,
        scratch_shapes=[
            V((4, 256, 2 * FF), BF16), V((4, 96, D), BF16),
            V((256, 2 * FF), BF16), V((96, D), BF16),
            V((128, 2 * FF), BF16), V((48, D), BF16),
            V((128, 2 * FF), BF16), V((48, D), BF16),
            V((256, 2 * FF), BF16), V((96, D), BF16),
            V((256, 2 * FF), BF16), V((96, D), BF16),
            V((256, 2 * FF), BF16), V((96, D), BF16),
            V((256, 2 * FF), BF16), V((96, D), BF16),
            V((NE, 16, 1024), BF16),
            V((NE, 8, 128), F32),
            V((8, 128), F32), V((NE, 8, 128), F32),
            V((8, 128), F32), V((ND, 8, 128), F32),
            V((NE, 16, 128), F32), V((NE, 16, 128), F32),
            V((16, 128), F32), V((ND, 16, 128), F32), V((16, 128), F32),
            dma((4, 2)), dma((4, 2)), dma((4,)), dma((4,)), dma((4,)), dma((4,)),
        ]
        + [dma] * 14,
        compiler_params=pltpu.CompilerParams(
            collective_id=1, has_side_effects=True, vmem_limit_bytes=60 * 1024 * 1024
        ),
    )(*args)


def column_product(a, b):
    return lax.dot_general(a, b, (((0,), (0,)), ((), ())), preferred_element_type=F32)


def per_device(tokens, out_grad, expert_ids, router_weight, w_gate, w_up, w_down):
    wg, wu, wd = w_gate[0], w_up[0], w_down[0]
    logits = jnp.dot(tokens, router_weight, preferred_element_type=F32)
    er = jnp.arange(NE, dtype=jnp.int32)
    picked = jnp.sum((expert_ids[:, :, None] == er).astype(jnp.int32), axis=1)
    before = (jnp.arange(TOK)[:, None] > jnp.arange(TOK)[None, :]).astype(BF16)
    rank = jnp.dot(before, picked.astype(BF16), preferred_element_type=F32).astype(jnp.int32)
    rank = jnp.where(picked > 0, rank, -64)
    packed = jnp.pad(logits.reshape(6, 128), ((0, 2), (0, 0)))
    logits_w = jnp.pad(logits, ((0, 0), (0, 96)))
    rank_w = jnp.pad(rank, ((0, 0), (0, 96)), constant_values=-64)
    sel = (rank.T[:, None, :] == jnp.arange(CAP)[None, :, None]).astype(BF16)
    zero = jnp.zeros_like(sel)
    both = jnp.concatenate(
        [jnp.concatenate([sel, zero], axis=2), jnp.concatenate([zero, sel], axis=2)], axis=1
    )
    xs = jnp.einsum(
        "ekt,td->ekd", both, jnp.concatenate([tokens, out_grad], axis=0),
        preferred_element_type=F32,
    ).astype(BF16)
    xr, gate_b, cols, gram = dispatch(packed, logits_w, rank_w, xs)

    flat_in = xr[:, :CAP].reshape(256, D)
    flat_grad = xr[:, CAP:].reshape(256, D)
    gate = gate_b[:, 0:1].astype(BF16).astype(F32)
    gate_pre = jnp.dot(flat_in, wg, preferred_element_type=F32)
    up_pre = jnp.dot(flat_in, wu, preferred_element_type=F32)
    sg = jax.nn.sigmoid(gate_pre)
    act = gate_pre * sg
    hidden = act * up_pre
    tc = (((1,), (1,)), ((), ()))
    hgrad = lax.dot_general(flat_grad, wd, tc, preferred_element_type=F32)
    score = jnp.sum(hgrad * hidden, axis=1, keepdims=True).astype(BF16).astype(F32)
    ggrad = (hgrad * up_pre * sg * (1.0 + gate_pre * (1.0 - sg))).astype(BF16)
    ugrad = (hgrad * act).astype(BF16)
    igrad = lax.dot_general(ggrad, wg, tc, preferred_element_type=F32)
    igrad = igrad + lax.dot_general(ugrad, wu, tc, preferred_element_type=F32)
    back = igrad.astype(BF16).reshape(NE, CAP, 2, 1024).transpose(0, 2, 1, 3).reshape(NE, 16, 1024)
    paired = jnp.concatenate([(gate * ggrad).astype(BF16), (gate * ugrad).astype(BF16)], axis=1)
    gp = column_product(flat_in, paired).astype(BF16).reshape(NX, 2, 256, 2 * FF)
    gd = column_product(hidden.astype(BF16), (gate * flat_grad).astype(BF16)).astype(BF16)
    gd = gd.reshape(NX, 2, 96, D)
    score_b = jnp.broadcast_to(score, (256, 128)).reshape(NE, CAP, 128)
    gt, pair, down, router = finish(
        gp, gd, back, score_b, tokens, logits_w, rank_w, cols, gram, router_weight.T
    )
    grad_router = router.reshape(16, 2, 16, 128).transpose(0, 3, 1, 2).reshape(D, NE)
    return gt, grad_router, pair[None, :, :FF], pair[None, :, FF:], down[None]


def solution(mesh):
    in_specs = (
        P(("dp", "expert"), None), P(("dp", "expert"), None), P(("dp", "expert"), None), P(),
        P("expert", None, None), P("expert", None, None), P("expert", None, None),
    )
    out_specs = (
        P(("dp", "expert"), None), P(),
        P("expert", "dp", None), P("expert", "dp", None), P("expert", "dp", None),
    )
    return jax.shard_map(
        per_device, mesh=mesh, in_specs=in_specs, out_specs=out_specs, check_vma=False
    )
```

```python
import functools

import jax
import jax.numpy as jnp
from jax import lax
from jax.experimental import pallas as pl
from jax.experimental.pallas import tpu as pltpu
from jax.sharding import PartitionSpec as P

HI = lax.Precision.HIGHEST
F32 = jnp.float32
BF16 = jnp.bfloat16
NE = 32
ND = 8
NX = 4
TOK = 24
CAP = 8
D = 2048
FF = 768
VM = pl.BlockSpec(memory_space=pltpu.VMEM)
MESH = pl.DeviceIdType.MESH


def iota(shape, dim):
    return lax.broadcasted_iota(jnp.int32, shape, dim)


def remote(src, dst, send, recv, dev):
    return pltpu.make_async_remote_copy(
        src_ref=src, dst_ref=dst, send_sem=send, recv_sem=recv, device_id=dev, device_id_type=MESH
    )


def drain(ref, sem):
    pltpu.make_async_copy(ref, ref, sem).wait()


def place():
    me_d = lax.axis_index("dp")
    return me_d, lax.axis_index("expert"), me_d // 2, lax.rem(me_d, 2)


def others(n, body):
    lax.fori_loop(1, n, lambda k, c: (body(k), c)[1], 0)


def greet(me_d, me_e):
    barrier = pltpu.get_barrier_semaphore()
    others(
        NE,
        lambda k: pl.semaphore_signal(
            barrier, inc=1, device_id=(me_d, lax.rem(me_e + k, NE)), device_id_type=MESH
        ),
    )
    others(
        ND,
        lambda k: pl.semaphore_signal(
            barrier, inc=1, device_id=(lax.rem(me_d + k, ND), me_e), device_id_type=MESH
        ),
    )
    pl.semaphore_wait(barrier, NE - 1 + ND - 1)


def own_state(logits, cols):
    lane = iota((TOK, 128), 1)
    d = jnp.where(lane < NE, jnp.exp(logits), 0.0)
    ds, qs = [d], []
    for p in range(3):
        q = d / cols[p : p + 1, :]
        d = q / jnp.sum(q, axis=1, keepdims=True)
        qs.append(q)
        ds.append(d)
    return ds, qs


NT = (((1,), (1,)), ((), ()))
TN = (((0,), (0,)), ((), ()))


def mm(a, b, dims=None, exact=False):
    dims = dims or (((1,), (0,)), ((), ()))
    return lax.dot_general(
        a, b, dims, precision=HI if exact else None, preferred_element_type=F32
    )


def moe_kernel(
    tokens, grads, ids, rw, wg_hbm, wu_hbm, wd_hbm,
    gt_out, pair_out, down_out, router_out,
    wg, wu, wd, packed, rk, rkbuf, lall, dd, cols, gram, gtile, gbuf,
    zt, zg, yt, yg, rt, rg, pt, hid, act, dsl, ht, pht, ds, pds, gg, ug, pair, ppair,
    g1, g2, ra1, ra2, rb1, rb2, rc1, rc2, rd1, rd2,
    bsend, ret, stile, sbuf, atile, abuf, btile, bbuf, rsend, rrecv, dsum, drecv, fin,
    w_sem, zs_t, zr_t, zs_g, zr_g, ys_t, yr_t, ys_g, yr_g, q_s, q_r, h_s, h_r, n_s, n_r, m_s, m_r,
    lg_s, lg_r, rk_s, rk_r, x_s, x_r, p_s, p_r, g_s, g_r, ret_s, ret_r, sc_s, sc_r,
    a_s, a_r, b_s, b_r, rs_s, rs_r, d_s, d_r, o_s, o_r,
):
    me_d, me_e, x, core = place()
    y, z = me_e // 8, lax.rem(me_e, 8)
    barrier = pltpu.get_barrier_semaphore()
    others(
        NE,
        lambda k: pl.semaphore_signal(
            barrier, inc=1, device_id=(me_d, lax.rem(me_e + k, NE)), device_id_type=MESH
        ),
    )
    others(
        ND,
        lambda k: pl.semaphore_signal(
            barrier, inc=1, device_id=(lax.rem(me_d + k, ND), me_e), device_id_type=MESH
        ),
    )
    loads = [
        pltpu.make_async_copy(a.at[0], b, w_sem.at[n])
        for n, (a, b) in enumerate(((wg_hbm, wg), (wu_hbm, wu), (wd_hbm, wd)))
    ]
    for c in loads:
        c.start()
    partner = (x * 2 + 1 - core, me_e)
    right = (lax.rem(x + 1, NX) * 2 + core, me_e)
    left = (lax.rem(x + 3, NX) * 2 + core, me_e)
    z_up = (me_d, y * 8 + lax.rem(z + 1, 8))
    z_down = (me_d, y * 8 + lax.rem(z + 7, 8))

    lane24 = iota((TOK, 128), 1)
    lane8, sub8 = iota((8, 128), 1), iota((8, 128), 0)
    logits = jnp.concatenate(
        [mm(tokens[...], rw[...]), jnp.zeros((TOK, 96), F32)], axis=1
    )
    packed[...] = (
        logits[0:8] + pltpu.roll(logits[8:16], 32, 1) + pltpu.roll(logits[16:24], 64, 1)
    )
    picked = jnp.zeros((TOK, 128), F32)
    for k in range(8):
        picked = picked + (ids[:, k : k + 1] == lane24).astype(F32)
    before = (iota((TOK, TOK), 0) > iota((TOK, TOK), 1)).astype(BF16)
    rank = jnp.where(picked > 0, mm(before, picked.astype(BF16)), -64.0)
    rank_pad = jnp.concatenate([rank, jnp.full((104, 128), -64.0, F32)], axis=0).astype(BF16)
    pi, pj = iota((64, 128), 0), iota((64, 128), 1)
    place_rows = ((lax.rem(pi, 8) < 4) & (pj == lax.rem(pi, 8) * 8 + pi // 8)).astype(BF16)
    rk[...] = mm(place_rows, rank_pad, NT).reshape(8, 8, 128)

    pl.semaphore_wait(barrier, NE - 1 + ND - 1)

    def z_ring(k):
        to = lax.rem(z + k, 8)
        remote(rk.at[to], rkbuf.at[z], rk_s, rk_r, (me_d, y * 8 + to)).start()

    pltpu.make_async_copy(rk.at[z], rkbuf.at[z], rk_r).start()
    others(8, z_ring)

    def z_copy(own, buf, ss, rs, k, sign):
        at = lambda n: (8 + sign * n) % 8
        return remote(
            own if k == 1 else buf.at[at(k - 1)], buf.at[at(k)], ss.at[at(k)], rs.at[at(k)],
            z_down if sign > 0 else z_up,
        )

    t_dn = [z_copy(tokens, zt, zs_t, zr_t, k, -1) for k in (1, 2, 3, 4)]
    t_up = [z_copy(tokens, zt, zs_t, zr_t, k, 1) for k in (1, 2, 3)]
    g_dn = [z_copy(grads, zg, zs_g, zr_g, k, -1) for k in (1, 2, 3)]
    g_up = [z_copy(grads, zg, zs_g, zr_g, k, 1) for k in (1, 2, 3, 4)]
    t_dn[0].start()
    t_up[0].start()

    def plane(src, dst, send, recv):
        pltpu.make_async_copy(src(me_e), dst, recv).start()

        def go(k):
            to = lax.rem(me_e + k, NE)
            remote(src(to), dst, send, recv, (me_d, to)).start()

        others(NE, go)

    plane(lambda e: packed, lall.at[core, x, me_e], lg_s, lg_r)
    g_dn[0].start()
    g_up[0].start()

    drain(rkbuf, rk_r)

    def choose(zs, half):
        parts = []
        for yy in range(4):
            row = rkbuf[zs, yy : yy + 1, :]
            hot = (jnp.broadcast_to(row, (8, 128)) == sub8.astype(F32)).astype(F32)
            none = jnp.zeros((8, 128), F32)
            parts += [hot, none] if half == 0 else [none, hot]
        return jnp.concatenate(parts, axis=0).astype(BF16)[:, :TOK]

    y_copies = []

    def y_phase(j, own, buf, send_buf, recv_buf, ss, rs):
        first = own[...] if j == 0 else buf[j]
        out = mm(choose(lax.rem(z + j, 8), 0), first)
        out = out + mm(choose(lax.rem(z + 7 - j, 8), 1), buf[7 - j])
        send_buf[j] = out.astype(BF16).reshape(4, 16, D)
        for m in range(1, 4):
            to = lax.rem(y + m, 4)
            c = remote(
                send_buf.at[j, to], recv_buf.at[y, j], ss.at[j, m], rs.at[j, m],
                (me_d, to * 8 + z),
            )
            c.start()
            y_copies.append(c)
        c = pltpu.make_async_copy(send_buf.at[j, y], recv_buf.at[y, j], rs.at[j, 0])
        c.start()

    def y_wait(recv_buf, rs):
        for j in range(4):
            for m in range(4):
                drain(recv_buf.at[0, 0], rs.at[j, m])

    t_dn[0].wait_recv()
    t_dn[1].start()
    t_up[0].wait_recv()
    t_up[1].start()
    y_phase(0, tokens, zt, yt, rt, ys_t, yr_t)
    g_dn[0].wait_recv()
    g_dn[1].start()
    g_up[0].wait_recv()
    g_up[1].start()
    t_dn[1].wait_recv()
    t_dn[2].start()
    t_up[1].wait_recv()
    t_up[2].start()
    y_phase(1, tokens, zt, yt, rt, ys_t, yr_t)

    drain(lall.at[core, x], lg_r)
    others(
        NX,
        lambda k: remote(
            lall.at[core, x], lall.at[core, x], x_s, x_r, (lax.rem(x + k, NX) * 2 + core, me_e)
        ).start(),
    )

    g_dn[1].wait_recv()
    g_dn[2].start()
    g_up[1].wait_recv()
    g_up[2].start()
    t_dn[2].wait_recv()
    t_dn[3].start()
    t_up[2].wait_recv()
    y_phase(2, tokens, zt, yt, rt, ys_t, yr_t)
    y_phase(0, grads, zg, yg, rg, ys_g, yr_g)
    g_dn[2].wait_recv()
    g_up[2].wait_recv()
    g_up[3].start()
    t_dn[3].wait_recv()
    y_phase(3, tokens, zt, yt, rt, ys_t, yr_t)
    y_phase(1, grads, zg, yg, rg, ys_g, yr_g)
    y_phase(2, grads, zg, yg, rg, ys_g, yr_g)
    drain(lall.at[core, pl.ds(0, NX - 1)], x_r)
    logit_pair = remote(lall.at[core], lall.at[core], p_s, p_r, partner)
    logit_pair.start()
    g_up[3].wait_recv()
    y_phase(3, grads, zg, yg, rg, ys_g, yr_g)
    drain(lall.at[1 - core], p_r)

    valid = iota((256, 128), 1) < 96
    li, lj = iota((128, 128), 0), iota((128, 128), 1)
    fold = (lax.rem(li, 32) == lax.rem(lj, 32)).astype(F32)
    block = (li // 32 == lj // 32).astype(F32)

    def rows_of(a):
        return jnp.sum(a.reshape(32, 8, 128), axis=0)

    def first(i, acc):
        d0 = jnp.where(valid, jnp.exp(lall[i // NX, lax.rem(i, NX)].reshape(256, 128)), 0.0)
        dd[i] = d0
        return acc + rows_of(d0)

    acc = lax.fori_loop(0, 8, first, jnp.zeros((8, 128), F32))
    pad = jnp.where(valid, 0.0, 1.0)

    def total(acc):
        one = jnp.broadcast_to(jnp.sum(acc, axis=0, keepdims=True), (8, 128))
        return mm(one, fold, exact=True)

    c = total(acc)
    cols[0:8, :] = c
    for p in range(2):
        def step(i, carry):
            acc, g = carry
            q = dd[i] / c[0:1, :]
            d = q / (mm(q, block, exact=True) + pad)
            dd[i] = d
            return acc + rows_of(d), g + mm(d, d, TN, exact=True)

        acc, g = lax.fori_loop(
            0, 8, step, (jnp.zeros((8, 128), F32), jnp.zeros((128, 128), F32))
        )
        gram[p] = mm(mm(fold, g * block, exact=True), fold, exact=True)
        c = total(acc)
        cols[8 * p + 8 : 8 * p + 16, :] = c

    c3 = jnp.concatenate([cols[0:1, :], cols[8:9, :], cols[16:17, :]], axis=0)
    dens, quot = own_state(logits, c3)
    gates = NE * dens[3]
    tile = jnp.zeros((8, 128), F32)
    for slot in range(CAP):
        one = jnp.sum(jnp.where(rank == slot, gates, 0.0), axis=0, keepdims=True)
        tile = tile + jnp.where(sub8 == slot, jnp.broadcast_to(one, (8, 128)), 0.0)
    gtile[...] = tile
    plane(lambda e: gtile, gbuf.at[me_e], g_s, g_r)

    for c in loads:
        c.wait()
    y_wait(rt, yr_t)
    cuts = []
    for o in range(4):
        at = pl.ds(pl.multiple_of(512 * o + 256 * (1 - core), 256), 256)
        cuts.append(
            remote(rt.at[:, :, :, at], pt.at[o], q_s.at[o], q_r.at[o], partner)
        )
        cuts[-1].start()

    def forward(i, carry):
        at = pl.ds(pl.multiple_of(i * 256, 256), 256)
        rows = rt[...].reshape(256, D)
        gate_pre = mm(rows, wg[:, at])
        up_pre = mm(rows, wu[:, at])
        sg = jax.nn.sigmoid(gate_pre)
        a = gate_pre * sg
        h = a * up_pre
        hid[:, at] = h
        act[:, at] = a
        dsl[:, at] = up_pre * sg * (1.0 + gate_pre * (1.0 - sg))
        ht[at, :] = h.T.astype(BF16)
        return carry

    lax.fori_loop(0, 3, forward, 0)
    ht_copy = remote(ht, pht, q_s.at[4], q_r.at[4], partner)
    ht_copy.start()

    def where_from(k):
        o = lax.rem(k, 8)
        j, h = o // 2, lax.rem(o, 2)
        yy = lax.rem(y + k // 8, 4)
        zz = lax.rem(z + j - h * (2 * j + 1) + 16, 8)
        return yy * 8 + o, yy * 8 + zz

    drain(gbuf, g_r)
    tiles = []
    for yy in range(4):
        for o in range(8):
            j, h = o // 2, o % 2
            tiles.append(gbuf[yy * 8 + lax.rem(z + (j if h == 0 else 7 - j), 8)])
    gate = jnp.sum(
        jnp.where(iota((256, 128), 1) == me_e, jnp.concatenate(tiles, axis=0), 0.0),
        axis=1, keepdims=True,
    ).astype(BF16).astype(F32)

    y_wait(rg, yr_g)
    for b in range(4):
        at = slice(512 * b, 512 * b + 512)
        ds[:, at] = (gate * rg[:, :, :, at].reshape(256, 512).astype(F32)).astype(BF16)
    ds_copy = remote(ds, pds, q_s.at[5], q_r.at[5], partner)
    ds_copy.start()

    def backward(i, total_score):
        at = pl.ds(pl.multiple_of(i * 256, 256), 256)
        at_up = pl.ds(pl.multiple_of(i * 256 + FF, 256), 256)
        h = mm(rg[...].reshape(256, D), wd[at, :], NT)
        a = (h * dsl[:, at]).astype(BF16)
        b = (h * act[:, at]).astype(BF16)
        gg[:, at] = a
        ug[:, at] = b
        pair[:, at] = (gate * a.astype(F32)).astype(BF16)
        pair[:, at_up] = (gate * b.astype(F32)).astype(BF16)
        return total_score + jnp.sum(h * hid[:, at], axis=1, keepdims=True)

    score = lax.fori_loop(0, 3, backward, jnp.zeros((256, 1), F32))
    pair_copy = remote(pair, ppair, q_s.at[6], q_r.at[6], partner)
    pair_copy.start()
    stile[...] = jnp.broadcast_to(score.astype(BF16).astype(F32), (256, 128)).reshape(NE, 8, 128)
    pltpu.make_async_copy(stile.at[where_from(0)[0]], sbuf.at[me_e], sc_r).start()

    def send_score(k):
        n, to = where_from(k)
        remote(stile.at[n], sbuf.at[me_e], sc_s, sc_r, (me_d, to)).start()

    others(NE, send_score)

    ht_copy.wait_recv()
    ds_copy.wait_recv()

    def my_rows(ref, j):
        o = lax.rem(x + j, NX)
        return ref[pl.ds(pl.multiple_of(192 * o + 96 * core, 32), 96), :]

    def down_part(i, carry):
        at = pl.ds(pl.multiple_of(i * 512, 512), 512)
        mine = jnp.concatenate([my_rows(ht, j) for j in range(4)], axis=0)
        theirs = jnp.concatenate([my_rows(pht, j) for j in range(4)], axis=0)
        out = mm(mine, ds[:, at]) + mm(theirs, pds[:, at])
        for j in range(4):
            g2[j, :, at] = out[96 * j : 96 * j + 96].astype(BF16)
        return carry

    lax.fori_loop(0, 4, down_part, 0)
    half = [
        remote(g2.at[2, pl.ds(0, 48)], ra2, h_s.at[0], h_r.at[0], right),
        remote(g2.at[2, pl.ds(48, 48)], rb2, h_s.at[1], h_r.at[1], left),
        remote(g1.at[2, pl.ds(0, 128)], ra1, h_s.at[2], h_r.at[2], right),
        remote(g1.at[2, pl.ds(128, 128)], rb1, h_s.at[3], h_r.at[3], left),
    ]
    half[0].start()
    half[1].start()
    for c in cuts:
        c.wait_recv()
    pair_copy.wait_recv()

    def pair_part(j):
        o = lax.rem(x + j, NX)
        col = pl.ds(pl.multiple_of(512 * o + 256 * core, 256), 256)

        def one(i, carry):
            at = pl.ds(pl.multiple_of(i * 512, 512), 512)
            out = mm(rt[:, :, :, col].reshape(256, 256), pair[:, at], TN)
            out = out + mm(pt[o].reshape(256, 256), ppair[:, at], TN)
            g1[j, :, at] = out.astype(BF16)
            return carry

        lax.fori_loop(0, 3, one, 0)

    pair_part(2)
    half[2].start()
    half[3].start()
    pair_part(1)
    pair_part(3)
    pair_part(0)

    drain(sbuf, sc_r)
    scores = jnp.zeros((8, 128), F32)
    for e in range(NE):
        scores = scores + jnp.where(lane8 == e, sbuf[e], 0.0)
    grad3 = jnp.zeros((TOK, 128), F32)
    for slot in range(CAP):
        grad3 = grad3 + jnp.where(
            rank == slot, jnp.broadcast_to(scores[slot : slot + 1, :], (TOK, 128)), 0.0
        )
    g = NE * grad3 * dens[3]
    h3 = g - dens[3] * jnp.sum(g, axis=1, keepdims=True)
    atile[...] = jnp.broadcast_to(jnp.sum(h3, axis=0, keepdims=True), (8, 128))
    plane(lambda e: atile, abuf.at[me_e], a_s, a_r)

    for b in range(4):
        at = slice(512 * b, 512 * b + 512)
        out = mm(gg[...], wg[at, :], NT) + mm(ug[...], wu[at, :], NT)
        rows = 8 * (b // 2)
        cut = slice(512 * (b % 2), 512 * (b % 2) + 512)
        bsend[:, rows : rows + 8, cut] = out.reshape(NE, 8, 512).astype(BF16)

    def send_back(k):
        n, to = where_from(k)
        remote(bsend.at[n], ret.at[me_e], ret_s, ret_r, (me_d, to)).start()

    pltpu.make_async_copy(bsend.at[where_from(0)[0]], ret.at[me_e], ret_r).start()
    lax.fori_loop(1, 16, lambda k, c: (send_back(k), c)[1], 0)

    gates_hi = gates.astype(BF16).astype(F32)
    ex_i, ex_j = iota((128, 512), 0), iota((128, 512), 1)
    spread = ((ex_i < NE) & (ex_j // 16 == ex_i)).astype(BF16)
    wide = mm(
        jnp.concatenate([rank, gates_hi, gates - gates_hi], axis=0).astype(BF16), spread
    )
    k16 = lax.rem(iota((TOK, 512), 1), 16)
    rank_w = wide[0:TOK].astype(jnp.int32)
    parts = []
    for m in (rank_w == k16, rank_w == k16 - 8):
        parts += [jnp.where(m, wide[TOK : 2 * TOK], 0.0), jnp.where(m, wide[2 * TOK :], 0.0)]
    weights = jnp.concatenate(parts, axis=0).astype(BF16)

    drain(abuf, a_r)
    btile[...] = jnp.sum(abuf[...], axis=0)
    pltpu.make_async_copy(btile, bbuf.at[me_d], b_r).start()
    others(
        ND,
        lambda k: remote(
            btile, bbuf.at[me_d], b_s, b_r, (lax.rem(me_d + k, ND), me_e)
        ).start(),
    )
    early = [
        remote(g2.at[1, pl.ds(48, 48)], rc2.at[pl.ds(48, 48)], n_s.at[0], n_r.at[0], right),
        remote(g2.at[3, pl.ds(0, 48)], rd2.at[pl.ds(0, 48)], n_s.at[1], n_r.at[1], left),
        remote(g1.at[1, pl.ds(128, 128)], rc1.at[pl.ds(128, 128)], n_s.at[2], n_r.at[2], right),
        remote(g1.at[3, pl.ds(0, 128)], rd1.at[pl.ds(0, 128)], n_s.at[3], n_r.at[3], left),
    ]
    for c in early:
        c.start()

    drain(bbuf, b_r)
    v = jnp.sum(bbuf[...], axis=0)
    first32 = lane8 < NE
    u = mm(jnp.where(first32, v / cols[16:24, :], 0.0), gram[1], exact=True)
    s = mm(jnp.where(first32, u / cols[8:16, :], 0.0), gram[0], exact=True)
    qv = quot[2] * v[0:1, :]
    h2 = h3 - qv + dens[2] * jnp.sum(qv, axis=1, keepdims=True)
    qu = quot[1] * u[0:1, :]
    h1 = h2 - qu + dens[1] * jnp.sum(qu, axis=1, keepdims=True)
    lgrad = (h1 - quot[0] * s[0:1, :]).astype(BF16)[:, :NE]
    router_t = mm(lgrad, tokens[...], TN)
    for p in range(NE):
        h, b = p % 2, p // 2
        rsend[p] = router_t[16 * h : 16 * h + 16, 128 * b : 128 * b + 128]
    plane(lambda e: rsend.at[e], rrecv.at[me_e], rs_s, rs_r)
    lax.fori_loop(16, NE, lambda k, c: (send_back(k), c)[1], 0)
    router_in = mm(lgrad, rw[...], NT)

    def add_rows(n, rows, terms, out):
        def one(i, c):
            at = pl.ds(pl.multiple_of(i * rows, rows), rows)
            out(at, functools.reduce(lambda a, b: a + b, [t(at).astype(F32) for t in terms]))
            return c

        lax.fori_loop(0, n // rows, one, 0)

    def put(ref, j, base):
        def f(at, value):
            ref[j, pl.ds(pl.multiple_of(at.start + base, 16), at.size), :] = value.astype(BF16)
        return f

    def take(ref, j, base):
        return lambda at: ref[j, pl.ds(pl.multiple_of(at.start + base, 16), at.size), :]

    for c in half:
        c.wait_recv()
    add_rows(48, 48, [take(g2, 1, 0), lambda at: ra2[at, :]], put(g2, 1, 0))
    add_rows(48, 48, [take(g2, 3, 48), lambda at: rb2[at, :]], put(g2, 3, 48))
    add_rows(128, 32, [take(g1, 1, 0), lambda at: ra1[at, :]], put(g1, 1, 0))
    add_rows(128, 32, [take(g1, 3, 128), lambda at: rb1[at, :]], put(g1, 3, 128))
    late = [
        remote(g2.at[1, pl.ds(0, 48)], rc2.at[pl.ds(0, 48)], m_s.at[0], m_r.at[0], right),
        remote(g2.at[3, pl.ds(48, 48)], rd2.at[pl.ds(48, 48)], m_s.at[1], m_r.at[1], left),
        remote(g1.at[1, pl.ds(0, 128)], rc1.at[pl.ds(0, 128)], m_s.at[2], m_r.at[2], right),
        remote(g1.at[3, pl.ds(128, 128)], rd1.at[pl.ds(128, 128)], m_s.at[3], m_r.at[3], left),
    ]
    late[0].start()
    late[1].start()

    drain(rrecv, rs_r)
    dsum[...] = jnp.sum(rrecv[...], axis=0)
    pltpu.make_async_copy(dsum, drecv.at[me_d], d_r).start()
    others(
        ND,
        lambda k: remote(
            dsum, drecv.at[me_d], d_s, d_r, (lax.rem(me_d + k, ND), me_e)
        ).start(),
    )
    late[2].start()
    late[3].start()
    drain(drecv, d_r)
    fin[...] = jnp.sum(drecv[...], axis=0)
    plane(lambda e: fin, router_out.at[me_e], o_s, o_r)

    drain(ret, ret_r)
    mixed = mm(weights, ret[...].reshape(512, 1024))
    gt_out[:, 0:1024] = (mixed[0:24] + mixed[24:48] + router_in[:, 0:1024]).astype(BF16)
    gt_out[:, 1024:2048] = (mixed[48:72] + mixed[72:96] + router_in[:, 1024:2048]).astype(BF16)

    for c in early + late:
        c.wait_recv()

    def store(ref):
        def f(at, value):
            ref[at, :] = value.astype(BF16)
        return f

    add_rows(
        96, 48, [take(g2, 0, 0), lambda at: rc2[at, :], lambda at: rd2[at, :]], store(down_out)
    )
    add_rows(
        256, 32, [take(g1, 0, 0), lambda at: rc1[at, :], lambda at: rd1[at, :]], store(pair_out)
    )
    drain(router_out, o_r)

    for c in t_dn + t_up + g_dn + g_up + y_copies + cuts + half + early + late:
        c.wait_send()
    for c in (logit_pair, ht_copy, ds_copy, pair_copy):
        c.wait_send()
    drain(rkbuf.at[pl.ds(0, 7)], rk_s)
    drain(lall.at[0, 0, pl.ds(0, NE - 1)], lg_s)
    drain(lall.at[0, pl.ds(0, NX - 1)], x_s)
    drain(gbuf.at[pl.ds(0, NE - 1)], g_s)
    drain(ret.at[pl.ds(0, NE - 1)], ret_s)
    drain(sbuf.at[pl.ds(0, NE - 1)], sc_s)
    drain(abuf.at[pl.ds(0, NE - 1)], a_s)
    drain(bbuf.at[pl.ds(0, ND - 1)], b_s)
    drain(rrecv.at[pl.ds(0, NE - 1)], rs_s)
    drain(drecv.at[pl.ds(0, ND - 1)], d_s)
    drain(router_out.at[pl.ds(0, NE - 1)], o_s)


def moe(*args):
    dma = pltpu.SemaphoreType.DMA
    V = pltpu.VMEM
    hbm = pl.BlockSpec(memory_space=pl.ANY)
    return pl.pallas_call(
        moe_kernel,
        name="moe",
        out_shape=(
            jax.ShapeDtypeStruct((TOK, D), BF16),
            jax.ShapeDtypeStruct((256, 2 * FF), BF16),
            jax.ShapeDtypeStruct((96, D), BF16),
            jax.ShapeDtypeStruct((NE, 16, 128), F32),
        ),
        in_specs=[VM] * 4 + [hbm] * 3,
        out_specs=(VM,) * 4,
        scratch_shapes=[
            V((D, FF), BF16), V((D, FF), BF16), V((FF, D), BF16),
            V((8, 128), F32), V((8, 8, 128), F32), V((8, 8, 128), F32),
            V((2, NX, NE, 8, 128), F32), V((8, 256, 128), F32),
            V((24, 128), F32), V((2, 128, 128), F32), V((8, 128), F32), V((NE, 8, 128), F32),
            V((8, TOK, D), BF16), V((8, TOK, D), BF16),
            V((4, 4, 16, D), BF16), V((4, 4, 16, D), BF16),
            V((4, 4, 16, D), BF16), V((4, 4, 16, D), BF16),
            V((4, 4, 4, 16, 256), BF16),
            V((256, FF), F32), V((256, FF), F32), V((256, FF), F32),
            V((FF, 256), BF16), V((FF, 256), BF16),
            V((256, D), BF16), V((256, D), BF16),
            V((256, FF), BF16), V((256, FF), BF16),
            V((256, 2 * FF), BF16), V((256, 2 * FF), BF16),
            V((4, 256, 2 * FF), BF16), V((4, 96, D), BF16),
            V((128, 2 * FF), BF16), V((48, D), BF16),
            V((128, 2 * FF), BF16), V((48, D), BF16),
            V((256, 2 * FF), BF16), V((96, D), BF16),
            V((256, 2 * FF), BF16), V((96, D), BF16),
            V((NE, 16, 1024), BF16), V((NE, 16, 1024), BF16),
            V((NE, 8, 128), F32), V((NE, 8, 128), F32),
            V((8, 128), F32), V((NE, 8, 128), F32),
            V((8, 128), F32), V((ND, 8, 128), F32),
            V((NE, 16, 128), F32), V((NE, 16, 128), F32),
            V((16, 128), F32), V((ND, 16, 128), F32), V((16, 128), F32),
            dma((3,)),
            dma((8,)), dma((8,)), dma((8,)), dma((8,)),
            dma((4, 4)), dma((4, 4)), dma((4, 4)), dma((4, 4)),
            dma((7,)), dma((7,)),
            dma((4,)), dma((4,)), dma((4,)), dma((4,)), dma((4,)), dma((4,)),
        ]
        + [dma] * 24,
        compiler_params=pltpu.CompilerParams(
            collective_id=0, has_side_effects=True, vmem_limit_bytes=61 * 1024 * 1024
        ),
    )(*args)


def write_kernel(gt, pair, down, router, gt_o, router_o, gate_o, up_o, down_o):
    gt_o[...] = gt[...]
    gate_o[0] = pair[:, 0:FF]
    up_o[0] = pair[:, FF : 2 * FF]
    down_o[0] = down[...]
    for b in range(16):
        t = jnp.concatenate([router[2 * b], router[2 * b + 1]], axis=0)
        router_o[128 * b : 128 * b + 128, :] = t.T


def write(*args):
    return pl.pallas_call(
        write_kernel,
        name="write",
        out_shape=(
            jax.ShapeDtypeStruct((TOK, D), BF16),
            jax.ShapeDtypeStruct((D, NE), F32),
            jax.ShapeDtypeStruct((1, 256, FF), BF16),
            jax.ShapeDtypeStruct((1, 256, FF), BF16),
            jax.ShapeDtypeStruct((1, 96, D), BF16),
        ),
        in_specs=[VM] * 4,
        out_specs=(VM,) * 5,
    )(*args)


def per_device(tokens, out_grad, expert_ids, router_weight, w_gate, w_up, w_down):
    gt, pair, down, router = moe(
        tokens, out_grad, expert_ids, router_weight, w_gate, w_up, w_down
    )
    return write(gt, pair, down, router)


def solution(mesh):
    in_specs = (
        P(("dp", "expert"), None), P(("dp", "expert"), None), P(("dp", "expert"), None), P(),
        P("expert", None, None), P("expert", None, None), P("expert", None, None),
    )
    out_specs = (
        P(("dp", "expert"), None), P(),
        P("expert", "dp", None), P("expert", "dp", None), P("expert", "dp", None),
    )
    return jax.shard_map(
        per_device, mesh=mesh, in_specs=in_specs, out_specs=out_specs, check_vma=False
    )
```

```python
import functools

import jax
import jax.numpy as jnp
from jax import lax
from jax.experimental import pallas as pl
from jax.experimental.pallas import tpu as pltpu
from jax.sharding import PartitionSpec as P

HI = lax.Precision.HIGHEST
F32 = jnp.float32
BF16 = jnp.bfloat16
NE = 32
ND = 8
NX = 4
TOK = 24
CAP = 8
D = 2048
FF = 768
VM = pl.BlockSpec(memory_space=pltpu.VMEM)
MESH = pl.DeviceIdType.MESH


def iota(shape, dim):
    return lax.broadcasted_iota(jnp.int32, shape, dim)


def remote(src, dst, send, recv, dev):
    return pltpu.make_async_remote_copy(
        src_ref=src, dst_ref=dst, send_sem=send, recv_sem=recv, device_id=dev, device_id_type=MESH
    )


def drain(ref, sem):
    pltpu.make_async_copy(ref, ref, sem).wait()


def place():
    me_d = lax.axis_index("dp")
    return me_d, lax.axis_index("expert"), me_d // 2, lax.rem(me_d, 2)


def others(n, body):
    lax.fori_loop(1, n, lambda k, c: (body(k), c)[1], 0)


def own_state(logits, cols):
    lane = iota((TOK, 128), 1)
    d = jnp.where(lane < NE, jnp.exp(logits), 0.0)
    ds, qs = [d], []
    for p in range(3):
        q = d / cols[p : p + 1, :]
        d = q / jnp.sum(q, axis=1, keepdims=True)
        qs.append(q)
        ds.append(d)
    return ds, qs


NT = (((1,), (1,)), ((), ()))
TN = (((0,), (0,)), ((), ()))


def mm(a, b, dims=None, exact=False):
    dims = dims or (((1,), (0,)), ((), ()))
    return lax.dot_general(
        a, b, dims, precision=HI if exact else None, preferred_element_type=F32
    )


def moe_kernel(
    tokens, grads, ids, rw, wg_hbm, wu_hbm, wd_hbm,
    gt_out, pair_out, down_out, router_out,
    wg, wu, wd, zmsg, zin, et, eg, qt, qg, lall, dd, db, cols, gram, gtile, gbuf,
    zt, zg, yt, yg, rt, rg, pt, hid, act, dsl, ht, pht, ds, pds, gg, ug, pair, ppair,
    g1, g2, ra1, ra2, rb1, rb2, rc1, rc2, rd1, rd2,
    bsend, ret, stile, sbuf, atile, abuf, btile, bbuf, rsend, rrecv, dsum, drecv, fin,
    w_sem, zs_t, zr_t, zs_g, zr_g, ys_t, yr_t, ys_g, yr_g, es_t, er_t, es_g, er_g, q_s, q_r, h_s, h_r, n_s, n_r, m_s, m_r,
    lg_s, lg_r, rk_s, rk_r, x_s, x_r, p_s, p_r, g_s, g_r, ret_s, ret_r, sc_s, sc_r,
    a_s, a_r, b_s, b_r, rs_s, rs_r, d_s, d_r, o_s, o_r,
):
    me_d, me_e, x, core = place()
    y, z = me_e // 8, lax.rem(me_e, 8)
    barrier = pltpu.get_barrier_semaphore()
    others(
        NE,
        lambda k: pl.semaphore_signal(
            barrier, inc=1, device_id=(me_d, lax.rem(me_e + k, NE)), device_id_type=MESH
        ),
    )
    others(
        ND,
        lambda k: pl.semaphore_signal(
            barrier, inc=1, device_id=(lax.rem(me_d + k, ND), me_e), device_id_type=MESH
        ),
    )
    loads = [
        pltpu.make_async_copy(a.at[0], b, w_sem.at[n])
        for n, (a, b) in enumerate(((wg_hbm, wg), (wu_hbm, wu), (wd_hbm, wd)))
    ]
    for c in loads:
        c.start()
    partner = (x * 2 + 1 - core, me_e)
    right = (lax.rem(x + 1, NX) * 2 + core, me_e)
    left = (lax.rem(x + 3, NX) * 2 + core, me_e)
    z_up = (me_d, y * 8 + lax.rem(z + 1, 8))
    z_down = (me_d, y * 8 + lax.rem(z + 7, 8))

    lane8, sub8 = iota((8, 128), 1), iota((8, 128), 0)
    logits = jnp.concatenate(
        [mm(tokens[...], rw[...], NT), jnp.zeros((TOK, 96), F32)], axis=1
    )
    packed = (
        logits[0:8] + pltpu.roll(logits[8:16], 32, 1) + pltpu.roll(logits[16:24], 64, 1)
    )
    picked_t = jnp.zeros((128, TOK), F32)
    for k in range(8):
        picked_t = picked_t + (ids[k : k + 1, :] == iota((128, TOK), 0)).astype(F32)
    picked_t = picked_t.astype(BF16)
    row_t, col_t = iota((TOK, TOK), 0), iota((TOK, TOK), 1)
    picked = mm((row_t == col_t).astype(BF16), picked_t, NT)
    rank = jnp.where(picked > 0, mm((row_t > col_t).astype(BF16), picked_t, NT), -64.0)
    rank_pad = jnp.concatenate([rank, jnp.full((104, 128), -64.0, F32)], axis=0).astype(BF16)
    pi, pj = iota((64, 128), 0), iota((64, 128), 1)
    place_rows = ((lax.rem(pi, 8) < 4) & (pj == lax.rem(pi, 8) * 8 + pi // 8)).astype(BF16)
    zmsg[:, 0:8, :] = mm(place_rows, rank_pad, NT).reshape(8, 8, 128)
    zmsg[:, 8:16, :] = jnp.broadcast_to(packed[None], (8, 8, 128))

    pl.semaphore_wait(barrier, NE - 1 + ND - 1)

    def z_send(k):
        to = lax.rem(z + k, 8)
        remote(zmsg.at[to], zin.at[z], rk_s, rk_r, (me_d, y * 8 + to)).start()

    pltpu.make_async_copy(zmsg.at[z], zin.at[z], rk_r).start()
    others(8, z_send)

    def z_copy(own, buf, ss, rs, k, sign):
        at = lambda n: (8 + sign * n) % 8
        return remote(
            own if k == 1 else buf.at[at(k - 1)], buf.at[at(k)], ss.at[at(k)], rs.at[at(k)],
            z_down if sign > 0 else z_up,
        )

    t_dn = [z_copy(tokens, zt, zs_t, zr_t, k, -1) for k in (1, 2, 3, 4)]
    t_up = [z_copy(tokens, zt, zs_t, zr_t, k, 1) for k in (1, 2, 3)]
    g_dn = [z_copy(grads, zg, zs_g, zr_g, k, -1) for k in (1, 2, 3)]
    g_up = [z_copy(grads, zg, zs_g, zr_g, k, 1) for k in (1, 2, 3, 4)]
    t_dn[0].start()
    t_up[0].start()

    g_dn[0].start()
    g_up[0].start()

    def hot(ref, at, yy):
        row = ref[at, yy : yy + 1, :]
        return (jnp.broadcast_to(row, (8, 128)) == sub8.astype(F32)).astype(F32)

    def choose(at, half):
        none = jnp.zeros((8, 128), F32)
        parts = []
        for yy in range(4):
            one = hot(zin, at, yy)
            parts += [one, none] if half == 0 else [none, one]
        return jnp.concatenate(parts, axis=0).astype(BF16)[:, :TOK]

    y_copies = []

    def y_send(src, dst, ss, rs, j):
        for m in range(1, 4):
            to = lax.rem(y + m, 4)
            c = remote(src(to), dst, ss.at[j, m], rs.at[j, m], (me_d, to * 8 + z))
            c.start()
            y_copies.append(c)
        pltpu.make_async_copy(src(y), dst, rs.at[j, 0]).start()

    def y_pair(j, buf, send_buf, recv_buf, ss, rs):
        out = mm(choose(lax.rem(z + 8 - j, 8), 0), buf[8 - j])
        out = out + mm(choose(lax.rem(z + j, 8), 1), buf[j])
        send_buf[j] = out.astype(BF16).reshape(4, 16, D)
        y_send(lambda to: send_buf.at[j, to], recv_buf.at[y, j], ss, rs, j)

    def y_single(n, block, ref, at, send_buf, recv_buf, ss, rs):
        pick = jnp.concatenate([hot(ref, at, yy) for yy in range(4)], axis=0)
        out = mm(pick.astype(BF16)[:, :TOK], block)
        for yy in range(4):
            rows = out[8 * yy : 8 * yy + 8]
            send_buf[n, yy] = jnp.concatenate([rows[:, :1024], rows[:, 1024:]], axis=0).astype(BF16)
        y_send(lambda to: send_buf.at[n, to], recv_buf.at[y, n], ss, rs, n)

    def y_wait(recv_buf, rs, one_buf, one_rs):
        for m in range(4):
            for j in range(1, 4):
                drain(recv_buf.at[0, 0], rs.at[j, m])
            for n in range(2):
                drain(one_buf.at[0, 0], one_rs.at[n, m])
        for yy in range(4):
            parts = []
            for n in range(2):
                a = one_buf[yy, n].astype(F32)
                parts.append(jnp.concatenate([a[0:8], a[8:16]], axis=1))
            recv_buf[yy, 0] = jnp.concatenate(parts, axis=0).astype(BF16)

    def arrive(down, up, k):
        if k < len(down):
            down[k].wait_recv()
            if k + 1 < len(down):
                down[k + 1].start()
        if k < len(up):
            up[k].wait_recv()
            if k + 1 < len(up):
                up[k + 1].start()

    y_single(0, tokens[...], zmsg, z, et, qt, es_t, er_t)
    y_single(0, grads[...], zmsg, z, eg, qg, es_g, er_g)

    drain(zin, rk_r)
    own_z = zin.at[:, pl.ds(8, 8), :]
    own_rows = lall.at[core, x, pl.ds(pl.multiple_of(y * 8, 8), 8)]
    pltpu.make_async_copy(own_z, own_rows, lg_r).start()
    lg_copies = []
    for m in range(1, 4):
        c = remote(
            own_z, own_rows, lg_s.at[m - 1], lg_r, (me_d, lax.rem(y + m, 4) * 8 + z)
        )
        c.start()
        lg_copies.append(c)

    arrive(t_dn, t_up, 0)
    y_pair(1, zt, yt, rt, ys_t, yr_t)
    drain(lall.at[core, x], lg_r)
    others(
        NX,
        lambda k: remote(
            lall.at[core, x], lall.at[core, x], x_s, x_r, (lax.rem(x + k, NX) * 2 + core, me_e)
        ).start(),
    )
    arrive(g_dn, g_up, 0)
    y_pair(1, zg, yg, rg, ys_g, yr_g)
    arrive(t_dn, t_up, 1)
    y_pair(2, zt, yt, rt, ys_t, yr_t)
    arrive(g_dn, g_up, 1)
    y_pair(2, zg, yg, rg, ys_g, yr_g)
    arrive(t_dn, t_up, 2)
    y_pair(3, zt, yt, rt, ys_t, yr_t)
    drain(lall.at[core, pl.ds(0, NX - 1)], x_r)
    logit_pair = remote(lall.at[core], lall.at[core], p_s, p_r, partner)
    logit_pair.start()
    arrive(g_dn, g_up, 2)
    far = lax.rem(z + 4, 8)
    arrive(t_dn, t_up, 3)
    y_single(1, zt[4], zin, far, et, qt, es_t, er_t)
    y_pair(3, zg, yg, rg, ys_g, yr_g)
    drain(lall.at[1 - core], p_r)

    valid = iota((1024, 128), 1) < 96
    li, lj = iota((128, 128), 0), iota((128, 128), 1)
    fold = (lax.rem(li, 32) == lax.rem(lj, 32)).astype(F32)
    block = (li // 32 == lj // 32).astype(F32)
    block_h = block.astype(BF16)

    def rows_of(a):
        return jnp.sum(jnp.sum(a.reshape(8, 16, 8, 128), axis=1), axis=0)

    def total(acc):
        one = jnp.broadcast_to(jnp.sum(acc, axis=0, keepdims=True), (8, 128))
        return mm(one, fold, exact=True)

    acc = jnp.zeros((8, 128), F32)
    for i in range(2):
        d0 = jnp.where(valid, jnp.exp(lall[i].reshape(1024, 128)), 0.0)
        dd[i] = d0
        acc = acc + rows_of(d0)
    pad = jnp.where(iota((1, 128), 1) < 96, 0.0, 1.0)
    c = total(acc)
    cols[0:8, :] = c
    for p in range(2):
        acc = jnp.zeros((8, 128), F32)
        inverse = 1.0 / c[0:1, :]
        for i in range(2):
            q = dd[i] * inverse
            q_hi = q.astype(BF16)
            q_lo = (q - q_hi.astype(F32)).astype(BF16)
            d = q / (mm(q_hi, block_h) + mm(q_lo, block_h) + pad)
            if p == 0:
                dd[i] = d
            db[p, i] = d.astype(BF16)
            acc = acc + rows_of(d)
        c = total(acc)
        cols[8 * p + 8 : 8 * p + 16, :] = c

    c3 = jnp.concatenate([cols[0:1, :], cols[8:9, :], cols[16:17, :]], axis=0)
    dens, quot = own_state(logits, c3)
    gates = NE * dens[3]
    tile = jnp.zeros((8, 128), F32)
    for slot in range(CAP):
        one = jnp.sum(jnp.where(rank == slot, gates, 0.0), axis=0, keepdims=True)
        tile = tile + jnp.where(sub8 == slot, jnp.broadcast_to(one, (8, 128)), 0.0)
    eye8 = (iota((8, 128), 0) == lane8).astype(BF16)
    gtile[...] = mm(tile.astype(BF16), eye8, TN)[0:NE].reshape(NE, 1, 128)
    def plane(src, dst, send, recv):
        pltpu.make_async_copy(src(me_e), dst, recv).start()

        def go(k):
            to = lax.rem(me_e + k, NE)
            remote(src(to), dst, send, recv, (me_d, to)).start()

        others(NE, go)

    plane(lambda e: gtile.at[e], gbuf.at[me_e], g_s, g_r)
    arrive(g_dn, g_up, 3)
    y_single(1, zg[4], zin, far, eg, qg, es_g, er_g)

    for c in loads:
        c.wait()
    y_wait(rt, yr_t, qt, er_t)
    cuts = []
    for o in range(4):
        at = pl.ds(pl.multiple_of(512 * o + 256 * (1 - core), 256), 256)
        cuts.append(
            remote(rt.at[:, :, :, at], pt.at[o], q_s.at[o], q_r.at[o], partner)
        )
        cuts[-1].start()

    def forward(i, carry):
        at = pl.ds(pl.multiple_of(i * 256, 256), 256)
        rows = rt[...].reshape(256, D)
        gate_pre = mm(rows, wg[:, at])
        up_pre = mm(rows, wu[:, at])
        sg = jax.nn.sigmoid(gate_pre)
        a = gate_pre * sg
        h = a * up_pre
        hid[:, at] = h
        act[:, at] = a
        dsl[:, at] = up_pre * sg * (1.0 + gate_pre * (1.0 - sg))
        ht[at, :] = h.T.astype(BF16)
        return carry

    lax.fori_loop(0, 3, forward, 0)
    ht_copy = remote(ht, pht, q_s.at[4], q_r.at[4], partner)
    ht_copy.start()

    def where_from(k):
        o = lax.rem(k, 8)
        j, h = o // 2, lax.rem(o, 2)
        yy = lax.rem(y + k // 8, 4)
        zz = lax.rem(z + h * (j + 4 * ((4 - j) // 4)) + (1 - h) * (8 - j), 8)
        return yy * 8 + o, yy * 8 + zz

    drain(gbuf, g_r)
    tiles = []
    for yy in range(4):
        for off in (0, 4, 7, 1, 6, 2, 5, 3):
            one = gbuf[yy * 8 + lax.rem(z + off, 8)]
            tiles.append(jnp.where(lane8 == sub8, jnp.broadcast_to(one, (8, 128)), 0.0))
    gate = jnp.sum(jnp.concatenate(tiles, axis=0), axis=1, keepdims=True)

    y_wait(rg, yr_g, qg, er_g)
    for b in range(4):
        at = slice(512 * b, 512 * b + 512)
        ds[:, at] = (gate * rg[:, :, :, at].reshape(256, 512).astype(F32)).astype(BF16)
    ds_copy = remote(ds, pds, q_s.at[5], q_r.at[5], partner)
    ds_copy.start()

    def backward(i, total_score):
        at = pl.ds(pl.multiple_of(i * 256, 256), 256)
        at_up = pl.ds(pl.multiple_of(i * 256 + FF, 256), 256)
        h = mm(rg[...].reshape(256, D), wd[at, :], NT)
        a = (h * dsl[:, at]).astype(BF16)
        b = (h * act[:, at]).astype(BF16)
        gg[:, at] = a
        ug[:, at] = b
        pair[:, at] = (gate * a.astype(F32)).astype(BF16)
        pair[:, at_up] = (gate * b.astype(F32)).astype(BF16)
        return total_score + jnp.sum(h * hid[:, at], axis=1, keepdims=True)

    score = lax.fori_loop(0, 3, backward, jnp.zeros((256, 1), F32))
    pair_copy = remote(pair, ppair, q_s.at[6], q_r.at[6], partner)
    pair_copy.start()
    spread8 = jnp.broadcast_to(score.astype(BF16).astype(F32), (256, 128)).reshape(NE, 8, 128)
    diag = iota((NE, 8, 128), 1) == iota((NE, 8, 128), 2)
    stile[...] = jnp.sum(jnp.where(diag, spread8, 0.0), axis=1).reshape(NE, 1, 128)
    pltpu.make_async_copy(stile.at[where_from(0)[0]], sbuf.at[me_e], sc_r).start()

    def send_score(k):
        n, to = where_from(k)
        remote(stile.at[n], sbuf.at[me_e], sc_s, sc_r, (me_d, to)).start()

    others(NE, send_score)

    ht_copy.wait_recv()
    ds_copy.wait_recv()

    def my_rows(ref, j):
        o = lax.rem(x + j, NX)
        return ref[pl.ds(pl.multiple_of(192 * o + 96 * core, 32), 96), :]

    def down_part(i, carry):
        at = pl.ds(pl.multiple_of(i * 512, 512), 512)
        mine = jnp.concatenate([my_rows(ht, j) for j in range(4)], axis=0)
        theirs = jnp.concatenate([my_rows(pht, j) for j in range(4)], axis=0)
        out = mm(mine, ds[:, at]) + mm(theirs, pds[:, at])
        for j in range(4):
            g2[j, :, at] = out[96 * j : 96 * j + 96].astype(BF16)
        return carry

    lax.fori_loop(0, 4, down_part, 0)
    half = [
        remote(g2.at[2, pl.ds(0, 48)], ra2, h_s.at[0], h_r.at[0], right),
        remote(g2.at[2, pl.ds(48, 48)], rb2, h_s.at[1], h_r.at[1], left),
    ]
    for n in range(2):
        at = pl.ds(64 * n, 64)
        half += [
            remote(g1.at[2, at], ra1.at[at], h_s.at[2 * n + 2], h_r.at[2 * n + 2], right),
            remote(
                g1.at[2, pl.ds(128 + 64 * n, 64)], rb1.at[at],
                h_s.at[2 * n + 3], h_r.at[2 * n + 3], left,
            ),
        ]
    half[0].start()
    half[1].start()
    for c in cuts:
        c.wait_recv()
    pair_copy.wait_recv()

    def pair_part(j):
        o = lax.rem(x + j, NX)
        col = pl.ds(pl.multiple_of(512 * o + 256 * core, 256), 256)

        def one(i, carry):
            at = pl.ds(pl.multiple_of(i * 512, 512), 512)
            out = mm(rt[:, :, :, col].reshape(256, 256), pair[:, at], TN)
            out = out + mm(pt[o].reshape(256, 256), ppair[:, at], TN)
            g1[j, :, at] = out.astype(BF16)
            return carry

        lax.fori_loop(0, 3, one, 0)

    pair_part(2)
    half[2].start()
    half[3].start()
    for b in range(4):
        at = slice(512 * b, 512 * b + 512)
        out = mm(gg[...], wg[at, :], NT) + mm(ug[...], wu[at, :], NT)
        rows = 8 * (b // 2)
        cut = slice(512 * (b % 2), 512 * (b % 2) + 512)
        bsend[:, rows : rows + 8, cut] = out.reshape(NE, 8, 512).astype(BF16)

    def send_back(k):
        n, to = where_from(k)
        remote(bsend.at[n], ret.at[me_e], ret_s, ret_r, (me_d, to)).start()

    pltpu.make_async_copy(bsend.at[where_from(0)[0]], ret.at[me_e], ret_r).start()
    lax.fori_loop(1, 5, lambda k, c: (send_back(k), c)[1], 0)
    pair_part(1)
    pair_part(3)
    pair_part(0)

    drain(sbuf, sc_r)
    eye32 = (iota((NE, 128), 0) == iota((NE, 128), 1)).astype(BF16)
    scores = mm(sbuf[...].reshape(NE, 128).astype(BF16), eye32, TN)
    grad3 = jnp.zeros((TOK, 128), F32)
    for slot in range(CAP):
        grad3 = grad3 + jnp.where(
            rank == slot, jnp.broadcast_to(scores[slot : slot + 1, :], (TOK, 128)), 0.0
        )
    g = NE * grad3 * dens[3]
    h3 = g - dens[3] * jnp.sum(g, axis=1, keepdims=True)
    atile[...] = jnp.sum(h3, axis=0, keepdims=True)
    plane(lambda e: atile, abuf.at[me_e], a_s, a_r)
    lax.fori_loop(5, 16, lambda k, c: (send_back(k), c)[1], 0)

    gates_hi = gates.astype(BF16).astype(F32)
    ex_i, ex_j = iota((128, 512), 0), iota((128, 512), 1)
    spread = ((ex_i < NE) & (ex_j // 16 == ex_i)).astype(BF16)
    wide = mm(
        jnp.concatenate([rank, gates_hi, gates - gates_hi], axis=0).astype(BF16), spread
    )
    k16 = lax.rem(iota((TOK, 512), 1), 16)
    rank_w = wide[0:TOK].astype(jnp.int32)
    parts = []
    for m in (rank_w == k16, rank_w == k16 - 8):
        parts += [jnp.where(m, wide[TOK : 2 * TOK], 0.0), jnp.where(m, wide[2 * TOK :], 0.0)]
    weights = jnp.concatenate(parts, axis=0).astype(BF16)

    for p in range(2):
        dens_h = db[p].reshape(2048, 128)
        g = mm(dens_h, dens_h, TN)
        gram[p] = mm(mm(fold, g * block, exact=True), fold, exact=True)

    drain(abuf, a_r)
    btile[...] = jnp.sum(abuf[...], axis=0)
    pltpu.make_async_copy(btile, bbuf.at[me_d], b_r).start()
    others(
        ND,
        lambda k: remote(
            btile, bbuf.at[me_d], b_s, b_r, (lax.rem(me_d + k, ND), me_e)
        ).start(),
    )
    half[4].start()
    half[5].start()
    early = [
        remote(g2.at[1, pl.ds(48, 48)], rc2.at[pl.ds(48, 48)], n_s.at[0], n_r.at[0], right),
        remote(g2.at[3, pl.ds(0, 48)], rd2.at[pl.ds(0, 48)], n_s.at[1], n_r.at[1], left),
    ]
    for n in range(2):
        up, down = pl.ds(128 + 64 * n, 64), pl.ds(64 * n, 64)
        early += [
            remote(g1.at[1, up], rc1.at[up], n_s.at[2 * n + 2], n_r.at[2 * n + 2], right),
            remote(g1.at[3, down], rd1.at[down], n_s.at[2 * n + 3], n_r.at[2 * n + 3], left),
        ]
    for c in early[0:4]:
        c.start()

    drain(bbuf, b_r)
    v = jnp.broadcast_to(jnp.sum(bbuf[...], axis=0), (8, 128))
    first32 = lane8 < NE
    u = mm(jnp.where(first32, v / cols[16:24, :], 0.0), gram[1], exact=True)
    s = mm(jnp.where(first32, u / cols[8:16, :], 0.0), gram[0], exact=True)
    qv = quot[2] * v[0:1, :]
    h2 = h3 - qv + dens[2] * jnp.sum(qv, axis=1, keepdims=True)
    qu = quot[1] * u[0:1, :]
    h1 = h2 - qu + dens[1] * jnp.sum(qu, axis=1, keepdims=True)
    lgrad = (h1 - quot[0] * s[0:1, :]).astype(BF16)[:, :NE]
    router_t = mm(lgrad, tokens[...], TN)
    for p in range(NE):
        h, b = p % 2, p // 2
        rsend[p] = router_t[16 * h : 16 * h + 16, 128 * b : 128 * b + 128].astype(BF16)
    plane(lambda e: rsend.at[e], rrecv.at[me_e], rs_s, rs_r)
    lax.fori_loop(16, NE, lambda k, c: (send_back(k), c)[1], 0)
    router_in = mm(lgrad, rw[...])

    def add_rows(n, rows, terms, out):
        def one(i, c):
            at = pl.ds(pl.multiple_of(i * rows, rows), rows)
            out(at, functools.reduce(lambda a, b: a + b, [t(at).astype(F32) for t in terms]))
            return c

        lax.fori_loop(0, n // rows, one, 0)

    def put(ref, j, base):
        def f(at, value):
            ref[j, pl.ds(pl.multiple_of(at.start + base, 16), at.size), :] = value.astype(BF16)
        return f

    def take(ref, j, base):
        return lambda at: ref[j, pl.ds(pl.multiple_of(at.start + base, 16), at.size), :]

    for c in half:
        c.wait_recv()
    add_rows(48, 48, [take(g2, 1, 0), lambda at: ra2[at, :]], put(g2, 1, 0))
    add_rows(48, 48, [take(g2, 3, 48), lambda at: rb2[at, :]], put(g2, 3, 48))
    add_rows(128, 32, [take(g1, 1, 0), lambda at: ra1[at, :]], put(g1, 1, 0))
    add_rows(128, 32, [take(g1, 3, 128), lambda at: rb1[at, :]], put(g1, 3, 128))
    late = [
        remote(g2.at[1, pl.ds(0, 48)], rc2.at[pl.ds(0, 48)], m_s.at[0], m_r.at[0], right),
        remote(g2.at[3, pl.ds(48, 48)], rd2.at[pl.ds(48, 48)], m_s.at[1], m_r.at[1], left),
        remote(g1.at[1, pl.ds(0, 128)], rc1.at[pl.ds(0, 128)], m_s.at[2], m_r.at[2], right),
        remote(g1.at[3, pl.ds(128, 128)], rd1.at[pl.ds(128, 128)], m_s.at[3], m_r.at[3], left),
    ]
    drain(rrecv, rs_r)
    dsum[...] = jnp.sum(rrecv[...].astype(F32), axis=0).astype(BF16)
    pltpu.make_async_copy(dsum, drecv.at[me_d], d_r).start()
    others(
        ND,
        lambda k: remote(
            dsum, drecv.at[me_d], d_s, d_r, (lax.rem(me_d + k, ND), me_e)
        ).start(),
    )
    early[4].start()
    early[5].start()
    for c in late:
        c.start()
    drain(drecv, d_r)
    fin[...] = jnp.sum(drecv[...].astype(F32), axis=0).astype(BF16)
    plane(lambda e: fin, router_out.at[me_e], o_s, o_r)

    drain(ret, ret_r)
    mixed = mm(weights, ret[...].reshape(512, 1024))
    gt_out[:, 0:1024] = (mixed[0:24] + mixed[24:48] + router_in[:, 0:1024]).astype(BF16)
    gt_out[:, 1024:2048] = (mixed[48:72] + mixed[72:96] + router_in[:, 1024:2048]).astype(BF16)

    for c in early + late:
        c.wait_recv()

    def store(ref):
        def f(at, value):
            ref[at, :] = value.astype(BF16)
        return f

    add_rows(
        96, 48, [take(g2, 0, 0), lambda at: rc2[at, :], lambda at: rd2[at, :]], store(down_out)
    )
    add_rows(
        256, 32, [take(g1, 0, 0), lambda at: rc1[at, :], lambda at: rd1[at, :]], store(pair_out)
    )
    drain(router_out, o_r)

    for c in t_dn + t_up + g_dn + g_up + y_copies + lg_copies + cuts + half + early + late:
        c.wait_send()
    for c in (logit_pair, ht_copy, ds_copy, pair_copy):
        c.wait_send()
    drain(zin.at[pl.ds(0, 7)], rk_s)
    drain(lall.at[0, pl.ds(0, NX - 1)], x_s)
    drain(gbuf.at[pl.ds(0, NE - 1)], g_s)
    drain(ret.at[pl.ds(0, NE - 1)], ret_s)
    drain(sbuf.at[pl.ds(0, NE - 1)], sc_s)
    drain(abuf.at[pl.ds(0, NE - 1)], a_s)
    drain(bbuf.at[pl.ds(0, ND - 1)], b_s)
    drain(rrecv.at[pl.ds(0, NE - 1)], rs_s)
    drain(drecv.at[pl.ds(0, ND - 1)], d_s)
    drain(router_out.at[pl.ds(0, NE - 1)], o_s)


def moe(*args):
    dma = pltpu.SemaphoreType.DMA
    V = pltpu.VMEM
    hbm = pl.BlockSpec(memory_space=pltpu.HBM)
    return pl.pallas_call(
        moe_kernel,
        name="moe",
        out_shape=(
            jax.ShapeDtypeStruct((TOK, D), BF16),
            jax.ShapeDtypeStruct((256, 2 * FF), BF16),
            jax.ShapeDtypeStruct((96, D), BF16),
            jax.ShapeDtypeStruct((NE, 16, 128), BF16),
        ),
        in_specs=[VM] * 4 + [hbm] * 3,
        out_specs=(VM,) * 4,
        scratch_shapes=[
            V((D, FF), BF16), V((D, FF), BF16), V((FF, D), BF16),
            V((8, 16, 128), F32), V((8, 16, 128), F32),
            V((2, 4, 16, 1024), BF16), V((2, 4, 16, 1024), BF16),
            V((4, 2, 16, 1024), BF16), V((4, 2, 16, 1024), BF16),
            V((2, NX, NE, 8, 128), F32), V((2, 1024, 128), F32), V((2, 2, 1024, 128), BF16),
            V((24, 128), F32), V((2, 128, 128), F32), V((NE, 1, 128), F32), V((NE, 1, 128), F32),
            V((8, TOK, D), BF16), V((8, TOK, D), BF16),
            V((4, 4, 16, D), BF16), V((4, 4, 16, D), BF16),
            V((4, 4, 16, D), BF16), V((4, 4, 16, D), BF16),
            V((4, 4, 4, 16, 256), BF16),
            V((256, FF), F32), V((256, FF), F32), V((256, FF), F32),
            V((FF, 256), BF16), V((FF, 256), BF16),
            V((256, D), BF16), V((256, D), BF16),
            V((256, FF), BF16), V((256, FF), BF16),
            V((256, 2 * FF), BF16), V((256, 2 * FF), BF16),
            V((4, 256, 2 * FF), BF16), V((4, 96, D), BF16),
            V((128, 2 * FF), BF16), V((48, D), BF16),
            V((128, 2 * FF), BF16), V((48, D), BF16),
            V((256, 2 * FF), BF16), V((96, D), BF16),
            V((256, 2 * FF), BF16), V((96, D), BF16),
            V((NE, 16, 1024), BF16), V((NE, 16, 1024), BF16),
            V((NE, 1, 128), F32), V((NE, 1, 128), F32),
            V((1, 128), F32), V((NE, 1, 128), F32),
            V((1, 128), F32), V((ND, 1, 128), F32),
            V((NE, 16, 128), BF16), V((NE, 16, 128), BF16),
            V((16, 128), BF16), V((ND, 16, 128), BF16), V((16, 128), BF16),
            dma((3,)),
            dma((8,)), dma((8,)), dma((8,)), dma((8,)),
            dma((4, 4)), dma((4, 4)), dma((4, 4)), dma((4, 4)),
            dma((2, 4)), dma((2, 4)), dma((2, 4)), dma((2, 4)),
            dma((7,)), dma((7,)),
            dma((6,)), dma((6,)), dma((6,)), dma((6,)), dma((4,)), dma((4,)), dma((3,)),
        ]
        + [dma] * 23,
        compiler_params=pltpu.CompilerParams(
            collective_id=0, has_side_effects=True, vmem_limit_bytes=52 * 1024 * 1024
        ),
    )(*args)


def write_kernel(gt, pair, down, router, gt_o, router_o, gate_o, up_o, down_o):
    gt_o[...] = gt[...]
    gate_o[0] = pair[:, 0:FF]
    up_o[0] = pair[:, FF : 2 * FF]
    down_o[0] = down[...]
    for p in range(NE):
        h, b = p % 2, p // 2
        router_o[16 * h : 16 * h + 16, 128 * b : 128 * b + 128] = router[p].astype(F32)


def write(*args):
    return pl.pallas_call(
        write_kernel,
        name="write",
        out_shape=(
            jax.ShapeDtypeStruct((TOK, D), BF16),
            jax.ShapeDtypeStruct((NE, D), F32),
            jax.ShapeDtypeStruct((1, 256, FF), BF16),
            jax.ShapeDtypeStruct((1, 256, FF), BF16),
            jax.ShapeDtypeStruct((1, 96, D), BF16),
        ),
        in_specs=[VM] * 4,
        out_specs=(VM,) * 5,
        compiler_params=pltpu.CompilerParams(vmem_limit_bytes=16 * 1024 * 1024),
    )(*args)


def per_device(tokens, out_grad, expert_ids, router_weight, w_gate, w_up, w_down):
    gt, pair, down, router = moe(
        tokens, out_grad, expert_ids.T, router_weight.T, w_gate, w_up, w_down
    )
    gt, router, gate, up, down = write(gt, pair, down, router)
    return gt, router.T, gate, up, down


def solution(mesh):
    in_specs = (
        P(("dp", "expert"), None), P(("dp", "expert"), None), P(("dp", "expert"), None), P(),
        P("expert", None, None), P("expert", None, None), P("expert", None, None),
    )
    out_specs = (
        P(("dp", "expert"), None), P(),
        P("expert", "dp", None), P("expert", "dp", None), P("expert", "dp", None),
    )
    return jax.shard_map(
        per_device, mesh=mesh, in_specs=in_specs, out_specs=out_specs, check_vma=False
    )
```

```python
import functools

import jax
import jax.numpy as jnp
from jax import lax
from jax.experimental import pallas as pl
from jax.experimental.pallas import tpu as pltpu
from jax.sharding import PartitionSpec as P

HI = lax.Precision.HIGHEST
F32 = jnp.float32
BF16 = jnp.bfloat16
NE = 32
ND = 8
NX = 4
TOK = 24
CAP = 8
D = 2048
FF = 768
VM = pl.BlockSpec(memory_space=pltpu.VMEM)
MESH = pl.DeviceIdType.MESH


def iota(shape, dim):
    return lax.broadcasted_iota(jnp.int32, shape, dim)


def remote(src, dst, send, recv, dev):
    return pltpu.make_async_remote_copy(
        src_ref=src, dst_ref=dst, send_sem=send, recv_sem=recv, device_id=dev, device_id_type=MESH
    )


def drain(ref, sem):
    pltpu.make_async_copy(ref, ref, sem).wait()


def place():
    me_d = lax.axis_index("dp")
    return me_d, lax.axis_index("expert"), me_d // 2, lax.rem(me_d, 2)


def others(n, body):
    lax.fori_loop(1, n, lambda k, c: (body(k), c)[1], 0)


def own_state(logits, cols):
    lane = iota((TOK, 128), 1)
    d = jnp.where(lane < NE, jnp.exp(logits), 0.0)
    ds, qs = [d], []
    for p in range(3):
        q = d / cols[p : p + 1, :]
        d = q / jnp.sum(q, axis=1, keepdims=True)
        qs.append(q)
        ds.append(d)
    return ds, qs


NT = (((1,), (1,)), ((), ()))
TN = (((0,), (0,)), ((), ()))


def mm(a, b, dims=None, exact=False):
    dims = dims or (((1,), (0,)), ((), ()))
    return lax.dot_general(
        a, b, dims, precision=HI if exact else None, preferred_element_type=F32
    )


def moe_kernel(
    tokens, grads, ids, rw, wg_hbm, wu_hbm, wd_hbm,
    gt_out, pair_out, down_out, router_out,
    wg, wu, wd, rk_out, rk_in, rk_col, pk_out, pk_in, et, eg, qt, qg,
    lall, dd, db, cols, gram, gcol,
    zt, zg, yt, yg, rt, rg, pt, hid, act, dsl, ht, pht, ds, pds, gg, ug, pair, ppair,
    g1, g2, ra1, ra2, rb1, rb2, rc1, rc2, rd1, rd2,
    bsend, ret, stile, sbuf, atile, abuf, btile, bbuf, rsend, rrecv, dsum, drecv, fin,
    w_sem, zs_t, zr_t, zs_g, zr_g, ys_t, yr_t, ys_g, yr_g, es_t, er_t, es_g, er_g, q_s, q_r, h_s, h_r, n_s, n_r, m_s, m_r,
    lg_s, lg_r, rc_s, rc_r, rk_s, rk_r, pk_s, pk_r, x_s, x_r, p_s, p_r, ret_s, ret_r, sc_s, sc_r,
    a_s, a_r, b_s, b_r, rs_s, rs_r, d_s, d_r, o_s, o_r,
):
    me_d, me_e, x, core = place()
    y, z = me_e // 8, lax.rem(me_e, 8)
    barrier = pltpu.get_barrier_semaphore()
    others(
        NE,
        lambda k: pl.semaphore_signal(
            barrier, inc=1, device_id=(me_d, lax.rem(me_e + k, NE)), device_id_type=MESH
        ),
    )
    others(
        ND,
        lambda k: pl.semaphore_signal(
            barrier, inc=1, device_id=(lax.rem(me_d + k, ND), me_e), device_id_type=MESH
        ),
    )
    loads = [
        pltpu.make_async_copy(a.at[0], b, w_sem.at[n])
        for n, (a, b) in enumerate(((wg_hbm, wg), (wu_hbm, wu), (wd_hbm, wd)))
    ]
    for c in loads:
        c.start()
    partner = (x * 2 + 1 - core, me_e)
    right = (lax.rem(x + 1, NX) * 2 + core, me_e)
    left = (lax.rem(x + 3, NX) * 2 + core, me_e)
    z_up = (me_d, y * 8 + lax.rem(z + 1, 8))
    z_down = (me_d, y * 8 + lax.rem(z + 7, 8))

    lane8, sub8 = iota((8, 128), 1), iota((8, 128), 0)
    logits = jnp.concatenate(
        [mm(tokens[...], rw[...], NT), jnp.zeros((TOK, 96), F32)], axis=1
    )
    packed = (
        logits[0:8] + pltpu.roll(logits[8:16], 32, 1) + pltpu.roll(logits[16:24], 64, 1)
    )
    picked_t = jnp.zeros((128, TOK), F32)
    for k in range(8):
        picked_t = picked_t + (ids[k : k + 1, :] == iota((128, TOK), 0)).astype(F32)
    picked_t = picked_t.astype(BF16)
    row_t, col_t = iota((TOK, TOK), 0), iota((TOK, TOK), 1)
    picked = mm((row_t == col_t).astype(BF16), picked_t, NT)
    rank = jnp.where(picked > 0, mm((row_t > col_t).astype(BF16), picked_t, NT), -64.0)
    rank_pad = jnp.concatenate([rank, jnp.full((104, 128), -64.0, F32)], axis=0).astype(BF16)
    pi, pj = iota((32, 128), 0), iota((32, 128), 1)
    place_rows = (pj == lax.rem(pi, 4) * 8 + pi // 4).astype(BF16)
    rk_out[...] = mm(place_rows, rank_pad, NT).reshape(8, 4, 1, 128)
    pk_out[...] = packed

    pl.semaphore_wait(barrier, NE - 1 + ND - 1)

    def z_send(k):
        to = lax.rem(z + k, 8)
        dev = (me_d, y * 8 + to)
        remote(rk_out.at[to], rk_in.at[z], rk_s, rk_r, dev).start()
        remote(pk_out, pk_in.at[z], pk_s, pk_r, dev).start()

    pltpu.make_async_copy(rk_out.at[z], rk_in.at[z], rk_r).start()
    pltpu.make_async_copy(pk_out, pk_in.at[z], pk_r).start()
    others(8, z_send)

    def z_copy(own, buf, ss, rs, k, sign):
        at = lambda n: (8 + sign * n) % 8
        return remote(
            own if k == 1 else buf.at[at(k - 1)], buf.at[at(k)], ss.at[at(k)], rs.at[at(k)],
            z_down if sign > 0 else z_up,
        )

    t_dn = [z_copy(tokens, zt, zs_t, zr_t, k, -1) for k in (1, 2, 3, 4)]
    t_up = [z_copy(tokens, zt, zs_t, zr_t, k, 1) for k in (1, 2, 3)]
    g_dn, g_up = [], []
    for h in range(2):
        own = grads.at[:, pl.ds(1024 * h, 1024)]
        g_dn.append(
            [z_copy(own, zg.at[h], zs_g.at[h], zr_g.at[h], k, -1) for k in (1, 2, 3)]
        )
        g_up.append(
            [z_copy(own, zg.at[h], zs_g.at[h], zr_g.at[h], k, 1) for k in (1, 2, 3, 4)]
        )
    for pipe in (t_dn, t_up, g_dn[0], g_up[0], g_dn[1], g_up[1]):
        pipe[0].start()

    def hot(ref, at, yy):
        row = ref[at, yy]
        return (jnp.broadcast_to(row, (8, 128)) == sub8.astype(F32)).astype(F32)

    def choose(at, half):
        none = jnp.zeros((8, 128), F32)
        parts = []
        for yy in range(4):
            one = hot(rk_in, at, yy)
            parts += [one, none] if half == 0 else [none, one]
        return jnp.concatenate(parts, axis=0).astype(BF16)[:, :TOK]

    y_copies = []

    def y_send(src, dst, ss, rs, j):
        for m in range(1, 4):
            to = lax.rem(y + m, 4)
            c = remote(src(to), dst, ss.at[j, m], rs.at[j, m], (me_d, to * 8 + z))
            c.start()
            y_copies.append(c)
        pltpu.make_async_copy(src(y), dst, rs.at[j, 0]).start()

    def y_pair(j, buf, send_buf, dst, ss, rs):
        out = mm(choose(lax.rem(z + 8 - j, 8), 0), buf[8 - j])
        out = out + mm(choose(lax.rem(z + j, 8), 1), buf[j])
        send_buf[j] = out.astype(BF16).reshape(4, 16, out.shape[1])
        y_send(lambda to: send_buf.at[j, to], dst, ss, rs, j)

    def y_single(n, block, ref, at, send_buf, dst, ss, rs):
        pick = jnp.concatenate([hot(ref, at, yy) for yy in range(4)], axis=0)
        out = mm(pick.astype(BF16)[:, :TOK], block)
        w = out.shape[1] // 2
        for yy in range(4):
            rows = out[8 * yy : 8 * yy + 8]
            send_buf[n, yy] = jnp.concatenate([rows[:, :w], rows[:, w:]], axis=0).astype(BF16)
        y_send(lambda to: send_buf.at[n, to], dst, ss, rs, n)

    def y_wait(view, rs, one_buf, one_rs, fill):
        for m in range(4):
            for j in range(1, 4):
                drain(view, rs.at[j, m])
            for n in range(2):
                drain(one_buf.at[0, 0], one_rs.at[n, m])
        for yy in range(4):
            parts = []
            for n in range(2):
                a = one_buf[yy, n].astype(F32)
                parts.append(jnp.concatenate([a[0:8], a[8:16]], axis=1))
            fill(yy, jnp.concatenate(parts, axis=0).astype(BF16))

    def arrive(down, up, k):
        if k < len(down):
            down[k].wait_recv()
            if k + 1 < len(down):
                down[k + 1].start()
        if k < len(up):
            up[k].wait_recv()
            if k + 1 < len(up):
                up[k + 1].start()

    def cut(h):
        return pl.ds(1024 * h, 1024)

    def t_pair(j):
        y_pair(j, zt, yt, rt.at[y, j], ys_t, yr_t)

    def t_single(n, block, ref, at):
        y_single(n, block, ref, at, et, qt.at[y, n], es_t, er_t)

    def g_pair(h, j):
        y_pair(j, zg.at[h], yg.at[h], rg.at[y, j, :, cut(h)], ys_g.at[h], yr_g.at[h])

    def g_single(h, n, block, ref, at):
        y_single(n, block, ref, at, eg.at[h], qg.at[h, y, n], es_g.at[h], er_g.at[h])

    t_single(0, tokens[...], rk_out, z)
    g_single(0, 0, grads[:, 0:1024], rk_out, z)
    g_single(1, 0, grads[:, 1024:2048], rk_out, z)

    drain(rk_in, rk_r)
    drain(pk_in, pk_r)
    own_rows = lall.at[core, x, pl.ds(pl.multiple_of(y * 8, 8), 8)]
    pltpu.make_async_copy(pk_in, own_rows, lg_r).start()
    pltpu.make_async_copy(rk_in.at[:, y], rk_col.at[y], rc_r).start()
    lg_copies = []
    for m in range(1, 4):
        to = lax.rem(y + m, 4)
        dev = (me_d, to * 8 + z)
        lg_copies.append(remote(pk_in, own_rows, lg_s.at[m - 1], lg_r, dev))
        lg_copies.append(remote(rk_in.at[:, to], rk_col.at[y], rc_s.at[m - 1], rc_r, dev))
    for c in lg_copies:
        c.start()

    far = lax.rem(z + 4, 8)
    arrive(t_dn, t_up, 0)
    t_pair(1)
    arrive(g_dn[0], g_up[0], 0)
    g_pair(0, 1)
    arrive(g_dn[1], g_up[1], 0)
    drain(lall.at[core, x], lg_r)
    others(
        NX,
        lambda k: remote(
            lall.at[core, x], lall.at[core, x], x_s, x_r, (lax.rem(x + k, NX) * 2 + core, me_e)
        ).start(),
    )
    arrive(t_dn, t_up, 1)
    t_pair(2)
    arrive(g_dn[0], g_up[0], 1)
    g_pair(0, 2)
    arrive(g_dn[1], g_up[1], 1)
    arrive(t_dn, t_up, 2)
    t_pair(3)
    arrive(g_dn[0], g_up[0], 2)
    g_pair(0, 3)
    arrive(g_dn[1], g_up[1], 2)
    arrive(t_dn, t_up, 3)
    t_single(1, zt[4], rk_in, far)
    drain(lall.at[core, pl.ds(0, NX - 1)], x_r)
    logit_pair = remote(lall.at[core], lall.at[core], p_s, p_r, partner)
    logit_pair.start()
    arrive(g_dn[0], g_up[0], 3)
    g_single(0, 1, zg[0, 4], rk_in, far)
    g_pair(1, 1)
    g_pair(1, 2)
    g_pair(1, 3)
    arrive(g_dn[1], g_up[1], 3)
    g_single(1, 1, zg[1, 4], rk_in, far)
    drain(lall.at[1 - core], p_r)

    valid = iota((1024, 128), 1) < 96
    li, lj = iota((128, 128), 0), iota((128, 128), 1)
    fold = (lax.rem(li, 32) == lax.rem(lj, 32)).astype(F32)
    block = (li // 32 == lj // 32).astype(F32)
    block_h = block.astype(BF16)

    def rows_of(a):
        return jnp.sum(jnp.sum(a.reshape(8, 16, 8, 128), axis=1), axis=0)

    def total(acc):
        one = jnp.broadcast_to(jnp.sum(acc, axis=0, keepdims=True), (8, 128))
        return mm(one, fold, exact=True)

    acc = jnp.zeros((8, 128), F32)
    for i in range(2):
        d0 = jnp.where(valid, jnp.exp(lall[i].reshape(1024, 128)), 0.0)
        dd[i] = d0
        acc = acc + rows_of(d0)
    pad = jnp.where(iota((1, 128), 1) < 96, 0.0, 1.0)
    c = total(acc)
    cols[0:8, :] = c
    for p in range(2):
        acc = jnp.zeros((8, 128), F32)
        inverse = 1.0 / c[0:1, :]
        for i in range(2):
            q = dd[i] * inverse
            q_hi = q.astype(BF16)
            q_lo = (q - q_hi.astype(F32)).astype(BF16)
            d = q / (mm(q_hi, block_h) + mm(q_lo, block_h) + pad)
            dd[i] = d
            db[p, i] = d.astype(BF16)
            acc = acc + rows_of(d)
        c = total(acc)
        cols[8 * p + 8 : 8 * p + 16, :] = c

    c3 = jnp.concatenate([cols[0:1, :], cols[8:9, :], cols[16:17, :]], axis=0)
    dens, quot = own_state(logits, c3)
    gates = NE * dens[3]

    lane256, row256 = iota((256, 128), 1), iota((256, 128), 0)
    q = dd[core, pl.ds(pl.multiple_of(x * 256, 256), 256), :] / c3[2:3, :]
    q_hi = q.astype(BF16)
    q_lo = (q - q_hi.astype(F32)).astype(BF16)
    group = NE * q / (mm(q_hi, block_h) + mm(q_lo, block_h) + pad)
    turned = jnp.zeros((256, 128), F32)
    for n in range(3):
        one = jnp.sum(jnp.where(lane256 == 32 * n + me_e, group, 0.0), axis=1, keepdims=True)
        turned = turned + jnp.where(lane256 == 8 * n + lax.rem(row256, 8), one, 0.0)
    gcol[...] = jnp.sum(turned.reshape(NE, 8, 128), axis=1).reshape(NE, 1, 128)
    drain(rk_col, rc_r)
    tiles = []
    for yy in range(4):
        for off in (0, 4, 7, 1, 6, 2, 5, 3):
            zz = lax.rem(z + off, 8)
            here = jnp.broadcast_to(rk_col[yy, zz], (8, 128)) == sub8.astype(F32)
            tiles.append(jnp.where(here, jnp.broadcast_to(gcol[yy * 8 + zz], (8, 128)), 0.0))
    gate = jnp.sum(jnp.concatenate(tiles, axis=0), axis=1, keepdims=True)
    gate = gate.astype(BF16).astype(F32)

    def plane(src, dst, send, recv):
        pltpu.make_async_copy(src(me_e), dst, recv).start()

        def go(k):
            to = lax.rem(me_e + k, NE)
            remote(src(to), dst, send, recv, (me_d, to)).start()

        others(NE, go)

    for c in loads:
        c.wait()

    def fill_t(yy, value):
        rt[yy, 0] = value

    y_wait(rt.at[0, 0], yr_t, qt, er_t, fill_t)
    cuts = []
    for o in range(4):
        at = pl.ds(pl.multiple_of(512 * o + 256 * (1 - core), 256), 256)
        cuts.append(
            remote(rt.at[:, :, :, at], pt.at[o], q_s.at[o], q_r.at[o], partner)
        )
        cuts[-1].start()

    def forward(i, carry):
        at = pl.ds(pl.multiple_of(i * 256, 256), 256)
        rows = rt[...].reshape(256, D)
        gate_pre = mm(rows, wg[:, at])
        up_pre = mm(rows, wu[:, at])
        sg = jax.nn.sigmoid(gate_pre)
        a = gate_pre * sg
        h = a * up_pre
        hid[:, at] = h
        act[:, at] = a
        dsl[:, at] = up_pre * sg * (1.0 + gate_pre * (1.0 - sg))
        ht[at, :] = h.T.astype(BF16)
        return carry

    lax.fori_loop(0, 3, forward, 0)
    ht_copy = remote(ht, pht, q_s.at[4], q_r.at[4], partner)
    ht_copy.start()

    def where_from(k):
        o = lax.rem(k, 8)
        j, h = o // 2, lax.rem(o, 2)
        yy = lax.rem(y + k // 8, 4)
        zz = lax.rem(z + h * (j + 4 * ((4 - j) // 4)) + (1 - h) * (8 - j), 8)
        return yy * 8 + o, yy * 8 + zz

    def fill_g(h):
        def f(yy, value):
            rg[yy, 0, :, 1024 * h : 1024 * h + 1024] = value
        return f

    ds_copies = []

    def scaled(h):
        y_wait(rg.at[0, 0, :, cut(h)], yr_g.at[h], qg.at[h], er_g.at[h], fill_g(h))
        for b in range(2 * h, 2 * h + 2):
            at = slice(512 * b, 512 * b + 512)
            ds[:, at] = (gate * rg[:, :, :, at].reshape(256, 512).astype(F32)).astype(BF16)
        c = remote(ds.at[:, cut(h)], pds.at[:, cut(h)], q_s.at[5 + h], q_r.at[5 + h], partner)
        c.start()
        ds_copies.append(c)

    def my_rows(ref, j):
        o = lax.rem(x + j, NX)
        return ref[pl.ds(pl.multiple_of(192 * o + 96 * core, 32), 96), :]

    half, early = [], []

    def down_half(h):
        ds_copies[h].wait_recv()

        def one(i, carry):
            at = pl.ds(pl.multiple_of(1024 * h + i * 512, 512), 512)
            to = pl.ds(pl.multiple_of(i * 512, 512), 512)
            mine = jnp.concatenate([my_rows(ht, j) for j in range(4)], axis=0)
            theirs = jnp.concatenate([my_rows(pht, j) for j in range(4)], axis=0)
            out = mm(mine, ds[:, at]) + mm(theirs, pds[:, at])
            for j in range(4):
                g2[h, j, :, to] = out[96 * j : 96 * j + 96].astype(BF16)
            return carry

        lax.fori_loop(0, 2, one, 0)
        top, low = pl.ds(0, 48), pl.ds(48, 48)
        n = 2 * h
        half.append(remote(g2.at[h, 2, top], ra2.at[h], h_s.at[n], h_r.at[n], right))
        half.append(remote(g2.at[h, 2, low], rb2.at[h], h_s.at[n + 1], h_r.at[n + 1], left))
        early.append(
            remote(g2.at[h, 1, low], rc2.at[h, low], n_s.at[n], n_r.at[n], right)
        )
        early.append(
            remote(g2.at[h, 3, top], rd2.at[h, top], n_s.at[n + 1], n_r.at[n + 1], left)
        )
        half[-2].start()
        half[-1].start()

    scaled(0)
    ht_copy.wait_recv()
    down_half(0)
    early[0].start()
    early[1].start()
    scaled(1)

    def backward(i, total_score):
        at = pl.ds(pl.multiple_of(i * 256, 256), 256)
        at_up = pl.ds(pl.multiple_of(i * 256 + FF, 256), 256)
        h = mm(rg[...].reshape(256, D), wd[at, :], NT)
        a = (h * dsl[:, at]).astype(BF16)
        b = (h * act[:, at]).astype(BF16)
        gg[:, at] = a
        ug[:, at] = b
        pair[:, at] = (gate * a.astype(F32)).astype(BF16)
        pair[:, at_up] = (gate * b.astype(F32)).astype(BF16)
        return total_score + jnp.sum(h * hid[:, at], axis=1, keepdims=True)

    score = lax.fori_loop(0, 3, backward, jnp.zeros((256, 1), F32))
    pair_copy = remote(pair, ppair, q_s.at[7], q_r.at[7], partner)
    pair_copy.start()
    spread8 = jnp.broadcast_to(score.astype(BF16).astype(F32), (256, 128)).reshape(NE, 8, 128)
    diag = iota((NE, 8, 128), 1) == iota((NE, 8, 128), 2)
    stile[...] = jnp.sum(jnp.where(diag, spread8, 0.0), axis=1).reshape(NE, 1, 128)
    pltpu.make_async_copy(stile.at[where_from(0)[0]], sbuf.at[me_e], sc_r).start()

    def send_score(k):
        n, to = where_from(k)
        remote(stile.at[n], sbuf.at[me_e], sc_s, sc_r, (me_d, to)).start()

    others(NE, send_score)

    down_half(1)
    for n in range(2):
        at = pl.ds(64 * n, 64)
        half += [
            remote(g1.at[2, at], ra1.at[at], h_s.at[2 * n + 4], h_r.at[2 * n + 4], right),
            remote(
                g1.at[2, pl.ds(128 + 64 * n, 64)], rb1.at[at],
                h_s.at[2 * n + 5], h_r.at[2 * n + 5], left,
            ),
        ]
    for c in cuts:
        c.wait_recv()
    pair_copy.wait_recv()

    def pair_part(j):
        o = lax.rem(x + j, NX)
        col = pl.ds(pl.multiple_of(512 * o + 256 * core, 256), 256)

        def one(i, carry):
            at = pl.ds(pl.multiple_of(i * 512, 512), 512)
            out = mm(rt[:, :, :, col].reshape(256, 256), pair[:, at], TN)
            out = out + mm(pt[o].reshape(256, 256), ppair[:, at], TN)
            g1[j, :, at] = out.astype(BF16)
            return carry

        lax.fori_loop(0, 3, one, 0)

    pair_part(2)
    for c in half[4:8]:
        c.start()
    for b in range(4):
        at = slice(512 * b, 512 * b + 512)
        out = mm(gg[...], wg[at, :], NT) + mm(ug[...], wu[at, :], NT)
        rows = 8 * (b // 2)
        cut = slice(512 * (b % 2), 512 * (b % 2) + 512)
        bsend[:, rows : rows + 8, cut] = out.reshape(NE, 8, 512).astype(BF16)

    def send_back(k):
        n, to = where_from(k)
        remote(bsend.at[n], ret.at[me_e], ret_s, ret_r, (me_d, to)).start()

    pltpu.make_async_copy(bsend.at[where_from(0)[0]], ret.at[me_e], ret_r).start()
    lax.fori_loop(1, 5, lambda k, c: (send_back(k), c)[1], 0)
    pair_part(1)
    pair_part(3)
    pair_part(0)

    drain(sbuf, sc_r)
    eye32 = (iota((NE, 128), 0) == iota((NE, 128), 1)).astype(BF16)
    scores = mm(sbuf[...].reshape(NE, 128).astype(BF16), eye32, TN)
    grad3 = jnp.zeros((TOK, 128), F32)
    for slot in range(CAP):
        grad3 = grad3 + jnp.where(
            rank == slot, jnp.broadcast_to(scores[slot : slot + 1, :], (TOK, 128)), 0.0
        )
    g = NE * grad3 * dens[3]
    h3 = g - dens[3] * jnp.sum(g, axis=1, keepdims=True)
    atile[...] = jnp.sum(h3, axis=0, keepdims=True)
    plane(lambda e: atile, abuf.at[me_e], a_s, a_r)
    lax.fori_loop(5, 16, lambda k, c: (send_back(k), c)[1], 0)

    gates_hi = gates.astype(BF16).astype(F32)
    ex_i, ex_j = iota((128, 512), 0), iota((128, 512), 1)
    spread = ((ex_i < NE) & (ex_j // 16 == ex_i)).astype(BF16)
    wide = mm(
        jnp.concatenate([rank, gates_hi, gates - gates_hi], axis=0).astype(BF16), spread
    )
    k16 = lax.rem(iota((TOK, 512), 1), 16)
    rank_w = wide[0:TOK].astype(jnp.int32)
    parts = []
    for m in (rank_w == k16, rank_w == k16 - 8):
        parts += [jnp.where(m, wide[TOK : 2 * TOK], 0.0), jnp.where(m, wide[2 * TOK :], 0.0)]
    weights = jnp.concatenate(parts, axis=0).astype(BF16)

    for p in range(2):
        dens_h = db[p].reshape(2048, 128)
        g = mm(dens_h, dens_h, TN)
        gram[p] = mm(mm(fold, g * block, exact=True), fold, exact=True)

    drain(abuf, a_r)
    btile[...] = jnp.sum(abuf[...], axis=0)
    pltpu.make_async_copy(btile, bbuf.at[me_d], b_r).start()
    others(
        ND,
        lambda k: remote(
            btile, bbuf.at[me_d], b_s, b_r, (lax.rem(me_d + k, ND), me_e)
        ).start(),
    )
    for n in range(2):
        up, down = pl.ds(128 + 64 * n, 64), pl.ds(64 * n, 64)
        early += [
            remote(g1.at[1, up], rc1.at[up], n_s.at[2 * n + 4], n_r.at[2 * n + 4], right),
            remote(g1.at[3, down], rd1.at[down], n_s.at[2 * n + 5], n_r.at[2 * n + 5], left),
        ]
    for c in early[2:6]:
        c.start()

    drain(bbuf, b_r)
    v = jnp.broadcast_to(jnp.sum(bbuf[...], axis=0), (8, 128))
    first32 = lane8 < NE
    u = mm(jnp.where(first32, v / cols[16:24, :], 0.0), gram[1], exact=True)
    s = mm(jnp.where(first32, u / cols[8:16, :], 0.0), gram[0], exact=True)
    qv = quot[2] * v[0:1, :]
    h2 = h3 - qv + dens[2] * jnp.sum(qv, axis=1, keepdims=True)
    qu = quot[1] * u[0:1, :]
    h1 = h2 - qu + dens[1] * jnp.sum(qu, axis=1, keepdims=True)
    lgrad = (h1 - quot[0] * s[0:1, :]).astype(BF16)[:, :NE]
    router_t = mm(lgrad, tokens[...], TN)
    for p in range(NE):
        h, b = p % 2, p // 2
        rsend[p] = router_t[16 * h : 16 * h + 16, 128 * b : 128 * b + 128].astype(BF16)
    plane(lambda e: rsend.at[e], rrecv.at[me_e], rs_s, rs_r)
    lax.fori_loop(16, NE, lambda k, c: (send_back(k), c)[1], 0)
    router_in = mm(lgrad, rw[...])

    def add_rows(n, rows, terms, out):
        def one(i, c):
            at = pl.ds(pl.multiple_of(i * rows, rows), rows)
            out(at, functools.reduce(lambda a, b: a + b, [t(at).astype(F32) for t in terms]))
            return c

        lax.fori_loop(0, n // rows, one, 0)

    def put(ref, j, base):
        def f(at, value):
            ref[j, pl.ds(pl.multiple_of(at.start + base, 16), at.size), :] = value.astype(BF16)
        return f

    def take(ref, j, base):
        return lambda at: ref[j, pl.ds(pl.multiple_of(at.start + base, 16), at.size), :]

    for c in half:
        c.wait_recv()
    for h in range(2):
        add_rows(
            48, 48, [take(g2.at[h], 1, 0), lambda at, h=h: ra2[h, at, :]], put(g2.at[h], 1, 0)
        )
        add_rows(
            48, 48, [take(g2.at[h], 3, 48), lambda at, h=h: rb2[h, at, :]], put(g2.at[h], 3, 48)
        )
    add_rows(128, 32, [take(g1, 1, 0), lambda at: ra1[at, :]], put(g1, 1, 0))
    add_rows(128, 32, [take(g1, 3, 128), lambda at: rb1[at, :]], put(g1, 3, 128))
    late = []
    for h in range(2):
        top, low = pl.ds(0, 48), pl.ds(48, 48)
        late += [
            remote(g2.at[h, 1, top], rc2.at[h, top], m_s.at[2 * h], m_r.at[2 * h], right),
            remote(
                g2.at[h, 3, low], rd2.at[h, low], m_s.at[2 * h + 1], m_r.at[2 * h + 1], left
            ),
        ]
    late += [
        remote(g1.at[1, pl.ds(0, 128)], rc1.at[pl.ds(0, 128)], m_s.at[4], m_r.at[4], right),
        remote(g1.at[3, pl.ds(128, 128)], rd1.at[pl.ds(128, 128)], m_s.at[5], m_r.at[5], left),
    ]

    drain(rrecv, rs_r)
    dsum[...] = jnp.sum(rrecv[...].astype(F32), axis=0).astype(BF16)
    pltpu.make_async_copy(dsum, drecv.at[me_d], d_r).start()
    others(
        ND,
        lambda k: remote(
            dsum, drecv.at[me_d], d_s, d_r, (lax.rem(me_d + k, ND), me_e)
        ).start(),
    )
    early[6].start()
    early[7].start()
    for c in late:
        c.start()
    drain(drecv, d_r)
    fin[...] = jnp.sum(drecv[...].astype(F32), axis=0).astype(BF16)
    plane(lambda e: fin, router_out.at[me_e], o_s, o_r)

    drain(ret, ret_r)
    mixed = mm(weights, ret[...].reshape(512, 1024))
    gt_out[:, 0:1024] = (mixed[0:24] + mixed[24:48] + router_in[:, 0:1024]).astype(BF16)
    gt_out[:, 1024:2048] = (mixed[48:72] + mixed[72:96] + router_in[:, 1024:2048]).astype(BF16)

    for c in early + late:
        c.wait_recv()

    def store(ref):
        def f(at, value):
            ref[at, :] = value.astype(BF16)
        return f

    def store_half(h):
        def f(at, value):
            down_out[at, 1024 * h : 1024 * h + 1024] = value.astype(BF16)
        return f

    for h in range(2):
        add_rows(
            96, 48,
            [
                take(g2.at[h], 0, 0),
                lambda at, h=h: rc2[h, at, :],
                lambda at, h=h: rd2[h, at, :],
            ],
            store_half(h),
        )
    add_rows(
        256, 32, [take(g1, 0, 0), lambda at: rc1[at, :], lambda at: rd1[at, :]], store(pair_out)
    )
    drain(router_out, o_r)

    for c in t_dn + t_up + g_dn[0] + g_dn[1] + g_up[0] + g_up[1] + ds_copies + y_copies + lg_copies + cuts + half + early + late:
        c.wait_send()
    for c in (logit_pair, ht_copy, pair_copy):
        c.wait_send()
    drain(rk_in.at[pl.ds(0, 7)], rk_s)
    drain(pk_in.at[pl.ds(0, 7)], pk_s)
    drain(lall.at[0, pl.ds(0, NX - 1)], x_s)
    drain(ret.at[pl.ds(0, NE - 1)], ret_s)
    drain(sbuf.at[pl.ds(0, NE - 1)], sc_s)
    drain(abuf.at[pl.ds(0, NE - 1)], a_s)
    drain(bbuf.at[pl.ds(0, ND - 1)], b_s)
    drain(rrecv.at[pl.ds(0, NE - 1)], rs_s)
    drain(drecv.at[pl.ds(0, ND - 1)], d_s)
    drain(router_out.at[pl.ds(0, NE - 1)], o_s)


def moe(*args):
    dma = pltpu.SemaphoreType.DMA
    V = pltpu.VMEM
    hbm = pl.BlockSpec(memory_space=pltpu.HBM)
    return pl.pallas_call(
        moe_kernel,
        name="moe",
        out_shape=(
            jax.ShapeDtypeStruct((TOK, D), BF16),
            jax.ShapeDtypeStruct((256, 2 * FF), BF16),
            jax.ShapeDtypeStruct((96, D), BF16),
            jax.ShapeDtypeStruct((NE, 16, 128), BF16),
        ),
        in_specs=[VM] * 4 + [hbm] * 3,
        out_specs=(VM,) * 4,
        scratch_shapes=[
            V((D, FF), BF16), V((D, FF), BF16), V((FF, D), BF16),
            V((8, 4, 1, 128), F32), V((8, 4, 1, 128), F32), V((4, 8, 1, 128), F32),
            V((8, 128), F32), V((8, 8, 128), F32),
            V((2, 4, 16, 1024), BF16), V((2, 2, 4, 16, 512), BF16),
            V((4, 2, 16, 1024), BF16), V((2, 4, 2, 16, 512), BF16),
            V((2, NX, NE, 8, 128), F32), V((2, 1024, 128), F32), V((2, 2, 1024, 128), BF16),
            V((24, 128), F32), V((2, 128, 128), F32), V((NE, 1, 128), F32),
            V((8, TOK, D), BF16), V((2, 8, TOK, 1024), BF16),
            V((4, 4, 16, D), BF16), V((2, 4, 4, 16, 1024), BF16),
            V((4, 4, 16, D), BF16), V((4, 4, 16, D), BF16),
            V((4, 4, 4, 16, 256), BF16),
            V((256, FF), F32), V((256, FF), F32), V((256, FF), F32),
            V((FF, 256), BF16), V((FF, 256), BF16),
            V((256, D), BF16), V((256, D), BF16),
            V((256, FF), BF16), V((256, FF), BF16),
            V((256, 2 * FF), BF16), V((256, 2 * FF), BF16),
            V((4, 256, 2 * FF), BF16), V((2, 4, 96, 1024), BF16),
            V((128, 2 * FF), BF16), V((2, 48, 1024), BF16),
            V((128, 2 * FF), BF16), V((2, 48, 1024), BF16),
            V((256, 2 * FF), BF16), V((2, 96, 1024), BF16),
            V((256, 2 * FF), BF16), V((2, 96, 1024), BF16),
            V((NE, 16, 1024), BF16), V((NE, 16, 1024), BF16),
            V((NE, 1, 128), F32), V((NE, 1, 128), F32),
            V((1, 128), F32), V((NE, 1, 128), F32),
            V((1, 128), F32), V((ND, 1, 128), F32),
            V((NE, 16, 128), BF16), V((NE, 16, 128), BF16),
            V((16, 128), BF16), V((ND, 16, 128), BF16), V((16, 128), BF16),
            dma((3,)),
            dma((8,)), dma((8,)), dma((2, 8)), dma((2, 8)),
            dma((4, 4)), dma((4, 4)), dma((2, 4, 4)), dma((2, 4, 4)),
            dma((2, 4)), dma((2, 4)), dma((2, 2, 4)), dma((2, 2, 4)),
            dma((8,)), dma((8,)),
            dma((8,)), dma((8,)), dma((8,)), dma((8,)), dma((6,)), dma((6,)),
            dma((3,)), dma, dma((3,)), dma,
        ]
        + [dma] * 22,
        compiler_params=pltpu.CompilerParams(
            collective_id=0, has_side_effects=True, vmem_limit_bytes=52 * 1024 * 1024
        ),
    )(*args)


def write_kernel(gt, pair, down, router, gt_o, router_o, gate_o, up_o, down_o):
    gt_o[...] = gt[...]
    gate_o[0] = pair[:, 0:FF]
    up_o[0] = pair[:, FF : 2 * FF]
    down_o[0] = down[...]
    for p in range(NE):
        h, b = p % 2, p // 2
        router_o[16 * h : 16 * h + 16, 128 * b : 128 * b + 128] = router[p].astype(F32)


def write(*args):
    return pl.pallas_call(
        write_kernel,
        name="write",
        out_shape=(
            jax.ShapeDtypeStruct((TOK, D), BF16),
            jax.ShapeDtypeStruct((NE, D), F32),
            jax.ShapeDtypeStruct((1, 256, FF), BF16),
            jax.ShapeDtypeStruct((1, 256, FF), BF16),
            jax.ShapeDtypeStruct((1, 96, D), BF16),
        ),
        in_specs=[VM] * 4,
        out_specs=(VM,) * 5,
        compiler_params=pltpu.CompilerParams(vmem_limit_bytes=16 * 1024 * 1024),
    )(*args)


def per_device(tokens, out_grad, expert_ids, router_weight, w_gate, w_up, w_down):
    gt, pair, down, router = moe(
        tokens, out_grad, expert_ids.T, router_weight.T, w_gate, w_up, w_down
    )
    gt, router, gate, up, down = write(gt, pair, down, router)
    return gt, router.T, gate, up, down


def solution(mesh):
    in_specs = (
        P(("dp", "expert"), None), P(("dp", "expert"), None), P(("dp", "expert"), None), P(),
        P("expert", None, None), P("expert", None, None), P("expert", None, None),
    )
    out_specs = (
        P(("dp", "expert"), None), P(),
        P("expert", "dp", None), P("expert", "dp", None), P("expert", "dp", None),
    )
    return jax.shard_map(
        per_device, mesh=mesh, in_specs=in_specs, out_specs=out_specs, check_vma=False
    )
```

```python
import functools

import jax
import jax.numpy as jnp
from jax import lax
from jax.experimental import pallas as pl
from jax.experimental.pallas import tpu as pltpu
from jax.sharding import PartitionSpec as P

HI = lax.Precision.HIGHEST
F32 = jnp.float32
BF16 = jnp.bfloat16
NE = 32
ND = 8
NX = 4
TOK = 24
CAP = 8
D = 2048
FF = 768
VM = pl.BlockSpec(memory_space=pltpu.VMEM)
MESH = pl.DeviceIdType.MESH


def iota(shape, dim):
    return lax.broadcasted_iota(jnp.int32, shape, dim)


def remote(src, dst, send, recv, dev):
    return pltpu.make_async_remote_copy(
        src_ref=src, dst_ref=dst, send_sem=send, recv_sem=recv, device_id=dev, device_id_type=MESH
    )


def drain(ref, sem):
    pltpu.make_async_copy(ref, ref, sem).wait()


def place():
    me_d = lax.axis_index("dp")
    return me_d, lax.axis_index("expert"), me_d // 2, lax.rem(me_d, 2)


def others(n, body):
    lax.fori_loop(1, n, lambda k, c: (body(k), c)[1], 0)


def own_state(logits, cols):
    lane = iota((TOK, 128), 1)
    d = jnp.where(lane < NE, jnp.exp(logits), 0.0)
    ds, qs = [d], []
    for p in range(3):
        q = d / cols[p : p + 1, :]
        d = q / jnp.sum(q, axis=1, keepdims=True)
        qs.append(q)
        ds.append(d)
    return ds, qs


NT = (((1,), (1,)), ((), ()))
TN = (((0,), (0,)), ((), ()))


def mm(a, b, dims=None, exact=False):
    dims = dims or (((1,), (0,)), ((), ()))
    return lax.dot_general(
        a, b, dims, precision=HI if exact else None, preferred_element_type=F32
    )


def moe_kernel(
    tokens_hbm, grads_hbm, ids_hbm, rw_hbm, wg_hbm, wu_hbm, wd_hbm,
    gt_out, pair_out, down_out, router_out,
    tokens, grads, ids, rw, wg, wu, wd, rk_out, rk_in, rk_col, pk_out, pk_in, et, eg, qt, qg,
    lall, dd, db, cols, gram, gcol,
    zt, zg, yt, yg, rt, rg, pt, hid, act, dsl, ht, pht, ds, pds, gg, ug, pair, ppair,
    g1, g2, ra1, ra2, rb1, rb2, rc1, rc2, rd1, rd2,
    bsend, ret, stile, sbuf, atile, abuf, btile, bbuf, rsend, rrecv, dsum, drecv, fin,
    in_sem, w_sem, zs_t, zr_t, zs_g, zr_g, ys_t, yr_t, ys_g, yr_g, es_t, er_t, es_g, er_g, q_s, q_r, h_s, h_r, n_s, n_r, m_s, m_r,
    ht_s, ht_r, lg_s, lg_r, rc_s, rc_r, rk_s, rk_r, pk_s, pk_r, x_s, x_r, p_s, p_r, ret_s, ret_r, sc_s, sc_r,
    a_s, a_r, b_s, b_r, rs_s, rs_r, d_s, d_r, o_s, o_r,
):
    me_d, me_e, x, core = place()
    y, z = me_e // 8, lax.rem(me_e, 8)
    inputs = [
        pltpu.make_async_copy(a, b, in_sem.at[n])
        for n, (a, b) in enumerate(
            ((tokens_hbm, tokens), (grads_hbm, grads), (ids_hbm, ids), (rw_hbm, rw))
        )
    ]
    for c in inputs:
        c.start()
    barrier = pltpu.get_barrier_semaphore()
    others(
        NE,
        lambda k: pl.semaphore_signal(
            barrier, inc=1, device_id=(me_d, lax.rem(me_e + k, NE)), device_id_type=MESH
        ),
    )
    others(
        ND,
        lambda k: pl.semaphore_signal(
            barrier, inc=1, device_id=(lax.rem(me_d + k, ND), me_e), device_id_type=MESH
        ),
    )
    loads = [
        pltpu.make_async_copy(a.at[0], b, w_sem.at[n])
        for n, (a, b) in enumerate(((wg_hbm, wg), (wu_hbm, wu), (wd_hbm, wd)))
    ]
    for c in loads:
        c.start()
    for c in inputs:
        c.wait()
    partner = (x * 2 + 1 - core, me_e)
    right = (lax.rem(x + 1, NX) * 2 + core, me_e)
    left = (lax.rem(x + 3, NX) * 2 + core, me_e)
    z_up = (me_d, y * 8 + lax.rem(z + 1, 8))
    z_down = (me_d, y * 8 + lax.rem(z + 7, 8))

    lane8, sub8 = iota((8, 128), 1), iota((8, 128), 0)
    logits = jnp.concatenate(
        [mm(tokens[...], rw[...], NT), jnp.zeros((TOK, 96), F32)], axis=1
    )
    packed = (
        logits[0:8] + pltpu.roll(logits[8:16], 32, 1) + pltpu.roll(logits[16:24], 64, 1)
    )
    picked_t = jnp.zeros((128, TOK), F32)
    for k in range(8):
        picked_t = picked_t + (ids[k : k + 1, :] == iota((128, TOK), 0)).astype(F32)
    picked_t = picked_t.astype(BF16)
    row_t, col_t = iota((TOK, TOK), 0), iota((TOK, TOK), 1)
    picked = mm((row_t == col_t).astype(BF16), picked_t, NT)
    rank = jnp.where(picked > 0, mm((row_t > col_t).astype(BF16), picked_t, NT), -64.0)
    rank_pad = jnp.concatenate([rank, jnp.full((104, 128), -64.0, F32)], axis=0).astype(BF16)
    pi, pj = iota((32, 128), 0), iota((32, 128), 1)
    place_rows = (pj == lax.rem(pi, 4) * 8 + pi // 4).astype(BF16)
    rk_out[...] = mm(place_rows, rank_pad, NT).reshape(8, 4, 1, 128)
    pk_out[...] = packed

    pl.semaphore_wait(barrier, NE - 1 + ND - 1)

    def z_send(k):
        to = lax.rem(z + k, 8)
        dev = (me_d, y * 8 + to)
        remote(rk_out.at[to], rk_in.at[z], rk_s, rk_r, dev).start()
        remote(pk_out, pk_in.at[z], pk_s, pk_r, dev).start()

    pltpu.make_async_copy(rk_out.at[z], rk_in.at[z], rk_r).start()
    pltpu.make_async_copy(pk_out, pk_in.at[z], pk_r).start()
    others(8, z_send)

    def z_copy(own, buf, ss, rs, k, sign):
        at = lambda n: (8 + sign * n) % 8
        return remote(
            own if k == 1 else buf.at[at(k - 1)], buf.at[at(k)], ss.at[at(k)], rs.at[at(k)],
            z_down if sign > 0 else z_up,
        )

    t_dn = [z_copy(tokens, zt, zs_t, zr_t, k, -1) for k in (1, 2, 3, 4)]
    t_up = [z_copy(tokens, zt, zs_t, zr_t, k, 1) for k in (1, 2, 3)]
    g_dn, g_up = [], []
    for h in range(2):
        own = grads.at[:, pl.ds(1024 * h, 1024)]
        g_dn.append(
            [z_copy(own, zg.at[h], zs_g.at[h], zr_g.at[h], k, -1) for k in (1, 2, 3)]
        )
        g_up.append(
            [z_copy(own, zg.at[h], zs_g.at[h], zr_g.at[h], k, 1) for k in (1, 2, 3, 4)]
        )
    for pipe in (t_dn, t_up, g_dn[0], g_up[0], g_dn[1], g_up[1]):
        pipe[0].start()

    def hot(ref, at, yy):
        row = ref[at, yy]
        return (jnp.broadcast_to(row, (8, 128)) == sub8.astype(F32)).astype(F32)

    def choose(at, half):
        none = jnp.zeros((8, 128), F32)
        parts = []
        for yy in range(4):
            one = hot(rk_in, at, yy)
            parts += [one, none] if half == 0 else [none, one]
        return jnp.concatenate(parts, axis=0).astype(BF16)[:, :TOK]

    y_copies = []

    def y_send(src, dst, ss, rs, j):
        for m in range(1, 4):
            to = lax.rem(y + m, 4)
            c = remote(src(to), dst, ss.at[j, m], rs.at[j, m], (me_d, to * 8 + z))
            c.start()
            y_copies.append(c)
        pltpu.make_async_copy(src(y), dst, rs.at[j, 0]).start()

    def y_pair(j, buf, send_buf, dst, ss, rs):
        out = mm(choose(lax.rem(z + 8 - j, 8), 0), buf[8 - j])
        out = out + mm(choose(lax.rem(z + j, 8), 1), buf[j])
        send_buf[j] = out.astype(BF16).reshape(4, 16, out.shape[1])
        y_send(lambda to: send_buf.at[j, to], dst, ss, rs, j)

    def y_single(n, block, ref, at, send_buf, dst, ss, rs):
        pick = jnp.concatenate([hot(ref, at, yy) for yy in range(4)], axis=0)
        out = mm(pick.astype(BF16)[:, :TOK], block)
        w = out.shape[1] // 2
        for yy in range(4):
            rows = out[8 * yy : 8 * yy + 8]
            send_buf[n, yy] = jnp.concatenate([rows[:, :w], rows[:, w:]], axis=0).astype(BF16)
        y_send(lambda to: send_buf.at[n, to], dst, ss, rs, n)

    def y_wait(view, rs, one_buf, one_rs, fill):
        for m in range(4):
            for j in range(1, 4):
                drain(view, rs.at[j, m])
            for n in range(2):
                drain(one_buf.at[0, 0], one_rs.at[n, m])
        for yy in range(4):
            parts = []
            for n in range(2):
                a = one_buf[yy, n].astype(F32)
                parts.append(jnp.concatenate([a[0:8], a[8:16]], axis=1))
            fill(yy, jnp.concatenate(parts, axis=0).astype(BF16))

    def arrive(down, up, k):
        if k < len(down):
            down[k].wait_recv()
            if k + 1 < len(down):
                down[k + 1].start()
        if k < len(up):
            up[k].wait_recv()
            if k + 1 < len(up):
                up[k + 1].start()

    def cut(h):
        return pl.ds(1024 * h, 1024)

    def t_pair(j):
        y_pair(j, zt, yt, rt.at[y, j], ys_t, yr_t)

    def t_single(n, block, ref, at):
        y_single(n, block, ref, at, et, qt.at[y, n], es_t, er_t)

    def g_pair(h, j):
        y_pair(j, zg.at[h], yg.at[h], rg.at[y, j, :, cut(h)], ys_g.at[h], yr_g.at[h])

    def g_single(h, n, block, ref, at):
        y_single(n, block, ref, at, eg.at[h], qg.at[h, y, n], es_g.at[h], er_g.at[h])

    t_single(0, tokens[...], rk_out, z)
    g_single(0, 0, grads[:, 0:1024], rk_out, z)
    g_single(1, 0, grads[:, 1024:2048], rk_out, z)

    drain(rk_in, rk_r)
    drain(pk_in, pk_r)
    own_rows = lall.at[core, x, pl.ds(pl.multiple_of(y * 8, 8), 8)]
    pltpu.make_async_copy(pk_in, own_rows, lg_r).start()
    pltpu.make_async_copy(rk_in.at[:, y], rk_col.at[y], rc_r).start()
    lg_copies = []
    for m in range(1, 4):
        to = lax.rem(y + m, 4)
        dev = (me_d, to * 8 + z)
        lg_copies.append(remote(pk_in, own_rows, lg_s.at[m - 1], lg_r, dev))
        lg_copies.append(remote(rk_in.at[:, to], rk_col.at[y], rc_s.at[m - 1], rc_r, dev))
    for c in lg_copies:
        c.start()

    far = lax.rem(z + 4, 8)
    arrive(t_dn, t_up, 0)
    t_pair(1)
    arrive(g_dn[0], g_up[0], 0)
    g_pair(0, 1)
    arrive(g_dn[1], g_up[1], 0)
    drain(lall.at[core, x], lg_r)
    others(
        NX,
        lambda k: remote(
            lall.at[core, x], lall.at[core, x], x_s, x_r, (lax.rem(x + k, NX) * 2 + core, me_e)
        ).start(),
    )
    arrive(t_dn, t_up, 1)
    t_pair(2)
    arrive(g_dn[0], g_up[0], 1)
    g_pair(0, 2)
    arrive(g_dn[1], g_up[1], 1)
    arrive(t_dn, t_up, 2)
    t_pair(3)
    arrive(g_dn[0], g_up[0], 2)
    g_pair(0, 3)
    arrive(g_dn[1], g_up[1], 2)
    arrive(t_dn, t_up, 3)
    t_single(1, zt[4], rk_in, far)
    drain(lall.at[core, pl.ds(0, NX - 1)], x_r)
    logit_pair = remote(lall.at[core], lall.at[core], p_s, p_r, partner)
    logit_pair.start()
    arrive(g_dn[0], g_up[0], 3)
    g_single(0, 1, zg[0, 4], rk_in, far)
    g_pair(1, 1)
    g_pair(1, 2)
    g_pair(1, 3)
    arrive(g_dn[1], g_up[1], 3)
    g_single(1, 1, zg[1, 4], rk_in, far)
    drain(lall.at[1 - core], p_r)

    valid = iota((1024, 128), 1) < 96
    li, lj = iota((128, 128), 0), iota((128, 128), 1)
    fold = (lax.rem(li, 32) == lax.rem(lj, 32)).astype(F32)
    block = (li // 32 == lj // 32).astype(F32)
    block_h = block.astype(BF16)

    def rows_of(a):
        return jnp.sum(jnp.sum(a.reshape(8, 16, 8, 128), axis=1), axis=0)

    def total(acc):
        one = jnp.broadcast_to(jnp.sum(acc, axis=0, keepdims=True), (8, 128))
        return mm(one, fold, exact=True)

    acc = jnp.zeros((8, 128), F32)
    for i in range(2):
        d0 = jnp.where(valid, jnp.exp(lall[i].reshape(1024, 128)), 0.0)
        dd[i] = d0
        acc = acc + rows_of(d0)
    pad = jnp.where(iota((1, 128), 1) < 96, 0.0, 1.0)
    c = total(acc)
    cols[0:8, :] = c
    for p in range(2):
        acc = jnp.zeros((8, 128), F32)
        inverse = 1.0 / c[0:1, :]
        for i in range(2):
            q = dd[i] * inverse
            q_hi = q.astype(BF16)
            q_lo = (q - q_hi.astype(F32)).astype(BF16)
            d = q / (mm(q_hi, block_h) + mm(q_lo, block_h) + pad)
            dd[i] = d
            db[p, i] = d.astype(BF16)
            acc = acc + rows_of(d)
        c = total(acc)
        cols[8 * p + 8 : 8 * p + 16, :] = c

    c3 = jnp.concatenate([cols[0:1, :], cols[8:9, :], cols[16:17, :]], axis=0)
    dens, quot = own_state(logits, c3)
    gates = NE * dens[3]

    lane256, row256 = iota((256, 128), 1), iota((256, 128), 0)
    q = dd[core, pl.ds(pl.multiple_of(x * 256, 256), 256), :] / c3[2:3, :]
    q_hi = q.astype(BF16)
    q_lo = (q - q_hi.astype(F32)).astype(BF16)
    group = NE * q / (mm(q_hi, block_h) + mm(q_lo, block_h) + pad)
    turned = jnp.zeros((256, 128), F32)
    for n in range(3):
        one = jnp.sum(jnp.where(lane256 == 32 * n + me_e, group, 0.0), axis=1, keepdims=True)
        turned = turned + jnp.where(lane256 == 8 * n + lax.rem(row256, 8), one, 0.0)
    gcol[...] = jnp.sum(turned.reshape(NE, 8, 128), axis=1).reshape(NE, 1, 128)
    drain(rk_col, rc_r)
    tiles = []
    for yy in range(4):
        for off in (0, 4, 7, 1, 6, 2, 5, 3):
            zz = lax.rem(z + off, 8)
            here = jnp.broadcast_to(rk_col[yy, zz], (8, 128)) == sub8.astype(F32)
            tiles.append(jnp.where(here, jnp.broadcast_to(gcol[yy * 8 + zz], (8, 128)), 0.0))
    gate = jnp.sum(jnp.concatenate(tiles, axis=0), axis=1, keepdims=True)
    gate = gate.astype(BF16).astype(F32)

    def plane(src, dst, send, recv):
        pltpu.make_async_copy(src(me_e), dst, recv).start()

        def go(k):
            to = lax.rem(me_e + k, NE)
            remote(src(to), dst, send, recv, (me_d, to)).start()

        others(NE, go)

    for c in loads:
        c.wait()

    def fill_t(yy, value):
        rt[yy, 0] = value

    y_wait(rt.at[0, 0], yr_t, qt, er_t, fill_t)
    cuts = []
    for o in range(4):
        at = pl.ds(pl.multiple_of(512 * o + 256 * (1 - core), 256), 256)
        cuts.append(
            remote(rt.at[:, :, :, at], pt.at[o], q_s.at[o], q_r.at[o], partner)
        )
        cuts[-1].start()

    def forward(i, carry):
        at = pl.ds(pl.multiple_of(i * 256, 256), 256)
        rows = rt[...].reshape(256, D)
        gate_pre = mm(rows, wg[:, at])
        up_pre = mm(rows, wu[:, at])
        sg = jax.nn.sigmoid(gate_pre)
        a = gate_pre * sg
        h = a * up_pre
        hid[:, at] = h
        act[:, at] = a
        dsl[:, at] = up_pre * sg * (1.0 + gate_pre * (1.0 - sg))
        ht[at, :] = h.T.astype(BF16)
        return carry

    ht_copies = [
        remote(ht.at[r], pht.at[r], ht_s.at[n], ht_r.at[n], partner)
        for n, r in enumerate(pl.ds(256 * i, 256) for i in range(3))
    ]

    def where_from(k):
        o = lax.rem(k, 8)
        j, h = o // 2, lax.rem(o, 2)
        yy = lax.rem(y + k // 8, 4)
        zz = lax.rem(z + h * (j + 4 * ((4 - j) // 4)) + (1 - h) * (8 - j), 8)
        return yy * 8 + o, yy * 8 + zz

    def fill_g(h):
        def f(yy, value):
            rg[yy, 0, :, 1024 * h : 1024 * h + 1024] = value
        return f

    ds_copies = []

    def scaled(h):
        y_wait(rg.at[0, 0, :, cut(h)], yr_g.at[h], qg.at[h], er_g.at[h], fill_g(h))
        for b in range(2 * h, 2 * h + 2):
            at = slice(512 * b, 512 * b + 512)
            ds[:, at] = (gate * rg[:, :, :, at].reshape(256, 512).astype(F32)).astype(BF16)
        c = remote(ds.at[:, cut(h)], pds.at[:, cut(h)], q_s.at[5 + h], q_r.at[5 + h], partner)
        c.start()
        ds_copies.append(c)

    def my_rows(ref, j):
        o = lax.rem(x + j, NX)
        return ref[pl.ds(pl.multiple_of(192 * o + 96 * core, 32), 96), :]

    half, early = [], []

    def down_half(h):
        ds_copies[h].wait_recv()

        def rows(js):
            def one(i, carry):
                at = pl.ds(pl.multiple_of(1024 * h + i * 512, 512), 512)
                to = pl.ds(pl.multiple_of(i * 512, 512), 512)
                mine = jnp.concatenate([my_rows(ht, j) for j in js], axis=0)
                theirs = jnp.concatenate([my_rows(pht, j) for j in js], axis=0)
                out = mm(mine, ds[:, at]) + mm(theirs, pds[:, at])
                for n, j in enumerate(js):
                    g2[h, j, :, to] = out[96 * n : 96 * n + 96].astype(BF16)
                return carry

            lax.fori_loop(0, 2, one, 0)

        top, low = pl.ds(0, 48), pl.ds(48, 48)
        n = 2 * h
        half.append(remote(g2.at[h, 2, top], ra2.at[h], h_s.at[n], h_r.at[n], right))
        half.append(remote(g2.at[h, 2, low], rb2.at[h], h_s.at[n + 1], h_r.at[n + 1], left))
        early.append(
            remote(g2.at[h, 1, low], rc2.at[h, low], n_s.at[n], n_r.at[n], right)
        )
        early.append(
            remote(g2.at[h, 3, top], rd2.at[h, top], n_s.at[n + 1], n_r.at[n + 1], left)
        )
        rows((2,))
        half[-2].start()
        half[-1].start()
        rows((1, 3, 0))

    for n in range(3):
        lax.fori_loop(n, n + 1, forward, 0)
        ht_copies[n].start()
        if n == 1:
            scaled(0)
    for c in ht_copies:
        c.wait_recv()
    down_half(0)
    early[0].start()
    early[1].start()
    scaled(1)

    def backward(i, total_score):
        at = pl.ds(pl.multiple_of(i * 256, 256), 256)
        at_up = pl.ds(pl.multiple_of(i * 256 + FF, 256), 256)
        h = mm(rg[...].reshape(256, D), wd[at, :], NT)
        a = (h * dsl[:, at]).astype(BF16)
        b = (h * act[:, at]).astype(BF16)
        gg[:, at] = a
        ug[:, at] = b
        pair[:, at] = (gate * a.astype(F32)).astype(BF16)
        pair[:, at_up] = (gate * b.astype(F32)).astype(BF16)
        return total_score + jnp.sum(h * hid[:, at], axis=1, keepdims=True)

    score = lax.fori_loop(0, 3, backward, jnp.zeros((256, 1), F32))
    pair_copy = remote(pair, ppair, q_s.at[7], q_r.at[7], partner)
    pair_copy.start()
    spread8 = jnp.broadcast_to(score.astype(BF16).astype(F32), (256, 128)).reshape(NE, 8, 128)
    diag = iota((NE, 8, 128), 1) == iota((NE, 8, 128), 2)
    stile[...] = jnp.sum(jnp.where(diag, spread8, 0.0), axis=1).reshape(NE, 1, 128)
    pltpu.make_async_copy(stile.at[where_from(0)[0]], sbuf.at[me_e], sc_r).start()

    def send_score(k):
        n, to = where_from(k)
        remote(stile.at[n], sbuf.at[me_e], sc_s, sc_r, (me_d, to)).start()

    others(NE, send_score)

    down_half(1)
    for n in range(2):
        at = pl.ds(64 * n, 64)
        half += [
            remote(g1.at[2, at], ra1.at[at], h_s.at[2 * n + 4], h_r.at[2 * n + 4], right),
            remote(
                g1.at[2, pl.ds(128 + 64 * n, 64)], rb1.at[at],
                h_s.at[2 * n + 5], h_r.at[2 * n + 5], left,
            ),
        ]
    for c in cuts:
        c.wait_recv()
    pair_copy.wait_recv()

    def pair_part(j):
        o = lax.rem(x + j, NX)
        col = pl.ds(pl.multiple_of(512 * o + 256 * core, 256), 256)

        def one(i, carry):
            at = pl.ds(pl.multiple_of(i * 512, 512), 512)
            out = mm(rt[:, :, :, col].reshape(256, 256), pair[:, at], TN)
            out = out + mm(pt[o].reshape(256, 256), ppair[:, at], TN)
            g1[j, :, at] = out.astype(BF16)
            return carry

        lax.fori_loop(0, 3, one, 0)

    pair_part(2)
    for c in half[4:8]:
        c.start()
    for b in range(4):
        at = slice(512 * b, 512 * b + 512)
        out = mm(gg[...], wg[at, :], NT) + mm(ug[...], wu[at, :], NT)
        rows = 8 * (b // 2)
        cut = slice(512 * (b % 2), 512 * (b % 2) + 512)
        bsend[:, rows : rows + 8, cut] = out.reshape(NE, 8, 512).astype(BF16)

    def send_back(k):
        n, to = where_from(k)
        remote(bsend.at[n], ret.at[me_e], ret_s, ret_r, (me_d, to)).start()

    pltpu.make_async_copy(bsend.at[where_from(0)[0]], ret.at[me_e], ret_r).start()
    lax.fori_loop(1, 5, lambda k, c: (send_back(k), c)[1], 0)
    pair_part(1)
    pair_part(3)
    pair_part(0)

    drain(sbuf, sc_r)
    eye32 = (iota((NE, 128), 0) == iota((NE, 128), 1)).astype(BF16)
    scores = mm(sbuf[...].reshape(NE, 128).astype(BF16), eye32, TN)
    grad3 = jnp.zeros((TOK, 128), F32)
    for slot in range(CAP):
        grad3 = grad3 + jnp.where(
            rank == slot, jnp.broadcast_to(scores[slot : slot + 1, :], (TOK, 128)), 0.0
        )
    g = NE * grad3 * dens[3]
    h3 = g - dens[3] * jnp.sum(g, axis=1, keepdims=True)
    atile[...] = jnp.sum(h3, axis=0, keepdims=True)
    plane(lambda e: atile, abuf.at[me_e], a_s, a_r)
    lax.fori_loop(5, 16, lambda k, c: (send_back(k), c)[1], 0)

    gates_hi = gates.astype(BF16).astype(F32)
    ex_i, ex_j = iota((128, 512), 0), iota((128, 512), 1)
    spread = ((ex_i < NE) & (ex_j // 16 == ex_i)).astype(BF16)
    wide = mm(
        jnp.concatenate([rank, gates_hi, gates - gates_hi], axis=0).astype(BF16), spread
    )
    k16 = lax.rem(iota((TOK, 512), 1), 16)
    rank_w = wide[0:TOK].astype(jnp.int32)
    parts = []
    for m in (rank_w == k16, rank_w == k16 - 8):
        parts += [jnp.where(m, wide[TOK : 2 * TOK], 0.0), jnp.where(m, wide[2 * TOK :], 0.0)]
    weights = jnp.concatenate(parts, axis=0).astype(BF16)

    for p in range(2):
        dens_h = db[p].reshape(2048, 128)
        g = mm(dens_h, dens_h, TN)
        gram[p] = mm(mm(fold, g * block, exact=True), fold, exact=True)

    drain(abuf, a_r)
    btile[...] = jnp.sum(abuf[...], axis=0)
    pltpu.make_async_copy(btile, bbuf.at[me_d], b_r).start()
    others(
        ND,
        lambda k: remote(
            btile, bbuf.at[me_d], b_s, b_r, (lax.rem(me_d + k, ND), me_e)
        ).start(),
    )
    for n in range(2):
        up, down = pl.ds(128 + 64 * n, 64), pl.ds(64 * n, 64)
        early += [
            remote(g1.at[1, up], rc1.at[up], n_s.at[2 * n + 4], n_r.at[2 * n + 4], right),
            remote(g1.at[3, down], rd1.at[down], n_s.at[2 * n + 5], n_r.at[2 * n + 5], left),
        ]
    for c in early[2:6]:
        c.start()

    drain(bbuf, b_r)
    v = jnp.broadcast_to(jnp.sum(bbuf[...], axis=0), (8, 128))
    first32 = lane8 < NE
    u = mm(jnp.where(first32, v / cols[16:24, :], 0.0), gram[1], exact=True)
    s = mm(jnp.where(first32, u / cols[8:16, :], 0.0), gram[0], exact=True)
    qv = quot[2] * v[0:1, :]
    h2 = h3 - qv + dens[2] * jnp.sum(qv, axis=1, keepdims=True)
    qu = quot[1] * u[0:1, :]
    h1 = h2 - qu + dens[1] * jnp.sum(qu, axis=1, keepdims=True)
    lgrad = (h1 - quot[0] * s[0:1, :]).astype(BF16)[:, :NE]
    router_t = mm(lgrad, tokens[...], TN)
    for p in range(NE):
        h, b = p % 2, p // 2
        rsend[p] = router_t[16 * h : 16 * h + 16, 128 * b : 128 * b + 128].astype(BF16)
    plane(lambda e: rsend.at[e], rrecv.at[me_e], rs_s, rs_r)
    lax.fori_loop(16, NE, lambda k, c: (send_back(k), c)[1], 0)
    router_in = mm(lgrad, rw[...])

    def add_rows(n, rows, terms, out):
        def one(i, c):
            at = pl.ds(pl.multiple_of(i * rows, rows), rows)
            out(at, functools.reduce(lambda a, b: a + b, [t(at).astype(F32) for t in terms]))
            return c

        lax.fori_loop(0, n // rows, one, 0)

    def put(ref, j, base):
        def f(at, value):
            ref[j, pl.ds(pl.multiple_of(at.start + base, 16), at.size), :] = value.astype(BF16)
        return f

    def take(ref, j, base):
        return lambda at: ref[j, pl.ds(pl.multiple_of(at.start + base, 16), at.size), :]

    for c in half:
        c.wait_recv()
    for h in range(2):
        add_rows(
            48, 48, [take(g2.at[h], 1, 0), lambda at, h=h: ra2[h, at, :]], put(g2.at[h], 1, 0)
        )
        add_rows(
            48, 48, [take(g2.at[h], 3, 48), lambda at, h=h: rb2[h, at, :]], put(g2.at[h], 3, 48)
        )
    add_rows(128, 32, [take(g1, 1, 0), lambda at: ra1[at, :]], put(g1, 1, 0))
    add_rows(128, 32, [take(g1, 3, 128), lambda at: rb1[at, :]], put(g1, 3, 128))
    late = []
    for h in range(2):
        top, low = pl.ds(0, 48), pl.ds(48, 48)
        late += [
            remote(g2.at[h, 1, top], rc2.at[h, top], m_s.at[2 * h], m_r.at[2 * h], right),
            remote(
                g2.at[h, 3, low], rd2.at[h, low], m_s.at[2 * h + 1], m_r.at[2 * h + 1], left
            ),
        ]
    late += [
        remote(g1.at[1, pl.ds(0, 128)], rc1.at[pl.ds(0, 128)], m_s.at[4], m_r.at[4], right),
        remote(g1.at[3, pl.ds(128, 128)], rd1.at[pl.ds(128, 128)], m_s.at[5], m_r.at[5], left),
    ]

    for c in late[0:2] + early[6:8]:
        c.start()
    drain(rrecv, rs_r)
    dsum[...] = jnp.sum(rrecv[...].astype(F32), axis=0).astype(BF16)
    pltpu.make_async_copy(dsum, drecv.at[me_d], d_r).start()
    others(
        ND,
        lambda k: remote(
            dsum, drecv.at[me_d], d_s, d_r, (lax.rem(me_d + k, ND), me_e)
        ).start(),
    )
    for c in late[2:6]:
        c.start()
    drain(drecv, d_r)
    fin[...] = jnp.sum(drecv[...].astype(F32), axis=0).astype(BF16)
    plane(lambda e: fin, router_out.at[me_e], o_s, o_r)

    drain(ret, ret_r)
    mixed = mm(weights, ret[...].reshape(512, 1024))
    gt_out[:, 0:1024] = (mixed[0:24] + mixed[24:48] + router_in[:, 0:1024]).astype(BF16)
    gt_out[:, 1024:2048] = (mixed[48:72] + mixed[72:96] + router_in[:, 1024:2048]).astype(BF16)

    for c in early + late:
        c.wait_recv()

    def store(ref):
        def f(at, value):
            ref[at, :] = value.astype(BF16)
        return f

    def store_half(h):
        def f(at, value):
            down_out[at, 1024 * h : 1024 * h + 1024] = value.astype(BF16)
        return f

    for h in range(2):
        add_rows(
            96, 48,
            [
                take(g2.at[h], 0, 0),
                lambda at, h=h: rc2[h, at, :],
                lambda at, h=h: rd2[h, at, :],
            ],
            store_half(h),
        )
    add_rows(
        256, 32, [take(g1, 0, 0), lambda at: rc1[at, :], lambda at: rd1[at, :]], store(pair_out)
    )
    drain(router_out, o_r)

    for c in t_dn + t_up + g_dn[0] + g_dn[1] + g_up[0] + g_up[1] + ds_copies + y_copies + lg_copies + cuts + half + early + late:
        c.wait_send()
    for c in [logit_pair, pair_copy] + ht_copies:
        c.wait_send()
    drain(rk_in.at[pl.ds(0, 7)], rk_s)
    drain(pk_in.at[pl.ds(0, 7)], pk_s)
    drain(lall.at[0, pl.ds(0, NX - 1)], x_s)
    drain(ret.at[pl.ds(0, NE - 1)], ret_s)
    drain(sbuf.at[pl.ds(0, NE - 1)], sc_s)
    drain(abuf.at[pl.ds(0, NE - 1)], a_s)
    drain(bbuf.at[pl.ds(0, ND - 1)], b_s)
    drain(rrecv.at[pl.ds(0, NE - 1)], rs_s)
    drain(drecv.at[pl.ds(0, ND - 1)], d_s)
    drain(router_out.at[pl.ds(0, NE - 1)], o_s)


def moe(*args):
    dma = pltpu.SemaphoreType.DMA
    V = pltpu.VMEM
    hbm = pl.BlockSpec(memory_space=pltpu.HBM)
    return pl.pallas_call(
        moe_kernel,
        name="moe",
        out_shape=(
            jax.ShapeDtypeStruct((TOK, D), BF16),
            jax.ShapeDtypeStruct((256, 2 * FF), BF16),
            jax.ShapeDtypeStruct((96, D), BF16),
            jax.ShapeDtypeStruct((NE, 16, 128), BF16),
        ),
        in_specs=[hbm] * 7,
        out_specs=(VM,) * 4,
        scratch_shapes=[
            V((TOK, D), BF16), V((TOK, D), BF16), V((8, TOK), jnp.int32), V((NE, D), BF16),
            V((D, FF), BF16), V((D, FF), BF16), V((FF, D), BF16),
            V((8, 4, 1, 128), F32), V((8, 4, 1, 128), F32), V((4, 8, 1, 128), F32),
            V((8, 128), F32), V((8, 8, 128), F32),
            V((2, 4, 16, 1024), BF16), V((2, 2, 4, 16, 512), BF16),
            V((4, 2, 16, 1024), BF16), V((2, 4, 2, 16, 512), BF16),
            V((2, NX, NE, 8, 128), F32), V((2, 1024, 128), F32), V((2, 2, 1024, 128), BF16),
            V((24, 128), F32), V((2, 128, 128), F32), V((NE, 1, 128), F32),
            V((8, TOK, D), BF16), V((2, 8, TOK, 1024), BF16),
            V((4, 4, 16, D), BF16), V((2, 4, 4, 16, 1024), BF16),
            V((4, 4, 16, D), BF16), V((4, 4, 16, D), BF16),
            V((4, 4, 4, 16, 256), BF16),
            V((256, FF), F32), V((256, FF), F32), V((256, FF), F32),
            V((FF, 256), BF16), V((FF, 256), BF16),
            V((256, D), BF16), V((256, D), BF16),
            V((256, FF), BF16), V((256, FF), BF16),
            V((256, 2 * FF), BF16), V((256, 2 * FF), BF16),
            V((4, 256, 2 * FF), BF16), V((2, 4, 96, 1024), BF16),
            V((128, 2 * FF), BF16), V((2, 48, 1024), BF16),
            V((128, 2 * FF), BF16), V((2, 48, 1024), BF16),
            V((256, 2 * FF), BF16), V((2, 96, 1024), BF16),
            V((256, 2 * FF), BF16), V((2, 96, 1024), BF16),
            V((NE, 16, 1024), BF16), V((NE, 16, 1024), BF16),
            V((NE, 1, 128), F32), V((NE, 1, 128), F32),
            V((1, 128), F32), V((NE, 1, 128), F32),
            V((1, 128), F32), V((ND, 1, 128), F32),
            V((NE, 16, 128), BF16), V((NE, 16, 128), BF16),
            V((16, 128), BF16), V((ND, 16, 128), BF16), V((16, 128), BF16),
            dma((4,)), dma((3,)),
            dma((8,)), dma((8,)), dma((2, 8)), dma((2, 8)),
            dma((4, 4)), dma((4, 4)), dma((2, 4, 4)), dma((2, 4, 4)),
            dma((2, 4)), dma((2, 4)), dma((2, 2, 4)), dma((2, 2, 4)),
            dma((8,)), dma((8,)),
            dma((8,)), dma((8,)), dma((8,)), dma((8,)), dma((6,)), dma((6,)),
            dma((3,)), dma((3,)), dma((3,)), dma, dma((3,)), dma,
        ]
        + [dma] * 22,
        compiler_params=pltpu.CompilerParams(
            collective_id=0, has_side_effects=True, vmem_limit_bytes=52 * 1024 * 1024
        ),
    )(*args)


def write_kernel(gt, pair, down, router, gt_o, router_o, gate_o, up_o, down_o):
    gt_o[...] = gt[...]
    gate_o[0] = pair[:, 0:FF]
    up_o[0] = pair[:, FF : 2 * FF]
    down_o[0] = down[...]
    for p in range(NE):
        h, b = p % 2, p // 2
        router_o[16 * h : 16 * h + 16, 128 * b : 128 * b + 128] = router[p].astype(F32)


def write(*args):
    return pl.pallas_call(
        write_kernel,
        name="write",
        out_shape=(
            jax.ShapeDtypeStruct((TOK, D), BF16),
            jax.ShapeDtypeStruct((NE, D), F32),
            jax.ShapeDtypeStruct((1, 256, FF), BF16),
            jax.ShapeDtypeStruct((1, 256, FF), BF16),
            jax.ShapeDtypeStruct((1, 96, D), BF16),
        ),
        in_specs=[VM] * 4,
        out_specs=(VM,) * 5,
        compiler_params=pltpu.CompilerParams(vmem_limit_bytes=16 * 1024 * 1024),
    )(*args)


def per_device(tokens, out_grad, expert_ids, router_weight, w_gate, w_up, w_down):
    gt, pair, down, router = moe(
        *[
            pltpu.with_memory_space_constraint(a, pltpu.HBM)
            for a in (tokens, out_grad, expert_ids.T, router_weight.T)
        ],
        w_gate, w_up, w_down
    )
    gt, router, gate, up, down = write(gt, pair, down, router)
    return gt, router.T, gate, up, down


def solution(mesh):
    in_specs = (
        P(("dp", "expert"), None), P(("dp", "expert"), None), P(("dp", "expert"), None), P(),
        P("expert", None, None), P("expert", None, None), P("expert", None, None),
    )
    out_specs = (
        P(("dp", "expert"), None), P(),
        P("expert", "dp", None), P("expert", "dp", None), P("expert", "dp", None),
    )
    return jax.shard_map(
        per_device, mesh=mesh, in_specs=in_specs, out_specs=out_specs, check_vma=False
    )
```

```python
import functools

import jax
import jax.numpy as jnp
from jax import lax
from jax.experimental import pallas as pl
from jax.experimental.pallas import tpu as pltpu
from jax.sharding import PartitionSpec as P

HI = lax.Precision.HIGHEST
F32 = jnp.float32
BF16 = jnp.bfloat16
NE = 32
ND = 8
NX = 4
TOK = 24
CAP = 8
D = 2048
FF = 768
VM = pl.BlockSpec(memory_space=pltpu.VMEM)
MESH = pl.DeviceIdType.MESH


def iota(shape, dim):
    return lax.broadcasted_iota(jnp.int32, shape, dim)


def remote(src, dst, send, recv, dev):
    return pltpu.make_async_remote_copy(
        src_ref=src, dst_ref=dst, send_sem=send, recv_sem=recv, device_id=dev, device_id_type=MESH
    )


def drain(ref, sem):
    pltpu.make_async_copy(ref, ref, sem).wait()


def place():
    me_d = lax.axis_index("dp")
    return me_d, lax.axis_index("expert"), me_d // 2, lax.rem(me_d, 2)


def others(n, body):
    lax.fori_loop(1, n, lambda k, c: (body(k), c)[1], 0)


def own_state(logits, cols):
    lane = iota((TOK, 128), 1)
    d = jnp.where(lane < NE, jnp.exp(logits), 0.0)
    ds, qs = [d], []
    for p in range(3):
        q = d / cols[p : p + 1, :]
        d = q / jnp.sum(q, axis=1, keepdims=True)
        qs.append(q)
        ds.append(d)
    return ds, qs


NT = (((1,), (1,)), ((), ()))
TN = (((0,), (0,)), ((), ()))


def mm(a, b, dims=None, exact=False):
    dims = dims or (((1,), (0,)), ((), ()))
    return lax.dot_general(
        a, b, dims, precision=HI if exact else None, preferred_element_type=F32
    )


def moe_kernel(
    tokens_hbm, grads_hbm, ids_hbm, rw_hbm, wg_hbm, wu_hbm, wd_hbm,
    gt_out, pair_out, down_out, router_out,
    tokens, grads, ids, rw, wg, wu, wd, rk_out, rk_in, rk_col, pk_out, pk_in, et, eg, qt, qg,
    lall, dd, db, cols, gram, gcol,
    zt, zg, yt, yg, rt, rg, pt, hid, act, dsl, ht, pht, ds, pds, gg, ug, pair, ppair,
    g1, g2, ra1, ra2, rb1, rb2, rc1, rc2, rd1, rd2,
    bsend, ret, stile, sbuf, atile, abuf, btile, bbuf, rsend, rrecv, dsum, drecv, fin,
    in_sem, w_sem, zs_t, zr_t, zs_g, zr_g, ys_t, yr_t, ys_g, yr_g, es_t, er_t, es_g, er_g, q_s, q_r, h_s, h_r, n_s, n_r, m_s, m_r,
    ht_s, ht_r, lg_s, lg_r, rc_s, rc_r, rk_s, rk_r, pk_s, pk_r, x_s, x_r, p_s, p_r, ret_s, ret_r, sc_s, sc_r,
    a_s, a_r, b_s, b_r, rs_s, rs_r, d_s, d_r, o_s, o_r,
):
    me_d, me_e, x, core = place()
    y, z = me_e // 8, lax.rem(me_e, 8)
    inputs = [
        pltpu.make_async_copy(a, b, in_sem.at[n])
        for n, (a, b) in enumerate(
            ((tokens_hbm, tokens), (grads_hbm, grads), (ids_hbm, ids), (rw_hbm, rw))
        )
    ]
    for c in inputs:
        c.start()
    barrier = pltpu.get_barrier_semaphore()
    others(
        NE,
        lambda k: pl.semaphore_signal(
            barrier, inc=1, device_id=(me_d, lax.rem(me_e + k, NE)), device_id_type=MESH
        ),
    )
    others(
        ND,
        lambda k: pl.semaphore_signal(
            barrier, inc=1, device_id=(lax.rem(me_d + k, ND), me_e), device_id_type=MESH
        ),
    )
    loads = [
        pltpu.make_async_copy(a.at[0], b, w_sem.at[n])
        for n, (a, b) in enumerate(((wg_hbm, wg), (wu_hbm, wu), (wd_hbm, wd)))
    ]
    for c in loads:
        c.start()
    for c in inputs:
        c.wait()
    partner = (x * 2 + 1 - core, me_e)
    right = (lax.rem(x + 1, NX) * 2 + core, me_e)
    left = (lax.rem(x + 3, NX) * 2 + core, me_e)
    z_up = (me_d, y * 8 + lax.rem(z + 1, 8))
    z_down = (me_d, y * 8 + lax.rem(z + 7, 8))

    lane8, sub8 = iota((8, 128), 1), iota((8, 128), 0)
    logits = jnp.concatenate(
        [mm(tokens[...], rw[...], NT), jnp.zeros((TOK, 96), F32)], axis=1
    )
    packed = (
        logits[0:8] + pltpu.roll(logits[8:16], 32, 1) + pltpu.roll(logits[16:24], 64, 1)
    )
    picked_t = jnp.zeros((128, TOK), F32)
    for k in range(8):
        picked_t = picked_t + (ids[k : k + 1, :] == iota((128, TOK), 0)).astype(F32)
    picked_t = picked_t.astype(BF16)
    row_t, col_t = iota((TOK, TOK), 0), iota((TOK, TOK), 1)
    picked = mm((row_t == col_t).astype(BF16), picked_t, NT)
    rank = jnp.where(picked > 0, mm((row_t > col_t).astype(BF16), picked_t, NT), -64.0)
    rank_pad = jnp.concatenate([rank, jnp.full((104, 128), -64.0, F32)], axis=0).astype(BF16)
    pi, pj = iota((32, 128), 0), iota((32, 128), 1)
    place_rows = (pj == lax.rem(pi, 4) * 8 + pi // 4).astype(BF16)
    rk_out[...] = mm(place_rows, rank_pad, NT).reshape(8, 4, 1, 128)
    pk_out[...] = packed

    pl.semaphore_wait(barrier, NE - 1 + ND - 1)

    def z_send(k):
        to = lax.rem(z + k, 8)
        dev = (me_d, y * 8 + to)
        remote(rk_out.at[to], rk_in.at[z], rk_s, rk_r, dev).start()
        remote(pk_out, pk_in.at[z], pk_s, pk_r, dev).start()

    pltpu.make_async_copy(rk_out.at[z], rk_in.at[z], rk_r).start()
    pltpu.make_async_copy(pk_out, pk_in.at[z], pk_r).start()
    others(8, z_send)

    def z_copy(own, buf, ss, rs, k, sign):
        at = lambda n: (8 + sign * n) % 8
        return remote(
            own if k == 1 else buf.at[at(k - 1)], buf.at[at(k)], ss.at[at(k)], rs.at[at(k)],
            z_down if sign > 0 else z_up,
        )

    def pipes(ref, buf, ss, rs, down, up):
        dn_list, up_list = [], []
        for h in range(2):
            own = ref.at[:, pl.ds(1024 * h, 1024)]
            args = (own, buf.at[h], ss.at[h], rs.at[h])
            dn_list.append([z_copy(*args, k, -1) for k in range(1, down + 1)])
            up_list.append([z_copy(*args, k, 1) for k in range(1, up + 1)])
        return dn_list, up_list

    t_dn, t_up = pipes(tokens, zt, zs_t, zr_t, 4, 3)
    g_dn, g_up = pipes(grads, zg, zs_g, zr_g, 3, 4)
    for pipe in (t_dn[0], t_up[0], t_dn[1], t_up[1], g_dn[0], g_up[0]):
        pipe[0].start()

    def hot(ref, at, yy):
        row = ref[at, yy]
        return (jnp.broadcast_to(row, (8, 128)) == sub8.astype(F32)).astype(F32)

    def choose(at, half):
        none = jnp.zeros((8, 128), F32)
        parts = []
        for yy in range(4):
            one = hot(rk_in, at, yy)
            parts += [one, none] if half == 0 else [none, one]
        return jnp.concatenate(parts, axis=0).astype(BF16)[:, :TOK]

    y_copies = []

    def y_send(src, dst, ss, rs, j):
        for m in range(1, 4):
            to = lax.rem(y + m, 4)
            c = remote(src(to), dst, ss.at[j, m], rs.at[j, m], (me_d, to * 8 + z))
            c.start()
            y_copies.append(c)
        pltpu.make_async_copy(src(y), dst, rs.at[j, 0]).start()

    def y_pair(j, buf, send_buf, dst, ss, rs):
        out = mm(choose(lax.rem(z + 8 - j, 8), 0), buf(8 - j))
        out = out + mm(choose(lax.rem(z + j, 8), 1), buf(j))
        send_buf[j] = out.astype(BF16).reshape(4, 16, out.shape[1])
        y_send(lambda to: send_buf.at[j, to], dst, ss, rs, j)

    def y_single(n, block, ref, at, send_buf, dst, ss, rs):
        pick = jnp.concatenate([hot(ref, at, yy) for yy in range(4)], axis=0)
        out = mm(pick.astype(BF16)[:, :TOK], block)
        w = out.shape[1] // 2
        for yy in range(4):
            rows = out[8 * yy : 8 * yy + 8]
            send_buf[n, yy] = jnp.concatenate([rows[:, :w], rows[:, w:]], axis=0).astype(BF16)
        y_send(lambda to: send_buf.at[n, to], dst, ss, rs, n)

    def y_wait(view, rs, one_buf, one_rs, fill):
        for m in range(4):
            for j in range(1, 4):
                drain(view, rs.at[j, m])
            for n in range(2):
                drain(one_buf.at[0, 0], one_rs.at[n, m])
        for yy in range(4):
            parts = []
            for n in range(2):
                a = one_buf[yy, n].astype(F32)
                parts.append(jnp.concatenate([a[0:8], a[8:16]], axis=1))
            fill(yy, jnp.concatenate(parts, axis=0).astype(BF16))

    def arrive(down, up, k):
        if k < len(down):
            down[k].wait_recv()
            if k + 1 < len(down):
                down[k + 1].start()
        if k < len(up):
            up[k].wait_recv()
            if k + 1 < len(up):
                up[k + 1].start()

    def cut(h):
        return pl.ds(1024 * h, 1024)

    def t_block(n):
        return jnp.concatenate([zt[0, n], zt[1, n]], axis=1)

    def t_pair(j):
        y_pair(j, t_block, yt, rt.at[y, j], ys_t, yr_t)

    def t_single(n, block, ref, at):
        y_single(n, block, ref, at, et, qt.at[y, n], es_t, er_t)

    def g_pair(h, j):
        y_pair(j, lambda n: zg[h, n], yg.at[h], rg.at[y, j, :, cut(h)], ys_g.at[h], yr_g.at[h])

    def g_single(h, n, block, ref, at):
        y_single(n, block, ref, at, eg.at[h], qg.at[h, y, n], es_g.at[h], er_g.at[h])

    t_single(0, tokens[...], rk_out, z)
    g_single(0, 0, grads[:, 0:1024], rk_out, z)

    drain(rk_in, rk_r)
    drain(pk_in, pk_r)
    own_rows = lall.at[core, x, pl.ds(pl.multiple_of(y * 8, 8), 8)]
    pltpu.make_async_copy(pk_in, own_rows, lg_r).start()
    pltpu.make_async_copy(rk_in.at[:, y], rk_col.at[y], rc_r).start()
    lg_copies = []
    for m in range(1, 4):
        to = lax.rem(y + m, 4)
        dev = (me_d, to * 8 + z)
        lg_copies.append(remote(pk_in, own_rows, lg_s.at[m - 1], lg_r, dev))
        lg_copies.append(remote(rk_in.at[:, to], rk_col.at[y], rc_s.at[m - 1], rc_r, dev))
    for c in lg_copies:
        c.start()

    far = lax.rem(z + 4, 8)
    def arrive_t(k):
        for h in range(2):
            arrive(t_dn[h], t_up[h], k)

    def arrive_g(h, k):
        arrive(g_dn[h], g_up[h], k)

    arrive_t(0)
    t_pair(1)
    arrive_g(0, 0)
    g_dn[1][0].start()
    g_up[1][0].start()
    g_pair(0, 1)
    drain(lall.at[core, x], lg_r)
    others(
        NX,
        lambda k: remote(
            lall.at[core, x], lall.at[core, x], x_s, x_r, (lax.rem(x + k, NX) * 2 + core, me_e)
        ).start(),
    )
    arrive_t(1)
    t_pair(2)
    arrive_g(0, 1)
    arrive_g(1, 0)
    g_pair(0, 2)
    arrive_t(2)
    t_pair(3)
    arrive_g(0, 2)
    arrive_g(1, 1)
    arrive_t(3)
    t_single(1, t_block(4), rk_in, far)
    g_pair(0, 3)
    drain(lall.at[core, pl.ds(0, NX - 1)], x_r)
    logit_pair = remote(lall.at[core], lall.at[core], p_s, p_r, partner)
    logit_pair.start()
    arrive_g(0, 3)
    g_single(0, 1, zg[0, 4], rk_in, far)
    arrive_g(1, 2)
    g_single(1, 0, grads[:, 1024:2048], rk_out, z)
    g_pair(1, 1)
    g_pair(1, 2)
    g_pair(1, 3)
    drain(lall.at[1 - core], p_r)

    valid = iota((1024, 128), 1) < 96
    li, lj = iota((128, 128), 0), iota((128, 128), 1)
    fold = (lax.rem(li, 32) == lax.rem(lj, 32)).astype(F32)
    block = (li // 32 == lj // 32).astype(F32)
    block_h = block.astype(BF16)

    def rows_of(a):
        return jnp.sum(jnp.sum(a.reshape(8, 16, 8, 128), axis=1), axis=0)

    def total(acc):
        one = jnp.broadcast_to(jnp.sum(acc, axis=0, keepdims=True), (8, 128))
        return mm(one, fold, exact=True)

    acc = jnp.zeros((8, 128), F32)
    for i in range(2):
        d0 = jnp.where(valid, jnp.exp(lall[i].reshape(1024, 128)), 0.0)
        dd[i] = d0
        acc = acc + rows_of(d0)
    pad = jnp.where(iota((1, 128), 1) < 96, 0.0, 1.0)
    c = total(acc)
    cols[0:8, :] = c
    for p in range(2):
        acc = jnp.zeros((8, 128), F32)
        inverse = 1.0 / c[0:1, :]
        for i in range(2):
            q = dd[i] * inverse
            q_hi = q.astype(BF16)
            q_lo = (q - q_hi.astype(F32)).astype(BF16)
            d = q / (mm(q_hi, block_h) + mm(q_lo, block_h) + pad)
            dd[i] = d
            db[p, i] = d.astype(BF16)
            acc = acc + rows_of(d)
        c = total(acc)
        cols[8 * p + 8 : 8 * p + 16, :] = c

    c3 = jnp.concatenate([cols[0:1, :], cols[8:9, :], cols[16:17, :]], axis=0)
    dens, quot = own_state(logits, c3)
    gates = NE * dens[3]

    lane256, row256 = iota((256, 128), 1), iota((256, 128), 0)
    q = dd[core, pl.ds(pl.multiple_of(x * 256, 256), 256), :] / c3[2:3, :]
    q_hi = q.astype(BF16)
    q_lo = (q - q_hi.astype(F32)).astype(BF16)
    group = NE * q / (mm(q_hi, block_h) + mm(q_lo, block_h) + pad)
    turned = jnp.zeros((256, 128), F32)
    for n in range(3):
        one = jnp.sum(jnp.where(lane256 == 32 * n + me_e, group, 0.0), axis=1, keepdims=True)
        turned = turned + jnp.where(lane256 == 8 * n + lax.rem(row256, 8), one, 0.0)
    gcol[...] = jnp.sum(turned.reshape(NE, 8, 128), axis=1).reshape(NE, 1, 128)
    drain(rk_col, rc_r)
    tiles = []
    for yy in range(4):
        for off in (0, 4, 7, 1, 6, 2, 5, 3):
            zz = lax.rem(z + off, 8)
            here = jnp.broadcast_to(rk_col[yy, zz], (8, 128)) == sub8.astype(F32)
            tiles.append(jnp.where(here, jnp.broadcast_to(gcol[yy * 8 + zz], (8, 128)), 0.0))
    gate = jnp.sum(jnp.concatenate(tiles, axis=0), axis=1, keepdims=True)
    gate = gate.astype(BF16).astype(F32)
    arrive_g(1, 3)
    g_single(1, 1, zg[1, 4], rk_in, far)

    def plane(src, dst, send, recv):
        pltpu.make_async_copy(src(me_e), dst, recv).start()

        def go(k):
            to = lax.rem(me_e + k, NE)
            remote(src(to), dst, send, recv, (me_d, to)).start()

        others(NE, go)

    for c in loads:
        c.wait()

    def fill_t(yy, value):
        rt[yy, 0] = value

    y_wait(rt.at[0, 0], yr_t, qt, er_t, fill_t)
    cuts = []
    for o in range(4):
        at = pl.ds(pl.multiple_of(512 * o + 256 * (1 - core), 256), 256)
        cuts.append(
            remote(rt.at[:, :, :, at], pt.at[o], q_s.at[o], q_r.at[o], partner)
        )

    def forward(i, carry):
        at = pl.ds(pl.multiple_of(i * 256, 256), 256)
        rows = rt[...].reshape(256, D)
        gate_pre = mm(rows, wg[:, at])
        up_pre = mm(rows, wu[:, at])
        sg = jax.nn.sigmoid(gate_pre)
        a = gate_pre * sg
        h = a * up_pre
        hid[:, at] = h
        act[:, at] = a
        dsl[:, at] = up_pre * sg * (1.0 + gate_pre * (1.0 - sg))
        ht[at, :] = h.T.astype(BF16)
        return carry

    ht_copies = [
        remote(ht.at[r], pht.at[r], ht_s.at[n], ht_r.at[n], partner)
        for n, r in enumerate(pl.ds(256 * i, 256) for i in range(3))
    ]

    def where_from(k):
        o = lax.rem(k, 8)
        j, h = o // 2, lax.rem(o, 2)
        yy = lax.rem(y + k // 8, 4)
        zz = lax.rem(z + h * (j + 4 * ((4 - j) // 4)) + (1 - h) * (8 - j), 8)
        return yy * 8 + o, yy * 8 + zz

    def fill_g(h):
        def f(yy, value):
            rg[yy, 0, :, 1024 * h : 1024 * h + 1024] = value
        return f

    ds_copies = []

    def scaled(h):
        y_wait(rg.at[0, 0, :, cut(h)], yr_g.at[h], qg.at[h], er_g.at[h], fill_g(h))
        for b in range(2 * h, 2 * h + 2):
            at = slice(512 * b, 512 * b + 512)
            ds[:, at] = (gate * rg[:, :, :, at].reshape(256, 512).astype(F32)).astype(BF16)
        c = remote(ds.at[:, cut(h)], pds.at[:, cut(h)], q_s.at[5 + h], q_r.at[5 + h], partner)
        c.start()
        ds_copies.append(c)

    def my_rows(ref, j):
        o = lax.rem(x + j, NX)
        return ref[pl.ds(pl.multiple_of(192 * o + 96 * core, 32), 96), :]

    half, early = [], []

    def down_half(h):
        ds_copies[h].wait_recv()

        def rows(js):
            def one(i, carry):
                at = pl.ds(pl.multiple_of(1024 * h + i * 512, 512), 512)
                to = pl.ds(pl.multiple_of(i * 512, 512), 512)
                mine = jnp.concatenate([my_rows(ht, j) for j in js], axis=0)
                theirs = jnp.concatenate([my_rows(pht, j) for j in js], axis=0)
                out = mm(mine, ds[:, at]) + mm(theirs, pds[:, at])
                for n, j in enumerate(js):
                    g2[h, j, :, to] = out[96 * n : 96 * n + 96].astype(BF16)
                return carry

            lax.fori_loop(0, 2, one, 0)

        top, low = pl.ds(0, 48), pl.ds(48, 48)
        n = 2 * h
        half.append(remote(g2.at[h, 2, top], ra2.at[h], h_s.at[n], h_r.at[n], right))
        half.append(remote(g2.at[h, 2, low], rb2.at[h], h_s.at[n + 1], h_r.at[n + 1], left))
        early.append(
            remote(g2.at[h, 1, low], rc2.at[h, low], n_s.at[n], n_r.at[n], right)
        )
        early.append(
            remote(g2.at[h, 3, top], rd2.at[h, top], n_s.at[n + 1], n_r.at[n + 1], left)
        )
        rows((2,))
        half[-2].start()
        half[-1].start()
        rows((1, 3, 0))

    for n in range(3):
        lax.fori_loop(n, n + 1, forward, 0)
        ht_copies[n].start()
        if n == 0:
            scaled(0)
            for c in cuts:
                c.start()
    for c in ht_copies:
        c.wait_recv()
    down_half(0)
    early[0].start()
    early[1].start()
    scaled(1)

    def backward(i, total_score):
        at = pl.ds(pl.multiple_of(i * 256, 256), 256)
        at_up = pl.ds(pl.multiple_of(i * 256 + FF, 256), 256)
        h = mm(rg[...].reshape(256, D), wd[at, :], NT)
        a = (h * dsl[:, at]).astype(BF16)
        b = (h * act[:, at]).astype(BF16)
        gg[:, at] = a
        ug[:, at] = b
        pair[:, at] = (gate * a.astype(F32)).astype(BF16)
        pair[:, at_up] = (gate * b.astype(F32)).astype(BF16)
        return total_score + jnp.sum(h * hid[:, at], axis=1, keepdims=True)

    score = lax.fori_loop(0, 3, backward, jnp.zeros((256, 1), F32))
    pair_copy = remote(pair, ppair, q_s.at[7], q_r.at[7], partner)
    pair_copy.start()
    spread8 = jnp.broadcast_to(score.astype(BF16).astype(F32), (256, 128)).reshape(NE, 8, 128)
    diag = iota((NE, 8, 128), 1) == iota((NE, 8, 128), 2)
    stile[...] = jnp.sum(jnp.where(diag, spread8, 0.0), axis=1).reshape(NE, 1, 128)
    pltpu.make_async_copy(stile.at[where_from(0)[0]], sbuf.at[me_e], sc_r).start()

    def send_score(k):
        n, to = where_from(k)
        remote(stile.at[n], sbuf.at[me_e], sc_s, sc_r, (me_d, to)).start()

    others(NE, send_score)

    down_half(1)
    for n in range(2):
        at = pl.ds(64 * n, 64)
        half += [
            remote(g1.at[2, at], ra1.at[at], h_s.at[2 * n + 4], h_r.at[2 * n + 4], right),
            remote(
                g1.at[2, pl.ds(128 + 64 * n, 64)], rb1.at[at],
                h_s.at[2 * n + 5], h_r.at[2 * n + 5], left,
            ),
        ]
    for c in cuts:
        c.wait_recv()
    pair_copy.wait_recv()

    def pair_part(j):
        o = lax.rem(x + j, NX)
        col = pl.ds(pl.multiple_of(512 * o + 256 * core, 256), 256)

        def one(i, carry):
            at = pl.ds(pl.multiple_of(i * 512, 512), 512)
            out = mm(rt[:, :, :, col].reshape(256, 256), pair[:, at], TN)
            out = out + mm(pt[o].reshape(256, 256), ppair[:, at], TN)
            g1[j, :, at] = out.astype(BF16)
            return carry

        lax.fori_loop(0, 3, one, 0)

    pair_part(2)
    for c in half[4:8]:
        c.start()
    for b in range(4):
        at = slice(512 * b, 512 * b + 512)
        out = mm(gg[...], wg[at, :], NT) + mm(ug[...], wu[at, :], NT)
        rows = 8 * (b // 2)
        cut = slice(512 * (b % 2), 512 * (b % 2) + 512)
        bsend[:, rows : rows + 8, cut] = out.reshape(NE, 8, 512).astype(BF16)

    def send_back(k):
        n, to = where_from(k)
        remote(bsend.at[n], ret.at[me_e], ret_s, ret_r, (me_d, to)).start()

    pltpu.make_async_copy(bsend.at[where_from(0)[0]], ret.at[me_e], ret_r).start()
    lax.fori_loop(1, 6, lambda k, c: (send_back(k), c)[1], 0)
    pair_part(1)
    pair_part(3)
    pair_part(0)

    drain(sbuf, sc_r)
    eye32 = (iota((NE, 128), 0) == iota((NE, 128), 1)).astype(BF16)
    scores = mm(sbuf[...].reshape(NE, 128).astype(BF16), eye32, TN)
    grad3 = jnp.zeros((TOK, 128), F32)
    for slot in range(CAP):
        grad3 = grad3 + jnp.where(
            rank == slot, jnp.broadcast_to(scores[slot : slot + 1, :], (TOK, 128)), 0.0
        )
    g = NE * grad3 * dens[3]
    h3 = g - dens[3] * jnp.sum(g, axis=1, keepdims=True)
    atile[...] = jnp.sum(h3, axis=0, keepdims=True)
    plane(lambda e: atile, abuf.at[me_e], a_s, a_r)
    lax.fori_loop(6, 19, lambda k, c: (send_back(k), c)[1], 0)

    gates_hi = gates.astype(BF16).astype(F32)
    ex_i, ex_j = iota((128, 512), 0), iota((128, 512), 1)
    spread = ((ex_i < NE) & (ex_j // 16 == ex_i)).astype(BF16)
    wide = mm(
        jnp.concatenate([rank, gates_hi, gates - gates_hi], axis=0).astype(BF16), spread
    )
    k16 = lax.rem(iota((TOK, 512), 1), 16)
    rank_w = wide[0:TOK].astype(jnp.int32)
    parts = []
    for m in (rank_w == k16, rank_w == k16 - 8):
        parts += [jnp.where(m, wide[TOK : 2 * TOK], 0.0), jnp.where(m, wide[2 * TOK :], 0.0)]
    weights = jnp.concatenate(parts, axis=0).astype(BF16)

    for p in range(2):
        dens_h = db[p].reshape(2048, 128)
        g = mm(dens_h, dens_h, TN)
        gram[p] = mm(mm(fold, g * block, exact=True), fold, exact=True)

    drain(abuf, a_r)
    btile[...] = jnp.sum(abuf[...], axis=0)
    pltpu.make_async_copy(btile, bbuf.at[me_d], b_r).start()
    others(
        ND,
        lambda k: remote(
            btile, bbuf.at[me_d], b_s, b_r, (lax.rem(me_d + k, ND), me_e)
        ).start(),
    )
    for n in range(2):
        up, down = pl.ds(128 + 64 * n, 64), pl.ds(64 * n, 64)
        early += [
            remote(g1.at[1, up], rc1.at[up], n_s.at[2 * n + 4], n_r.at[2 * n + 4], right),
            remote(g1.at[3, down], rd1.at[down], n_s.at[2 * n + 5], n_r.at[2 * n + 5], left),
        ]
    for c in early[2:6]:
        c.start()

    drain(bbuf, b_r)
    v = jnp.broadcast_to(jnp.sum(bbuf[...], axis=0), (8, 128))
    first32 = lane8 < NE
    u = mm(jnp.where(first32, v / cols[16:24, :], 0.0), gram[1], exact=True)
    s = mm(jnp.where(first32, u / cols[8:16, :], 0.0), gram[0], exact=True)
    qv = quot[2] * v[0:1, :]
    h2 = h3 - qv + dens[2] * jnp.sum(qv, axis=1, keepdims=True)
    qu = quot[1] * u[0:1, :]
    h1 = h2 - qu + dens[1] * jnp.sum(qu, axis=1, keepdims=True)
    lgrad = (h1 - quot[0] * s[0:1, :]).astype(BF16)[:, :NE]
    router_t = mm(lgrad, tokens[...], TN)
    for p in range(NE):
        h, b = p % 2, p // 2
        rsend[p] = router_t[16 * h : 16 * h + 16, 128 * b : 128 * b + 128].astype(BF16)
    plane(lambda e: rsend.at[e], rrecv.at[me_e], rs_s, rs_r)
    lax.fori_loop(19, NE, lambda k, c: (send_back(k), c)[1], 0)
    router_in = mm(lgrad, rw[...])

    def add_rows(n, rows, terms, out):
        def one(i, c):
            at = pl.ds(pl.multiple_of(i * rows, rows), rows)
            out(at, functools.reduce(lambda a, b: a + b, [t(at).astype(F32) for t in terms]))
            return c

        lax.fori_loop(0, n // rows, one, 0)

    def put(ref, j, base):
        def f(at, value):
            ref[j, pl.ds(pl.multiple_of(at.start + base, 16), at.size), :] = value.astype(BF16)
        return f

    def take(ref, j, base):
        return lambda at: ref[j, pl.ds(pl.multiple_of(at.start + base, 16), at.size), :]

    for c in half:
        c.wait_recv()
    for h in range(2):
        add_rows(
            48, 48, [take(g2.at[h], 1, 0), lambda at, h=h: ra2[h, at, :]], put(g2.at[h], 1, 0)
        )
        add_rows(
            48, 48, [take(g2.at[h], 3, 48), lambda at, h=h: rb2[h, at, :]], put(g2.at[h], 3, 48)
        )
    add_rows(128, 32, [take(g1, 1, 0), lambda at: ra1[at, :]], put(g1, 1, 0))
    add_rows(128, 32, [take(g1, 3, 128), lambda at: rb1[at, :]], put(g1, 3, 128))
    late = []
    for h in range(2):
        top, low = pl.ds(0, 48), pl.ds(48, 48)
        late += [
            remote(g2.at[h, 1, top], rc2.at[h, top], m_s.at[2 * h], m_r.at[2 * h], right),
            remote(
                g2.at[h, 3, low], rd2.at[h, low], m_s.at[2 * h + 1], m_r.at[2 * h + 1], left
            ),
        ]
    late += [
        remote(g1.at[1, pl.ds(0, 128)], rc1.at[pl.ds(0, 128)], m_s.at[4], m_r.at[4], right),
        remote(g1.at[3, pl.ds(128, 128)], rd1.at[pl.ds(128, 128)], m_s.at[5], m_r.at[5], left),
    ]

    for c in late[0:2] + early[6:8]:
        c.start()
    drain(rrecv, rs_r)
    dsum[...] = jnp.sum(rrecv[...].astype(F32), axis=0).astype(BF16)
    pltpu.make_async_copy(dsum, drecv.at[me_d], d_r).start()
    others(
        ND,
        lambda k: remote(
            dsum, drecv.at[me_d], d_s, d_r, (lax.rem(me_d + k, ND), me_e)
        ).start(),
    )
    for c in late[2:6]:
        c.start()
    drain(drecv, d_r)
    fin[...] = jnp.sum(drecv[...].astype(F32), axis=0).astype(BF16)
    plane(lambda e: fin, router_out.at[me_e], o_s, o_r)

    drain(ret, ret_r)
    mixed = mm(weights, ret[...].reshape(512, 1024))
    gt_out[:, 0:1024] = (mixed[0:24] + mixed[24:48] + router_in[:, 0:1024]).astype(BF16)
    gt_out[:, 1024:2048] = (mixed[48:72] + mixed[72:96] + router_in[:, 1024:2048]).astype(BF16)

    for c in early + late:
        c.wait_recv()

    def store(ref):
        def f(at, value):
            ref[at, :] = value.astype(BF16)
        return f

    def store_half(h):
        def f(at, value):
            down_out[at, 1024 * h : 1024 * h + 1024] = value.astype(BF16)
        return f

    for h in range(2):
        add_rows(
            96, 48,
            [
                take(g2.at[h], 0, 0),
                lambda at, h=h: rc2[h, at, :],
                lambda at, h=h: rd2[h, at, :],
            ],
            store_half(h),
        )
    add_rows(
        256, 32, [take(g1, 0, 0), lambda at: rc1[at, :], lambda at: rd1[at, :]], store(pair_out)
    )
    drain(router_out, o_r)

    for c in t_dn[0] + t_dn[1] + t_up[0] + t_up[1] + g_dn[0] + g_dn[1] + g_up[0] + g_up[1] + ds_copies + y_copies + lg_copies + cuts + half + early + late:
        c.wait_send()
    for c in [logit_pair, pair_copy] + ht_copies:
        c.wait_send()
    drain(rk_in.at[pl.ds(0, 7)], rk_s)
    drain(pk_in.at[pl.ds(0, 7)], pk_s)
    drain(lall.at[0, pl.ds(0, NX - 1)], x_s)
    drain(ret.at[pl.ds(0, NE - 1)], ret_s)
    drain(sbuf.at[pl.ds(0, NE - 1)], sc_s)
    drain(abuf.at[pl.ds(0, NE - 1)], a_s)
    drain(bbuf.at[pl.ds(0, ND - 1)], b_s)
    drain(rrecv.at[pl.ds(0, NE - 1)], rs_s)
    drain(drecv.at[pl.ds(0, ND - 1)], d_s)
    drain(router_out.at[pl.ds(0, NE - 1)], o_s)


def moe(*args):
    dma = pltpu.SemaphoreType.DMA
    V = pltpu.VMEM
    hbm = pl.BlockSpec(memory_space=pltpu.HBM)
    return pl.pallas_call(
        moe_kernel,
        name="moe",
        out_shape=(
            jax.ShapeDtypeStruct((TOK, D), BF16),
            jax.ShapeDtypeStruct((256, 2 * FF), BF16),
            jax.ShapeDtypeStruct((96, D), BF16),
            jax.ShapeDtypeStruct((NE, 16, 128), BF16),
        ),
        in_specs=[hbm] * 7,
        out_specs=(VM,) * 4,
        scratch_shapes=[
            V((TOK, D), BF16), V((TOK, D), BF16), V((8, TOK), jnp.int32), V((NE, D), BF16),
            V((D, FF), BF16), V((D, FF), BF16), V((FF, D), BF16),
            V((8, 4, 1, 128), F32), V((8, 4, 1, 128), F32), V((4, 8, 1, 128), F32),
            V((8, 128), F32), V((8, 8, 128), F32),
            V((2, 4, 16, 1024), BF16), V((2, 2, 4, 16, 512), BF16),
            V((4, 2, 16, 1024), BF16), V((2, 4, 2, 16, 512), BF16),
            V((2, NX, NE, 8, 128), F32), V((2, 1024, 128), F32), V((2, 2, 1024, 128), BF16),
            V((24, 128), F32), V((2, 128, 128), F32), V((NE, 1, 128), F32),
            V((2, 8, TOK, 1024), BF16), V((2, 8, TOK, 1024), BF16),
            V((4, 4, 16, D), BF16), V((2, 4, 4, 16, 1024), BF16),
            V((4, 4, 16, D), BF16), V((4, 4, 16, D), BF16),
            V((4, 4, 4, 16, 256), BF16),
            V((256, FF), F32), V((256, FF), F32), V((256, FF), F32),
            V((FF, 256), BF16), V((FF, 256), BF16),
            V((256, D), BF16), V((256, D), BF16),
            V((256, FF), BF16), V((256, FF), BF16),
            V((256, 2 * FF), BF16), V((256, 2 * FF), BF16),
            V((4, 256, 2 * FF), BF16), V((2, 4, 96, 1024), BF16),
            V((128, 2 * FF), BF16), V((2, 48, 1024), BF16),
            V((128, 2 * FF), BF16), V((2, 48, 1024), BF16),
            V((256, 2 * FF), BF16), V((2, 96, 1024), BF16),
            V((256, 2 * FF), BF16), V((2, 96, 1024), BF16),
            V((NE, 16, 1024), BF16), V((NE, 16, 1024), BF16),
            V((NE, 1, 128), F32), V((NE, 1, 128), F32),
            V((1, 128), F32), V((NE, 1, 128), F32),
            V((1, 128), F32), V((ND, 1, 128), F32),
            V((NE, 16, 128), BF16), V((NE, 16, 128), BF16),
            V((16, 128), BF16), V((ND, 16, 128), BF16), V((16, 128), BF16),
            dma((4,)), dma((3,)),
            dma((2, 8)), dma((2, 8)), dma((2, 8)), dma((2, 8)),
            dma((4, 4)), dma((4, 4)), dma((2, 4, 4)), dma((2, 4, 4)),
            dma((2, 4)), dma((2, 4)), dma((2, 2, 4)), dma((2, 2, 4)),
            dma((8,)), dma((8,)),
            dma((8,)), dma((8,)), dma((8,)), dma((8,)), dma((6,)), dma((6,)),
            dma((3,)), dma((3,)), dma((3,)), dma, dma((3,)), dma,
        ]
        + [dma] * 22,
        compiler_params=pltpu.CompilerParams(
            collective_id=0, has_side_effects=True, vmem_limit_bytes=52 * 1024 * 1024
        ),
    )(*args)


def write_kernel(gt, pair, down, router, gt_o, router_o, gate_o, up_o, down_o):
    gt_o[...] = gt[...]
    gate_o[0] = pair[:, 0:FF]
    up_o[0] = pair[:, FF : 2 * FF]
    down_o[0] = down[...]
    for p in range(NE):
        h, b = p % 2, p // 2
        router_o[16 * h : 16 * h + 16, 128 * b : 128 * b + 128] = router[p].astype(F32)


def write(*args):
    return pl.pallas_call(
        write_kernel,
        name="write",
        out_shape=(
            jax.ShapeDtypeStruct((TOK, D), BF16),
            jax.ShapeDtypeStruct((NE, D), F32),
            jax.ShapeDtypeStruct((1, 256, FF), BF16),
            jax.ShapeDtypeStruct((1, 256, FF), BF16),
            jax.ShapeDtypeStruct((1, 96, D), BF16),
        ),
        in_specs=[VM] * 4,
        out_specs=(VM,) * 5,
        compiler_params=pltpu.CompilerParams(vmem_limit_bytes=16 * 1024 * 1024),
    )(*args)


def per_device(tokens, out_grad, expert_ids, router_weight, w_gate, w_up, w_down):
    gt, pair, down, router = moe(
        *[
            pltpu.with_memory_space_constraint(a, pltpu.HBM)
            for a in (tokens, out_grad, expert_ids.T, router_weight.T)
        ],
        w_gate, w_up, w_down
    )
    gt, router, gate, up, down = write(gt, pair, down, router)
    return gt, router.T, gate, up, down


def solution(mesh):
    in_specs = (
        P(("dp", "expert"), None), P(("dp", "expert"), None), P(("dp", "expert"), None), P(),
        P("expert", None, None), P("expert", None, None), P("expert", None, None),
    )
    out_specs = (
        P(("dp", "expert"), None), P(),
        P("expert", "dp", None), P("expert", "dp", None), P("expert", "dp", None),
    )
    return jax.shard_map(
        per_device, mesh=mesh, in_specs=in_specs, out_specs=out_specs, check_vma=False
    )
```

```python
import functools

import jax
import jax.numpy as jnp
from jax import lax
from jax.experimental import pallas as pl
from jax.experimental.pallas import tpu as pltpu
from jax.sharding import PartitionSpec as P

HI = lax.Precision.HIGHEST
F32 = jnp.float32
BF16 = jnp.bfloat16
NE = 32
ND = 8
NX = 4
TOK = 24
CAP = 8
D = 2048
FF = 768
VM = pl.BlockSpec(memory_space=pltpu.VMEM)
MESH = pl.DeviceIdType.MESH


def iota(shape, dim):
    return lax.broadcasted_iota(jnp.int32, shape, dim)


def remote(src, dst, send, recv, dev):
    return pltpu.make_async_remote_copy(
        src_ref=src, dst_ref=dst, send_sem=send, recv_sem=recv, device_id=dev, device_id_type=MESH
    )


def drain(ref, sem):
    pltpu.make_async_copy(ref, ref, sem).wait()


def place():
    me_d = lax.axis_index("dp")
    return me_d, lax.axis_index("expert"), me_d // 2, lax.rem(me_d, 2)


def others(n, body):
    lax.fori_loop(1, n, lambda k, c: (body(k), c)[1], 0)


def own_state(logits, cols):
    lane = iota((TOK, 128), 1)
    d = jnp.where(lane < NE, jnp.exp(logits), 0.0)
    ds, qs = [d], []
    for p in range(3):
        q = d / cols[p : p + 1, :]
        d = q / jnp.sum(q, axis=1, keepdims=True)
        qs.append(q)
        ds.append(d)
    return ds, qs


NT = (((1,), (1,)), ((), ()))
TN = (((0,), (0,)), ((), ()))


def mm(a, b, dims=None, exact=False):
    dims = dims or (((1,), (0,)), ((), ()))
    return lax.dot_general(
        a, b, dims, precision=HI if exact else None, preferred_element_type=F32
    )


def moe_kernel(
    tokens_hbm, grads_hbm, ids_hbm, rw_hbm, wg_hbm, wu_hbm, wd_hbm,
    gt_out, pair_out, down_out, router_out,
    tokens, grads, ids, rw, wg, wu, wd, rk_out, rk_in, rk_col, pk_out, pk_in, et, eg, qt, qg,
    lall, dd, db, cols, gram, gcol,
    zt, zg, yt, yg, rt, rg, pt, hid, act, dsl, ht, pht, ds, pds, gg, ug, pair, ppair,
    g1, g2, ra1, ra2, rb1, rb2, rc1, rc2, rd1, rd2,
    bsend, ret, stile, sbuf, atile, abuf, btile, bbuf, rsend, rrecv, dsum, drecv, fin,
    in_sem, w_sem, zs_t, zr_t, zs_g, zr_g, ys_t, yr_t, ys_g, yr_g, es_t, er_t, es_g, er_g, q_s, q_r, h_s, h_r, n_s, n_r, m_s, m_r,
    ht_s, ht_r, lg_s, lg_r, rc_s, rc_r, rk_s, rk_r, pk_s, pk_r, x_s, x_r, p_s, p_r, ret_s, ret_r, sc_s, sc_r,
    a_s, a_r, b_s, b_r, rs_s, rs_r, d_s, d_r, o_s, o_r,
):
    me_d, me_e, x, core = place()
    y, z = me_e // 8, lax.rem(me_e, 8)
    inputs = [
        pltpu.make_async_copy(a, b, in_sem.at[n])
        for n, (a, b) in enumerate(
            ((tokens_hbm, tokens), (grads_hbm, grads), (ids_hbm, ids), (rw_hbm, rw))
        )
    ]
    for c in inputs:
        c.start()
    barrier = pltpu.get_barrier_semaphore()
    others(
        NE,
        lambda k: pl.semaphore_signal(
            barrier, inc=1, device_id=(me_d, lax.rem(me_e + k, NE)), device_id_type=MESH
        ),
    )
    others(
        ND,
        lambda k: pl.semaphore_signal(
            barrier, inc=1, device_id=(lax.rem(me_d + k, ND), me_e), device_id_type=MESH
        ),
    )
    loads = [
        pltpu.make_async_copy(a.at[0], b, w_sem.at[n])
        for n, (a, b) in enumerate(((wg_hbm, wg), (wu_hbm, wu), (wd_hbm, wd)))
    ]
    for c in loads:
        c.start()
    for c in inputs:
        c.wait()
    partner = (x * 2 + 1 - core, me_e)
    right = (lax.rem(x + 1, NX) * 2 + core, me_e)
    left = (lax.rem(x + 3, NX) * 2 + core, me_e)
    z_up = (me_d, y * 8 + lax.rem(z + 1, 8))
    z_down = (me_d, y * 8 + lax.rem(z + 7, 8))

    lane8, sub8 = iota((8, 128), 1), iota((8, 128), 0)
    logits = jnp.concatenate(
        [mm(tokens[...], rw[...], NT), jnp.zeros((TOK, 96), F32)], axis=1
    )
    packed = (
        logits[0:8] + pltpu.roll(logits[8:16], 32, 1) + pltpu.roll(logits[16:24], 64, 1)
    )
    picked_t = jnp.zeros((128, TOK), F32)
    for k in range(8):
        picked_t = picked_t + (ids[k : k + 1, :] == iota((128, TOK), 0)).astype(F32)
    picked_t = picked_t.astype(BF16)
    row_t, col_t = iota((TOK, TOK), 0), iota((TOK, TOK), 1)
    picked = mm((row_t == col_t).astype(BF16), picked_t, NT)
    rank = jnp.where(picked > 0, mm((row_t > col_t).astype(BF16), picked_t, NT), -64.0)
    rank_pad = jnp.concatenate([rank, jnp.full((104, 128), -64.0, F32)], axis=0).astype(BF16)
    pi, pj = iota((32, 128), 0), iota((32, 128), 1)
    place_rows = (pj == lax.rem(pi, 4) * 8 + pi // 4).astype(BF16)
    rk_out[...] = mm(place_rows, rank_pad, NT).reshape(8, 4, 1, 128)
    pk_out[...] = packed

    pl.semaphore_wait(barrier, NE - 1 + ND - 1)

    def z_send(k):
        to = lax.rem(z + k, 8)
        dev = (me_d, y * 8 + to)
        remote(rk_out.at[to], rk_in.at[z], rk_s, rk_r, dev).start()
        remote(pk_out, pk_in.at[z], pk_s, pk_r, dev).start()

    pltpu.make_async_copy(rk_out.at[z], rk_in.at[z], rk_r).start()
    pltpu.make_async_copy(pk_out, pk_in.at[z], pk_r).start()
    others(8, z_send)

    def z_copy(own, buf, ss, rs, k, sign):
        at = lambda n: (8 + sign * n) % 8
        return remote(
            own if k == 1 else buf.at[at(k - 1)], buf.at[at(k)], ss.at[at(k)], rs.at[at(k)],
            z_down if sign > 0 else z_up,
        )

    def pipes(ref, buf, ss, rs, down, up):
        dn_list, up_list = [], []
        for h in range(2):
            own = ref.at[:, pl.ds(1024 * h, 1024)]
            args = (own, buf.at[h], ss.at[h], rs.at[h])
            dn_list.append([z_copy(*args, k, -1) for k in range(1, down + 1)])
            up_list.append([z_copy(*args, k, 1) for k in range(1, up + 1)])
        return dn_list, up_list

    t_dn, t_up = pipes(tokens, zt, zs_t, zr_t, 4, 3)
    g_dn, g_up = pipes(grads, zg, zs_g, zr_g, 3, 4)
    for pipe in (t_dn[0], t_up[0], t_dn[1], t_up[1], g_dn[0], g_up[0]):
        pipe[0].start()

    def hot(ref, at, yy):
        row = ref[at, yy]
        return (jnp.broadcast_to(row, (8, 128)) == sub8.astype(F32)).astype(F32)

    def choose(at, half):
        none = jnp.zeros((8, 128), F32)
        parts = []
        for yy in range(4):
            one = hot(rk_in, at, yy)
            parts += [one, none] if half == 0 else [none, one]
        return jnp.concatenate(parts, axis=0).astype(BF16)[:, :TOK]

    y_copies = []

    def y_send(src, dst, ss, rs, j):
        for m in range(1, 4):
            to = lax.rem(y + m, 4)
            c = remote(src(to), dst, ss.at[j, m], rs.at[j, m], (me_d, to * 8 + z))
            c.start()
            y_copies.append(c)
        pltpu.make_async_copy(src(y), dst, rs.at[j, 0]).start()

    def y_pair(j, buf, send_buf, dst, ss, rs):
        out = mm(choose(lax.rem(z + 8 - j, 8), 0), buf(8 - j))
        out = out + mm(choose(lax.rem(z + j, 8), 1), buf(j))
        send_buf[j] = out.astype(BF16).reshape(4, 16, out.shape[1])
        y_send(lambda to: send_buf.at[j, to], dst, ss, rs, j)

    def y_single(n, block, ref, at, send_buf, dst, ss, rs):
        pick = jnp.concatenate([hot(ref, at, yy) for yy in range(4)], axis=0)
        out = mm(pick.astype(BF16)[:, :TOK], block)
        w = out.shape[1] // 2
        for yy in range(4):
            rows = out[8 * yy : 8 * yy + 8]
            send_buf[n, yy] = jnp.concatenate([rows[:, :w], rows[:, w:]], axis=0).astype(BF16)
        y_send(lambda to: send_buf.at[n, to], dst, ss, rs, n)

    def y_wait(view, rs, one_buf, one_rs, fill):
        for m in range(4):
            for j in range(1, 4):
                drain(view, rs.at[j, m])
            for n in range(2):
                drain(one_buf.at[0, 0], one_rs.at[n, m])
        for yy in range(4):
            parts = []
            for n in range(2):
                a = one_buf[yy, n].astype(F32)
                parts.append(jnp.concatenate([a[0:8], a[8:16]], axis=1))
            fill(yy, jnp.concatenate(parts, axis=0).astype(BF16))

    def arrive(down, up, k):
        if k < len(down):
            down[k].wait_recv()
            if k + 1 < len(down):
                down[k + 1].start()
        if k < len(up):
            up[k].wait_recv()
            if k + 1 < len(up):
                up[k + 1].start()

    def cut(h):
        return pl.ds(1024 * h, 1024)

    def t_block(n):
        return jnp.concatenate([zt[0, n], zt[1, n]], axis=1)

    def t_pair(j):
        y_pair(j, t_block, yt, rt.at[y, j], ys_t, yr_t)

    def t_single(n, block, ref, at):
        y_single(n, block, ref, at, et, qt.at[y, n], es_t, er_t)

    def g_pair(h, j):
        y_pair(j, lambda n: zg[h, n], yg.at[h], rg.at[y, j, :, cut(h)], ys_g.at[h], yr_g.at[h])

    def g_single(h, n, block, ref, at):
        y_single(n, block, ref, at, eg.at[h], qg.at[h, y, n], es_g.at[h], er_g.at[h])

    t_single(0, tokens[...], rk_out, z)
    g_single(0, 0, grads[:, 0:1024], rk_out, z)

    drain(rk_in, rk_r)
    drain(pk_in, pk_r)
    own_rows = lall.at[core, x, pl.ds(pl.multiple_of(y * 8, 8), 8)]
    pltpu.make_async_copy(pk_in, own_rows, lg_r).start()
    pltpu.make_async_copy(rk_in.at[:, y], rk_col.at[y], rc_r).start()
    lg_copies = []
    for m in range(1, 4):
        to = lax.rem(y + m, 4)
        dev = (me_d, to * 8 + z)
        lg_copies.append(remote(pk_in, own_rows, lg_s.at[m - 1], lg_r, dev))
        lg_copies.append(remote(rk_in.at[:, to], rk_col.at[y], rc_s.at[m - 1], rc_r, dev))
    for c in lg_copies:
        c.start()

    far = lax.rem(z + 4, 8)
    def arrive_t(k):
        for h in range(2):
            arrive(t_dn[h], t_up[h], k)

    def arrive_g(h, k):
        arrive(g_dn[h], g_up[h], k)

    arrive_t(0)
    t_pair(1)
    arrive_g(0, 0)
    g_dn[1][0].start()
    g_up[1][0].start()
    g_pair(0, 1)
    drain(lall.at[core, x], lg_r)
    others(
        NX,
        lambda k: remote(
            lall.at[core, x], lall.at[core, x], x_s, x_r, (lax.rem(x + k, NX) * 2 + core, me_e)
        ).start(),
    )
    arrive_t(1)
    t_pair(2)
    arrive_g(0, 1)
    arrive_g(1, 0)
    g_pair(0, 2)
    arrive_t(2)
    t_pair(3)
    arrive_g(0, 2)
    arrive_g(1, 1)
    arrive_t(3)
    t_single(1, t_block(4), rk_in, far)
    g_pair(0, 3)
    drain(lall.at[core, pl.ds(0, NX - 1)], x_r)
    logit_pair = remote(lall.at[core], lall.at[core], p_s, p_r, partner)
    logit_pair.start()
    arrive_g(0, 3)
    g_single(0, 1, zg[0, 4], rk_in, far)
    arrive_g(1, 2)
    g_single(1, 0, grads[:, 1024:2048], rk_out, z)
    g_pair(1, 1)
    g_pair(1, 2)
    g_pair(1, 3)
    drain(lall.at[1 - core], p_r)

    valid = iota((1024, 128), 1) < 96
    li, lj = iota((128, 128), 0), iota((128, 128), 1)
    fold = (lax.rem(li, 32) == lax.rem(lj, 32)).astype(F32)
    block = (li // 32 == lj // 32).astype(F32)
    block_h = block.astype(BF16)

    def rows_of(a):
        return jnp.sum(jnp.sum(a.reshape(8, 16, 8, 128), axis=1), axis=0)

    def total(acc):
        one = jnp.broadcast_to(jnp.sum(acc, axis=0, keepdims=True), (8, 128))
        return mm(one, fold, exact=True)

    acc = jnp.zeros((8, 128), F32)
    for i in range(2):
        d0 = jnp.where(valid, jnp.exp(lall[i].reshape(1024, 128)), 0.0)
        dd[i] = d0
        acc = acc + rows_of(d0)
    pad = jnp.where(iota((1, 128), 1) < 96, 0.0, 1.0)
    c = total(acc)
    cols[0:8, :] = c
    for p in range(2):
        acc = jnp.zeros((8, 128), F32)
        inverse = 1.0 / c[0:1, :]
        for i in range(2):
            q = dd[i] * inverse
            q_hi = q.astype(BF16)
            q_lo = (q - q_hi.astype(F32)).astype(BF16)
            d = q / (mm(q_hi, block_h) + mm(q_lo, block_h) + pad)
            dd[i] = d
            db[p, i] = d.astype(BF16)
            acc = acc + rows_of(d)
        c = total(acc)
        cols[8 * p + 8 : 8 * p + 16, :] = c

    c3 = jnp.concatenate([cols[0:1, :], cols[8:9, :], cols[16:17, :]], axis=0)
    dens, quot = own_state(logits, c3)
    gates = NE * dens[3]

    lane256, row256 = iota((256, 128), 1), iota((256, 128), 0)
    q = dd[core, pl.ds(pl.multiple_of(x * 256, 256), 256), :] / c3[2:3, :]
    q_hi = q.astype(BF16)
    q_lo = (q - q_hi.astype(F32)).astype(BF16)
    group = NE * q / (mm(q_hi, block_h) + mm(q_lo, block_h) + pad)
    turned = jnp.zeros((256, 128), F32)
    for n in range(3):
        one = jnp.sum(jnp.where(lane256 == 32 * n + me_e, group, 0.0), axis=1, keepdims=True)
        turned = turned + jnp.where(lane256 == 8 * n + lax.rem(row256, 8), one, 0.0)
    gcol[...] = jnp.sum(turned.reshape(NE, 8, 128), axis=1).reshape(NE, 1, 128)
    drain(rk_col, rc_r)
    tiles = []
    for yy in range(4):
        for off in (0, 4, 7, 1, 6, 2, 5, 3):
            zz = lax.rem(z + off, 8)
            here = jnp.broadcast_to(rk_col[yy, zz], (8, 128)) == sub8.astype(F32)
            tiles.append(jnp.where(here, jnp.broadcast_to(gcol[yy * 8 + zz], (8, 128)), 0.0))
    gate = jnp.sum(jnp.concatenate(tiles, axis=0), axis=1, keepdims=True)
    gate = gate.astype(BF16).astype(F32)
    arrive_g(1, 3)
    g_single(1, 1, zg[1, 4], rk_in, far)

    def plane(src, dst, send, recv):
        pltpu.make_async_copy(src(me_e), dst, recv).start()

        def go(k):
            to = lax.rem(me_e + k, NE)
            remote(src(to), dst, send, recv, (me_d, to)).start()

        others(NE, go)

    for c in loads:
        c.wait()

    def fill_t(yy, value):
        rt[yy, 0] = value

    y_wait(rt.at[0, 0], yr_t, qt, er_t, fill_t)
    cuts = []
    for o in range(4):
        at = pl.ds(pl.multiple_of(512 * o + 256 * (1 - core), 256), 256)
        cuts.append(
            remote(rt.at[:, :, :, at], pt.at[o], q_s.at[o], q_r.at[o], partner)
        )

    def forward(i, carry):
        at = pl.ds(pl.multiple_of(i * 256, 256), 256)
        rows = rt[...].reshape(256, D)
        gate_pre = mm(rows, wg[:, at])
        up_pre = mm(rows, wu[:, at])
        sg = jax.nn.sigmoid(gate_pre)
        a = gate_pre * sg
        h = a * up_pre
        hid[:, at] = h
        act[:, at] = a
        dsl[:, at] = up_pre * sg * (1.0 + gate_pre * (1.0 - sg))
        ht[at, :] = h.T.astype(BF16)
        return carry

    ht_copies = [
        remote(ht.at[r], pht.at[r], ht_s.at[n], ht_r.at[n], partner)
        for n, r in enumerate(pl.ds(256 * i, 256) for i in range(3))
    ]

    def where_from(k):
        o = lax.rem(k, 8)
        j, h = o // 2, lax.rem(o, 2)
        yy = lax.rem(y + k // 8, 4)
        zz = lax.rem(z + h * (j + 4 * ((4 - j) // 4)) + (1 - h) * (8 - j), 8)
        return yy * 8 + o, yy * 8 + zz

    def fill_g(h):
        def f(yy, value):
            rg[yy, 0, :, 1024 * h : 1024 * h + 1024] = value
        return f

    ds_copies = []

    def scaled(h):
        y_wait(rg.at[0, 0, :, cut(h)], yr_g.at[h], qg.at[h], er_g.at[h], fill_g(h))
        for b in range(2 * h, 2 * h + 2):
            at = slice(512 * b, 512 * b + 512)
            ds[:, at] = (gate * rg[:, :, :, at].reshape(256, 512).astype(F32)).astype(BF16)
        c = remote(ds.at[:, cut(h)], pds.at[:, cut(h)], q_s.at[5 + h], q_r.at[5 + h], partner)
        c.start()
        ds_copies.append(c)

    def my_rows(ref, j):
        o = lax.rem(x + j, NX)
        return ref[pl.ds(pl.multiple_of(192 * o + 96 * core, 32), 96), :]

    half, early = [], []

    def down_half(h):
        ds_copies[h].wait_recv()

        def rows(js):
            def one(i, carry):
                at = pl.ds(pl.multiple_of(1024 * h + i * 512, 512), 512)
                to = pl.ds(pl.multiple_of(i * 512, 512), 512)
                mine = jnp.concatenate([my_rows(ht, j) for j in js], axis=0)
                theirs = jnp.concatenate([my_rows(pht, j) for j in js], axis=0)
                out = mm(mine, ds[:, at]) + mm(theirs, pds[:, at])
                for n, j in enumerate(js):
                    g2[h, j, :, to] = out[96 * n : 96 * n + 96].astype(BF16)
                return carry

            lax.fori_loop(0, 2, one, 0)

        top, low = pl.ds(0, 48), pl.ds(48, 48)
        n = 2 * h
        half.append(remote(g2.at[h, 2, top], ra2.at[h], h_s.at[n], h_r.at[n], right))
        half.append(remote(g2.at[h, 2, low], rb2.at[h], h_s.at[n + 1], h_r.at[n + 1], left))
        early.append(
            remote(g2.at[h, 1, low], rc2.at[h, low], n_s.at[n], n_r.at[n], right)
        )
        early.append(
            remote(g2.at[h, 3, top], rd2.at[h, top], n_s.at[n + 1], n_r.at[n + 1], left)
        )
        rows((2,))
        half[-2].start()
        half[-1].start()
        rows((1, 3, 0))

    for n in range(3):
        lax.fori_loop(n, n + 1, forward, 0)
        ht_copies[n].start()
        if n == 0:
            scaled(0)
            for c in cuts:
                c.start()
    for c in ht_copies:
        c.wait_recv()
    down_half(0)
    early[0].start()
    early[1].start()
    scaled(1)

    def backward(i, total_score):
        at = pl.ds(pl.multiple_of(i * 256, 256), 256)
        at_up = pl.ds(pl.multiple_of(i * 256 + FF, 256), 256)
        h = mm(rg[...].reshape(256, D), wd[at, :], NT)
        a = (h * dsl[:, at]).astype(BF16)
        b = (h * act[:, at]).astype(BF16)
        gg[:, at] = a
        ug[:, at] = b
        pair[:, at] = (gate * a.astype(F32)).astype(BF16)
        pair[:, at_up] = (gate * b.astype(F32)).astype(BF16)
        return total_score + jnp.sum(h * hid[:, at], axis=1, keepdims=True)

    score = lax.fori_loop(0, 3, backward, jnp.zeros((256, 1), F32))
    pair_copy = remote(pair, ppair, q_s.at[7], q_r.at[7], partner)
    pair_copy.start()
    spread8 = jnp.broadcast_to(score.astype(BF16).astype(F32), (256, 128)).reshape(NE, 8, 128)
    diag = iota((NE, 8, 128), 1) == iota((NE, 8, 128), 2)
    stile[...] = jnp.sum(jnp.where(diag, spread8, 0.0), axis=1).reshape(NE, 1, 128)
    pltpu.make_async_copy(stile.at[where_from(0)[0]], sbuf.at[me_e], sc_r).start()

    def send_score(k):
        n, to = where_from(k)
        remote(stile.at[n], sbuf.at[me_e], sc_s, sc_r, (me_d, to)).start()

    others(NE, send_score)

    down_half(1)
    for n in range(2):
        at = pl.ds(64 * n, 64)
        half += [
            remote(g1.at[2, at], ra1.at[at], h_s.at[2 * n + 4], h_r.at[2 * n + 4], right),
            remote(
                g1.at[2, pl.ds(128 + 64 * n, 64)], rb1.at[at],
                h_s.at[2 * n + 5], h_r.at[2 * n + 5], left,
            ),
        ]
    for c in cuts:
        c.wait_recv()
    pair_copy.wait_recv()

    def pair_part(j):
        o = lax.rem(x + j, NX)
        col = pl.ds(pl.multiple_of(512 * o + 256 * core, 256), 256)

        def one(i, carry):
            at = pl.ds(pl.multiple_of(i * 512, 512), 512)
            out = mm(rt[:, :, :, col].reshape(256, 256), pair[:, at], TN)
            out = out + mm(pt[o].reshape(256, 256), ppair[:, at], TN)
            g1[j, :, at] = out.astype(BF16)
            return carry

        lax.fori_loop(0, 3, one, 0)

    pair_part(2)
    for c in half[4:8] + early[2:4]:
        c.start()
    for b in range(4):
        at = slice(512 * b, 512 * b + 512)
        out = mm(gg[...], wg[at, :], NT) + mm(ug[...], wu[at, :], NT)
        rows = 8 * (b // 2)
        cut = slice(512 * (b % 2), 512 * (b % 2) + 512)
        bsend[:, rows : rows + 8, cut] = out.reshape(NE, 8, 512).astype(BF16)

    def send_back(k):
        n, to = where_from(k)
        remote(bsend.at[n], ret.at[me_e], ret_s, ret_r, (me_d, to)).start()

    pltpu.make_async_copy(bsend.at[where_from(0)[0]], ret.at[me_e], ret_r).start()
    lax.fori_loop(1, 6, lambda k, c: (send_back(k), c)[1], 0)
    pair_part(1)
    pair_part(3)
    pair_part(0)

    drain(sbuf, sc_r)
    eye32 = (iota((NE, 128), 0) == iota((NE, 128), 1)).astype(BF16)
    scores = mm(sbuf[...].reshape(NE, 128).astype(BF16), eye32, TN)
    grad3 = jnp.zeros((TOK, 128), F32)
    for slot in range(CAP):
        grad3 = grad3 + jnp.where(
            rank == slot, jnp.broadcast_to(scores[slot : slot + 1, :], (TOK, 128)), 0.0
        )
    g = NE * grad3 * dens[3]
    h3 = g - dens[3] * jnp.sum(g, axis=1, keepdims=True)
    atile[...] = jnp.sum(h3, axis=0, keepdims=True)
    plane(lambda e: atile, abuf.at[me_e], a_s, a_r)
    lax.fori_loop(6, 19, lambda k, c: (send_back(k), c)[1], 0)

    gates_hi = gates.astype(BF16).astype(F32)
    ex_i, ex_j = iota((128, 512), 0), iota((128, 512), 1)
    spread = ((ex_i < NE) & (ex_j // 16 == ex_i)).astype(BF16)
    wide = mm(
        jnp.concatenate([rank, gates_hi, gates - gates_hi], axis=0).astype(BF16), spread
    )
    k16 = lax.rem(iota((TOK, 512), 1), 16)
    rank_w = wide[0:TOK].astype(jnp.int32)
    parts = []
    for m in (rank_w == k16, rank_w == k16 - 8):
        parts += [jnp.where(m, wide[TOK : 2 * TOK], 0.0), jnp.where(m, wide[2 * TOK :], 0.0)]
    weights = jnp.concatenate(parts, axis=0).astype(BF16)

    for p in range(2):
        dens_h = db[p].reshape(2048, 128)
        g = mm(dens_h, dens_h, TN)
        gram[p] = mm(mm(fold, g * block, exact=True), fold, exact=True)

    drain(abuf, a_r)
    btile[...] = jnp.sum(abuf[...], axis=0)
    pltpu.make_async_copy(btile, bbuf.at[me_d], b_r).start()
    others(
        ND,
        lambda k: remote(
            btile, bbuf.at[me_d], b_s, b_r, (lax.rem(me_d + k, ND), me_e)
        ).start(),
    )
    for n in range(2):
        up, down = pl.ds(128 + 64 * n, 64), pl.ds(64 * n, 64)
        early += [
            remote(g1.at[1, up], rc1.at[up], n_s.at[2 * n + 4], n_r.at[2 * n + 4], right),
            remote(g1.at[3, down], rd1.at[down], n_s.at[2 * n + 5], n_r.at[2 * n + 5], left),
        ]
    for c in early[4:8]:
        c.start()

    drain(bbuf, b_r)
    v = jnp.broadcast_to(jnp.sum(bbuf[...], axis=0), (8, 128))
    first32 = lane8 < NE
    u = mm(jnp.where(first32, v / cols[16:24, :], 0.0), gram[1], exact=True)
    s = mm(jnp.where(first32, u / cols[8:16, :], 0.0), gram[0], exact=True)
    qv = quot[2] * v[0:1, :]
    h2 = h3 - qv + dens[2] * jnp.sum(qv, axis=1, keepdims=True)
    qu = quot[1] * u[0:1, :]
    h1 = h2 - qu + dens[1] * jnp.sum(qu, axis=1, keepdims=True)
    lgrad = (h1 - quot[0] * s[0:1, :]).astype(BF16)[:, :NE]
    router_t = mm(lgrad, tokens[...], TN)
    for p in range(NE):
        h, b = p % 2, p // 2
        rsend[p] = router_t[16 * h : 16 * h + 16, 128 * b : 128 * b + 128].astype(BF16)
    plane(lambda e: rsend.at[e], rrecv.at[me_e], rs_s, rs_r)
    lax.fori_loop(19, NE, lambda k, c: (send_back(k), c)[1], 0)
    router_in = mm(lgrad, rw[...])

    def add_rows(n, rows, terms, out):
        def one(i, c):
            at = pl.ds(pl.multiple_of(i * rows, rows), rows)
            out(at, functools.reduce(lambda a, b: a + b, [t(at).astype(F32) for t in terms]))
            return c

        lax.fori_loop(0, n // rows, one, 0)

    def put(ref, j, base):
        def f(at, value):
            ref[j, pl.ds(pl.multiple_of(at.start + base, 16), at.size), :] = value.astype(BF16)
        return f

    def take(ref, j, base):
        return lambda at: ref[j, pl.ds(pl.multiple_of(at.start + base, 16), at.size), :]

    for c in half:
        c.wait_recv()
    for h in range(2):
        add_rows(
            48, 48, [take(g2.at[h], 1, 0), lambda at, h=h: ra2[h, at, :]], put(g2.at[h], 1, 0)
        )
        add_rows(
            48, 48, [take(g2.at[h], 3, 48), lambda at, h=h: rb2[h, at, :]], put(g2.at[h], 3, 48)
        )
    add_rows(128, 32, [take(g1, 1, 0), lambda at: ra1[at, :]], put(g1, 1, 0))
    add_rows(128, 32, [take(g1, 3, 128), lambda at: rb1[at, :]], put(g1, 3, 128))
    late = []
    for h in range(2):
        top, low = pl.ds(0, 48), pl.ds(48, 48)
        late += [
            remote(g2.at[h, 1, top], rc2.at[h, top], m_s.at[2 * h], m_r.at[2 * h], right),
            remote(
                g2.at[h, 3, low], rd2.at[h, low], m_s.at[2 * h + 1], m_r.at[2 * h + 1], left
            ),
        ]
    late += [
        remote(g1.at[1, pl.ds(0, 128)], rc1.at[pl.ds(0, 128)], m_s.at[4], m_r.at[4], right),
        remote(g1.at[3, pl.ds(128, 128)], rd1.at[pl.ds(128, 128)], m_s.at[5], m_r.at[5], left),
    ]

    for c in late[0:2]:
        c.start()
    drain(rrecv, rs_r)
    dsum[...] = jnp.sum(rrecv[...].astype(F32), axis=0).astype(BF16)
    pltpu.make_async_copy(dsum, drecv.at[me_d], d_r).start()
    others(
        ND,
        lambda k: remote(
            dsum, drecv.at[me_d], d_s, d_r, (lax.rem(me_d + k, ND), me_e)
        ).start(),
    )
    for c in late[2:6]:
        c.start()
    drain(drecv, d_r)
    fin[...] = jnp.sum(drecv[...].astype(F32), axis=0).astype(BF16)
    plane(lambda e: fin, router_out.at[me_e], o_s, o_r)

    drain(ret, ret_r)
    mixed = mm(weights, ret[...].reshape(512, 1024))
    gt_out[:, 0:1024] = (mixed[0:24] + mixed[24:48] + router_in[:, 0:1024]).astype(BF16)
    gt_out[:, 1024:2048] = (mixed[48:72] + mixed[72:96] + router_in[:, 1024:2048]).astype(BF16)

    for c in early + late:
        c.wait_recv()

    def store(ref):
        def f(at, value):
            ref[at, :] = value.astype(BF16)
        return f

    def store_half(h):
        def f(at, value):
            down_out[at, 1024 * h : 1024 * h + 1024] = value.astype(BF16)
        return f

    for h in range(2):
        add_rows(
            96, 48,
            [
                take(g2.at[h], 0, 0),
                lambda at, h=h: rc2[h, at, :],
                lambda at, h=h: rd2[h, at, :],
            ],
            store_half(h),
        )
    add_rows(
        256, 32, [take(g1, 0, 0), lambda at: rc1[at, :], lambda at: rd1[at, :]], store(pair_out)
    )
    drain(router_out, o_r)

    for c in t_dn[0] + t_dn[1] + t_up[0] + t_up[1] + g_dn[0] + g_dn[1] + g_up[0] + g_up[1] + ds_copies + y_copies + lg_copies + cuts + half + early + late:
        c.wait_send()
    for c in [logit_pair, pair_copy] + ht_copies:
        c.wait_send()
    drain(rk_in.at[pl.ds(0, 7)], rk_s)
    drain(pk_in.at[pl.ds(0, 7)], pk_s)
    drain(lall.at[0, pl.ds(0, NX - 1)], x_s)
    drain(ret.at[pl.ds(0, NE - 1)], ret_s)
    drain(sbuf.at[pl.ds(0, NE - 1)], sc_s)
    drain(abuf.at[pl.ds(0, NE - 1)], a_s)
    drain(bbuf.at[pl.ds(0, ND - 1)], b_s)
    drain(rrecv.at[pl.ds(0, NE - 1)], rs_s)
    drain(drecv.at[pl.ds(0, ND - 1)], d_s)
    drain(router_out.at[pl.ds(0, NE - 1)], o_s)


def moe(*args):
    dma = pltpu.SemaphoreType.DMA
    V = pltpu.VMEM
    hbm = pl.BlockSpec(memory_space=pltpu.HBM)
    return pl.pallas_call(
        moe_kernel,
        name="moe",
        out_shape=(
            jax.ShapeDtypeStruct((TOK, D), BF16),
            jax.ShapeDtypeStruct((256, 2 * FF), BF16),
            jax.ShapeDtypeStruct((96, D), BF16),
            jax.ShapeDtypeStruct((NE, 16, 128), BF16),
        ),
        in_specs=[hbm] * 7,
        out_specs=(VM,) * 4,
        scratch_shapes=[
            V((TOK, D), BF16), V((TOK, D), BF16), V((8, TOK), jnp.int32), V((NE, D), BF16),
            V((D, FF), BF16), V((D, FF), BF16), V((FF, D), BF16),
            V((8, 4, 1, 128), F32), V((8, 4, 1, 128), F32), V((4, 8, 1, 128), F32),
            V((8, 128), F32), V((8, 8, 128), F32),
            V((2, 4, 16, 1024), BF16), V((2, 2, 4, 16, 512), BF16),
            V((4, 2, 16, 1024), BF16), V((2, 4, 2, 16, 512), BF16),
            V((2, NX, NE, 8, 128), F32), V((2, 1024, 128), F32), V((2, 2, 1024, 128), BF16),
            V((24, 128), F32), V((2, 128, 128), F32), V((NE, 1, 128), F32),
            V((2, 8, TOK, 1024), BF16), V((2, 8, TOK, 1024), BF16),
            V((4, 4, 16, D), BF16), V((2, 4, 4, 16, 1024), BF16),
            V((4, 4, 16, D), BF16), V((4, 4, 16, D), BF16),
            V((4, 4, 4, 16, 256), BF16),
            V((256, FF), F32), V((256, FF), F32), V((256, FF), F32),
            V((FF, 256), BF16), V((FF, 256), BF16),
            V((256, D), BF16), V((256, D), BF16),
            V((256, FF), BF16), V((256, FF), BF16),
            V((256, 2 * FF), BF16), V((256, 2 * FF), BF16),
            V((4, 256, 2 * FF), BF16), V((2, 4, 96, 1024), BF16),
            V((128, 2 * FF), BF16), V((2, 48, 1024), BF16),
            V((128, 2 * FF), BF16), V((2, 48, 1024), BF16),
            V((256, 2 * FF), BF16), V((2, 96, 1024), BF16),
            V((256, 2 * FF), BF16), V((2, 96, 1024), BF16),
            V((NE, 16, 1024), BF16), V((NE, 16, 1024), BF16),
            V((NE, 1, 128), F32), V((NE, 1, 128), F32),
            V((1, 128), F32), V((NE, 1, 128), F32),
            V((1, 128), F32), V((ND, 1, 128), F32),
            V((NE, 16, 128), BF16), V((NE, 16, 128), BF16),
            V((16, 128), BF16), V((ND, 16, 128), BF16), V((16, 128), BF16),
            dma((4,)), dma((3,)),
            dma((2, 8)), dma((2, 8)), dma((2, 8)), dma((2, 8)),
            dma((4, 4)), dma((4, 4)), dma((2, 4, 4)), dma((2, 4, 4)),
            dma((2, 4)), dma((2, 4)), dma((2, 2, 4)), dma((2, 2, 4)),
            dma((8,)), dma((8,)),
            dma((8,)), dma((8,)), dma((8,)), dma((8,)), dma((6,)), dma((6,)),
            dma((3,)), dma((3,)), dma((3,)), dma, dma((3,)), dma,
        ]
        + [dma] * 22,
        compiler_params=pltpu.CompilerParams(
            collective_id=0, has_side_effects=True, vmem_limit_bytes=52 * 1024 * 1024
        ),
    )(*args)


def write_kernel(gt, pair, down, router, gt_o, router_o, gate_o, up_o, down_o):
    gt_o[...] = gt[...]
    gate_o[0] = pair[:, 0:FF]
    up_o[0] = pair[:, FF : 2 * FF]
    down_o[0] = down[...]
    for p in range(NE):
        h, b = p % 2, p // 2
        router_o[16 * h : 16 * h + 16, 128 * b : 128 * b + 128] = router[p].astype(F32)


def write(*args):
    return pl.pallas_call(
        write_kernel,
        name="write",
        out_shape=(
            jax.ShapeDtypeStruct((TOK, D), BF16),
            jax.ShapeDtypeStruct((NE, D), F32),
            jax.ShapeDtypeStruct((1, 256, FF), BF16),
            jax.ShapeDtypeStruct((1, 256, FF), BF16),
            jax.ShapeDtypeStruct((1, 96, D), BF16),
        ),
        in_specs=[VM] * 4,
        out_specs=(VM,) * 5,
        compiler_params=pltpu.CompilerParams(vmem_limit_bytes=16 * 1024 * 1024),
    )(*args)


def per_device(tokens, out_grad, expert_ids, router_weight, w_gate, w_up, w_down):
    gt, pair, down, router = moe(
        *[
            pltpu.with_memory_space_constraint(a, pltpu.HBM)
            for a in (tokens, out_grad, expert_ids.T, router_weight.T)
        ],
        w_gate, w_up, w_down
    )
    gt, router, gate, up, down = write(gt, pair, down, router)
    return gt, router.T, gate, up, down


def solution(mesh):
    in_specs = (
        P(("dp", "expert"), None), P(("dp", "expert"), None), P(("dp", "expert"), None), P(),
        P("expert", None, None), P("expert", None, None), P("expert", None, None),
    )
    out_specs = (
        P(("dp", "expert"), None), P(),
        P("expert", "dp", None), P("expert", "dp", None), P("expert", "dp", None),
    )
    return jax.shard_map(
        per_device, mesh=mesh, in_specs=in_specs, out_specs=out_specs, check_vma=False
    )
```
